128 devices in a mesh: gx: 8 (over y, core), gy: 16 (over x, z).
Axes of the slice: x: 4, y: 4, z: 4, core: 2. Of those that a mesh axis runs over, the one named last changes fastest.
Arguments:
- right_side: float32 [8, 16, 176, 1152], P('gx', 'gy'), may hold values from -6 to 6
- flex: bfloat16 [8, 16, 1152, 1152], P('gx', 'gy'), as said below
- stiff: bfloat16 [8, 16, 1152, 1152], P('gx', 'gy')
- coarse_inv: float32 [3072, 3072], P('gx', 'gy'), as said below
- corner_map: int32 [8, 16, 24], P('gx', 'gy'), may hold values from 0 to 3071
- side_rows: int32 [8, 16, 2], P('gx', 'gy'), may hold values from 1 to 288, as said below
Outputs:
- solution: float32 [8, 16, 176, 1152], P('gx', 'gy')
- residual: float32 [8, 16, 176, 1152], P('gx', 'gy')
- resid_norm: float32 [3, 176], replicated
The draws below stay inside these ranges and needn't reach their ends.
Inputs may be any that keep to these rules, and one draw needn't show every extreme that they name: Entry 0 of side_rows at the first subdomain equals 288. flex and stiff are near one on the diagonal plus small full off-diagonal parts. coarse_inv is a dense matrix.
All inputs are finite; a program needn't handle non-finite values.
Results may differ from the reference program's by a relative error of at most 0.0056.
Values sent between devices are 32-bit elements; how exact they have to be, the bound alone decides.
No kernel may reach another device: no remote copies, remote signals or barrier semaphores. Data moves between devices by JAX's collectives and lax.ppermute only.
A program may use at most 64 MiB of HBM per device.

```python
import jax
import jax.numpy as jnp
from jax import lax

M = 1152
SIDE = 288
COARSE = 3072
CORN = 24
LOADS = 176
ITERS = 3
N_GX = 8
N_GY = 16


def dominant_block(key, count, order, spread):
    noise = jax.random.normal(key, (count, order, order), jnp.float32)
    return jnp.eye(order, dtype=jnp.float32)[None] + noise * (spread / order ** 0.5)


def draw_flex(key, part):
    blocks = dominant_block(jax.random.fold_in(key, 11), N_GX * N_GY, M, 0.3)
    return blocks.reshape((N_GX, N_GY, M, M)).astype(jnp.bfloat16)


def draw_stiff(key, part):
    blocks = dominant_block(jax.random.fold_in(key, 23), N_GX * N_GY, M, 0.3)
    return blocks.reshape((N_GX, N_GY, M, M)).astype(jnp.bfloat16)


def draw_coarse_inv(key, part):
    blocks = dominant_block(jax.random.fold_in(key, 37), 1, COARSE, 0.3)
    return (blocks[0] * 0.6).astype(jnp.float32)


def draw_side_rows(key, part):
    counts = jax.random.randint(jax.random.fold_in(key, 41), (N_GX, N_GY, 2), 1, SIDE + 1)
    return counts.at[0, 0, 0].set(SIDE).astype(jnp.int32)


def touch_ends(drawn, rng, least, largest):
    index_at = [jax.random.randint(jax.random.fold_in(rng, axis), (), 0, length) for axis, length in enumerate(drawn.shape)]
    main_axis = drawn.shape.index(max(drawn.shape))
    neighbour = index_at[:main_axis] + [(index_at[main_axis] + 1) % drawn.shape[main_axis]] + index_at[main_axis + 1:]
    return drawn.at[tuple(index_at)].set(least).at[tuple(neighbour)].set(largest)


def level_of(stream_key, shape, pieces, low, high):
    gain = 1.0
    for dim, shards_of in pieces:
        steps = jax.random.uniform(jax.random.fold_in(jax.random.fold_in(stream_key, 6), dim), (shards_of,), jnp.float32, low / len(pieces), high / len(pieces))
        gain = gain * jnp.repeat(jnp.exp(steps), shape[dim] // shards_of).reshape((-1,) + (1,) * (len(shape) - 1 - dim))
    return gain


def normal_values(rng, dims, width, bound, cuts=(), held_as=jnp.bfloat16):
    values = width * jax.random.normal(rng, dims, jnp.float32)
    if cuts:
        values = values * level_of(rng, dims, cuts, -0.22, 0.18)
    return jnp.clip(values, -bound, bound).astype(held_as)


def setup_inputs(seed: int = 0) -> dict:
    keys = jax.random.split(jax.random.key(seed), 7)
    return {
        "right_side": normal_values(keys[0], (N_GX, N_GY, LOADS, M), 1.0, 6.0, ((0, 8), (1, 16)), jnp.float32),
        "flex": draw_flex(jax.random.fold_in(keys[6], 71), 0),
        "stiff": draw_stiff(jax.random.fold_in(keys[6], 71), 0),
        "coarse_inv": draw_coarse_inv(jax.random.fold_in(keys[6], 71), 0),
        "corner_map": touch_ends(jax.random.randint(keys[4], (N_GX, N_GY, CORN), 0, COARSE), jax.random.fold_in(keys[4], 1), 0, COARSE - 1).astype(jnp.int32),
        "side_rows": draw_side_rows(jax.random.fold_in(keys[6], 71), 0),
    }


cheb_center = 1.15
cheb_half = 0.85
cheb_sigma = cheb_center / cheb_half

def local_product(vectors, blocks):

    def single(pair):
        return lax.dot_general(pair[0], pair[1], (((1,), (1,)), ((), ())), preferred_element_type=jnp.float32)
    shape = vectors.shape
    flat_vec = vectors.reshape((-1,) + shape[2:])
    flat_blk = blocks.reshape((-1,) + blocks.shape[2:])
    return lax.map(single, (flat_vec, flat_blk)).reshape(shape[:3] + (blocks.shape[2],))

def apply_operator(field, flex, stiff, coarse_inv, corner_map, side_rows):
    flexed = local_product(field.astype(jnp.bfloat16), flex)
    side = flexed.shape[-1] // 4
    west_side = flexed[..., 0:side]
    east_side = flexed[..., side:2 * side]
    north_side = flexed[..., 2 * side:3 * side]
    south_side = flexed[..., 3 * side:4 * side]
    row_ids = jnp.arange(side)
    grid_cols = jnp.arange(N_GY)
    grid_rows = jnp.arange(N_GX)
    mask_east = ((row_ids[None, None, :] < side_rows[:, :, 0:1]) & (grid_cols[None, :, None] < N_GY - 1)).astype(jnp.float32)
    mask_south = ((row_ids[None, None, :] < side_rows[:, :, 1:2]) & (grid_rows[:, None, None] < N_GX - 1)).astype(jnp.float32)
    from_east = jnp.concatenate([west_side[:, 1:], jnp.zeros_like(west_side[:, :1])], axis=1)
    jump_east = mask_east[:, :, None, :] * (east_side - from_east)
    back_west = jnp.concatenate([jnp.zeros_like(jump_east[:, :1]), jump_east[:, :-1]], axis=1)
    from_south = jnp.concatenate([north_side[1:], jnp.zeros_like(north_side[:1])], axis=0)
    jump_south = mask_south[:, :, None, :] * (south_side - from_south)
    back_north = jnp.concatenate([jnp.zeros_like(jump_south[:1]), jump_south[:-1]], axis=0)
    balanced = jnp.concatenate([west_side + 0.5 * back_west, east_side - 0.5 * jump_east, north_side + 0.5 * back_north, south_side - 0.5 * jump_south], axis=-1)
    stiffed = local_product(balanced.astype(jnp.bfloat16), stiff)
    corners = corner_map.shape[-1]
    corner_vals = stiffed[..., :corners]
    flat_vals = jnp.transpose(corner_vals, (0, 1, 3, 2)).reshape((-1, corner_vals.shape[2]))
    coarse_rhs = jax.ops.segment_sum(flat_vals, corner_map.reshape(-1), num_segments=coarse_inv.shape[0])
    coarse_sol = jnp.dot(coarse_inv, coarse_rhs, precision=lax.Precision.HIGHEST)
    correction = jnp.transpose(coarse_sol[corner_map], (0, 1, 3, 2))
    return jnp.concatenate([corner_vals + correction, stiffed[..., corners:]], axis=-1)

def reference(right_side, flex, stiff, coarse_inv, corner_map, side_rows):
    solution = jnp.zeros_like(right_side)
    residual = right_side
    direction = residual / cheb_center
    rho_prev = 1.0 / cheb_sigma
    norm_list = []
    for iteration in range(ITERS):
        solution = solution + direction
        residual = residual - apply_operator(direction, flex, stiff, coarse_inv, corner_map, side_rows)
        norm_list.append(jnp.sqrt(lax.optimization_barrier(jnp.sum(residual * residual, axis=(0, 1, 3))) / (N_GX * N_GY * M)))
        if iteration + 1 < ITERS:
            rho_next = 1.0 / (2.0 * cheb_sigma - rho_prev)
            direction = rho_next * rho_prev * direction + 2.0 * rho_next / cheb_half * residual
            rho_prev = rho_next
    return (solution, residual, jnp.stack(norm_list))
```

```python
import jax
import jax.numpy as jnp
from jax import lax
from jax.sharding import Mesh
from jax.sharding import PartitionSpec as P

ITERS = 3
GX = ("y", "c")
GY = ("x", "z")
ALL = ("y", "c", "x", "z")
NY, NC, NX, NZ = 4, 2, 4, 4

cheb_center = 1.15
cheb_half = 0.85
cheb_sigma = cheb_center / cheb_half
HIGHEST = lax.Precision.HIGHEST


def turned(array, axes, count, by):
    return lax.ppermute(array, axes, [(i, (i + by) % count) for i in range(count)])


def told_to_all(array, axes, count):
    copies = jnp.broadcast_to(array, (count, *array.shape))
    return lax.all_to_all(copies, axes, split_axis=0, concat_axis=0, tiled=True)


def exact_dot(a, b):
    return jnp.dot(a, b, precision=HIGHEST, preferred_element_type=jnp.float32)


def local(right_side, flex, stiff, coarse_inv, corner_map, side_rows):
    flex_block = flex[0, 0]
    stiff_block = stiff[0, 0]
    order = flex_block.shape[0]
    side = order // 4
    loads = right_side.shape[2]
    corners = corner_map.shape[2]
    n_gx, n_gy = NY * NC, NX * NZ
    rows_held, cols_held = coarse_inv.shape
    my_y, my_c, my_x, my_z = (lax.axis_index(a) for a in ALL)
    contract = (((1,), (1,)), ((), ()))

    inv_blocks = [coarse_inv] + [turned(coarse_inv, "y", NY, k) for k in range(1, NY)]

    facts = jnp.concatenate([corner_map[0, 0], side_rows[0, 0]]).astype(jnp.float32)
    facts = told_to_all(facts[None, :], ALL, n_gx * n_gy)
    facts = facts.reshape(NY, NC, NX, NZ, corners + 2)
    ids = facts[..., :corners]
    counts = facts[..., corners:].reshape(n_gx, n_gy, 2)

    row_index = my_y * NC + my_c
    col_index = my_x * NZ + my_z
    ids_of_row = lax.dynamic_index_in_dim(ids, my_y, 0, keepdims=False)
    ids_own = lax.dynamic_index_in_dim(ids_of_row, my_c, 0, keepdims=False).reshape(-1)
    ids_other = lax.dynamic_index_in_dim(ids_of_row, 1 - my_c, 0, keepdims=False).reshape(-1)
    held = jnp.concatenate(
        [
            (((my_y - k) % NY) * NC + my_c) * rows_held + jnp.arange(rows_held)
            for k in range(NY)
        ]
    ).astype(jnp.float32)
    wanted = jnp.concatenate([ids_own, ids_other])
    pick_rows = (wanted[:, None] == held[None, :]).astype(jnp.float32)
    picked = exact_dot(pick_rows, jnp.concatenate(inv_blocks, axis=0))
    half = n_gy * corners
    own_rows = picked[:half] + turned(picked[half:], "c", NC, 1)

    row_parts = [own_rows] + [turned(own_rows, "z", NZ, k) for k in range(1, NZ)]
    cols = jnp.concatenate(
        [
            (my_x * NZ + (my_z - k) % NZ) * cols_held + jnp.arange(cols_held)
            for k in range(NZ)
        ]
    ).astype(jnp.float32)
    ids_z = lax.dynamic_index_in_dim(ids, my_z, 3, keepdims=False)
    src = jnp.stack(
        [
            lax.dynamic_index_in_dim(ids_z, my_c, 1, keepdims=False),
            lax.dynamic_index_in_dim(ids_z, 1 - my_c, 1, keepdims=False),
        ],
        axis=2,
    ).reshape(-1)
    pick_cols = (cols[:, None] == src[None, :]).astype(jnp.float32)
    coarse_block = exact_dot(jnp.concatenate(row_parts, axis=1), pick_cols)

    row_ids = jnp.arange(side).astype(jnp.float32)

    def live(r, q, which, inside):
        count = counts[r % n_gx, q % n_gy, which]
        return ((row_ids < count) & inside)[None, :]

    live_east = live(row_index, col_index, 0, col_index < n_gy - 1)
    live_west = live(row_index, col_index - 1, 0, col_index > 0)
    live_south = live(row_index, col_index, 1, row_index < n_gx - 1)
    live_north = live(row_index - 1, col_index, 1, row_index > 0)

    def half_jump(live_rows, ahead, behind):
        return jnp.where(live_rows, 0.5 * (ahead - behind), 0.0)

    residual = right_side[0, 0]
    solution = jnp.zeros_like(residual)
    direction = residual / cheb_center
    rho_prev = 1.0 / cheb_sigma
    sums = []
    for iteration in range(ITERS):
        solution = solution + direction
        flexed = lax.dot_general(
            direction.astype(jnp.bfloat16), flex_block, contract, preferred_element_type=jnp.float32
        )
        west = flexed[:, 0:side]
        east = flexed[:, side : 2 * side]
        north = flexed[:, 2 * side : 3 * side]
        south = flexed[:, 3 * side : 4 * side]
        next_west = turned(west, GY, n_gy, -1)
        last_east = turned(east, GY, n_gy, 1)
        next_north = turned(north, GX, n_gx, -1)
        last_south = turned(south, GX, n_gx, 1)
        balanced = jnp.concatenate(
            [
                west + half_jump(live_west, last_east, west),
                east - half_jump(live_east, east, next_west),
                north + half_jump(live_north, last_south, north),
                south - half_jump(live_south, south, next_north),
            ],
            axis=1,
        ).astype(jnp.bfloat16)
        corner_vals = lax.dot_general(
            stiff_block[:corners], balanced, contract, preferred_element_type=jnp.float32
        )
        pair = jnp.concatenate([corner_vals, turned(corner_vals, "c", NC, 1)], axis=0)
        sources = told_to_all(pair, ("y", "x"), NY * NX).reshape(-1, loads)
        partial = exact_dot(coarse_block, sources).reshape(n_gy, corners, loads)
        terms = lax.all_to_all(partial, GY, split_axis=0, concat_axis=0, tiled=True)
        correction = terms.sum(axis=0)
        stiffed = lax.dot_general(
            balanced, stiff_block, contract, preferred_element_type=jnp.float32
        )
        residual = residual - stiffed
        residual = residual - jnp.pad(correction.T, ((0, 0), (0, order - corners)))
        sums.append(jnp.sum(residual * residual, axis=1))
        if iteration + 1 < ITERS:
            rho_next = 1.0 / (2.0 * cheb_sigma - rho_prev)
            direction = rho_next * rho_prev * direction + 2.0 * rho_next / cheb_half * residual
            rho_prev = rho_next
    flat = jnp.concatenate(sums)
    flat = jnp.pad(flat, (0, -flat.size % 128)).reshape(-1, 128)
    totals = told_to_all(flat, ALL, n_gx * n_gy).sum(axis=0).reshape(-1)[: ITERS * loads]
    resid_norm = jnp.sqrt(totals.reshape(ITERS, loads) / (n_gx * n_gy * order))
    return (solution[None, None], residual[None, None], resid_norm)


def solution(mesh):
    torus = Mesh(mesh.devices.reshape(NY, NC, NX, NZ), ALL)
    return jax.shard_map(
        local,
        mesh=torus,
        in_specs=(
            P(GX, GY, None, None),
            P(GX, GY, None, None),
            P(GX, GY, None, None),
            P(GX, GY),
            P(GX, GY, None),
            P(GX, GY, None),
        ),
        out_specs=(P(GX, GY, None, None), P(GX, GY, None, None), P()),
        check_vma=False,
    )
```

```python
import functools

import jax
import jax.numpy as jnp
from jax import lax
from jax.experimental import pallas as pl
from jax.experimental.pallas import tpu as pltpu
from jax.sharding import Mesh
from jax.sharding import PartitionSpec as P

ITERS = 3
GX = ("y", "c")
GY = ("x", "z")
ALL = ("y", "c", "x", "z")
NY, NC, NX, NZ = 4, 2, 4, 4
TOP = 128

cheb_center = 1.15
cheb_half = 0.85
cheb_sigma = cheb_center / cheb_half
F32 = jnp.float32
BF16 = jnp.bfloat16


def turned(array, axes, count, by):
    return lax.ppermute(array, axes, [(i, (i + by) % count) for i in range(count)])


def swapped(array, axes, count, shift):
    pairs = [(i, (((i + shift) ^ 1) - shift) % count) for i in range(count)]
    return lax.ppermute(array, axes, pairs)


def to_all(copies, axes):
    return lax.all_to_all(copies, axes, split_axis=0, concat_axis=0, tiled=True)


def told_to_all(array, axes, count):
    return to_all(jnp.broadcast_to(array, (count, *array.shape)), axes)


def vm():
    return pl.BlockSpec(memory_space=pltpu.VMEM)


def sm():
    return pl.BlockSpec(memory_space=pltpu.SMEM)


def call(body, outs, specs, name):
    many = isinstance(outs, (tuple, list))
    return pl.pallas_call(
        body,
        out_shape=outs,
        in_specs=specs,
        out_specs=[vm() for _ in outs] if many else vm(),
        name=name,
    )


def shape(*dims, dtype=F32):
    return jax.ShapeDtypeStruct(dims, dtype)


def dot(a, b, contract=((1,), (0,)), precision=None):
    return lax.dot_general(a, b, (contract, ((), ())), precision=precision, preferred_element_type=F32)


def thirds(a):
    high = a.astype(BF16)
    rest = a - high.astype(F32)
    mid = rest.astype(BF16)
    low = (rest - mid.astype(F32)).astype(BF16)
    return high, mid, low


def rows_kernel(base, wanted, *refs):
    blocks, own, other = refs[:-2], refs[-2], refs[-1]
    half = own.shape[1]
    total = 0.0
    for k, block in enumerate(blocks):
        at = lax.broadcasted_iota(jnp.int32, (block.shape[1], 2 * half), 0) + base[k]
        pick = jnp.where(at == wanted[...], 1.0, 0.0).astype(BF16)
        for part in thirds(block[...]):
            total = total + dot(part, pick)
    own[...] = total[:, :half]
    other[...] = total[:, half:]


def cols_kernel(base, source, *refs):
    blocks, own, other = refs[:-2], refs[-2], refs[-1]
    half = own.shape[1]
    total = 0.0
    for k, block in enumerate(blocks):
        at = lax.broadcasted_iota(jnp.int32, (block.shape[0], 2 * half), 0) + base[k]
        pick = jnp.where(at == source[...], 1.0, 0.0).astype(BF16)
        for part in thirds(block[...].T):
            total = total + dot(part, pick)
    own[...] = total[:, :half]
    other[...] = total[:, half:]


def send_sides(place, flexed, out_a, out_b, out_c, out_y):
    side = out_a.shape[0]
    odd_b, odd_a = place[0], place[1]

    def part(k):
        return flexed[pl.ds(pl.multiple_of(k * side, 32), side), :]

    out_a[...] = part(1 - odd_b)
    out_b[...] = part(odd_b)
    out_c[...] = part(3 - odd_a)
    out_y[...] = part(2 + odd_a)


def first_kernel(place, right, flex, flexed, *sends):
    direction = right[...] / cheb_center
    flexed[...] = dot(flex[...], direction.astype(BF16), ((1,), (1,)))
    send_sides(place, flexed, *sends)


def balance_kernel(place, live, flexed, in_a, in_b, in_c, in_y, stiff_top, balanced, told):
    side = in_a.shape[0]
    corners = told.shape[1]
    odd_b, odd_a = place[0] == 1, place[1] == 1
    at = lax.broadcasted_iota(jnp.int32, in_a.shape, 0)

    def half_jump(which, ahead, behind):
        return jnp.where(at < live[which], 0.5 * (ahead - behind), 0.0)

    west = flexed[0:side, :]
    east = flexed[side : 2 * side, :]
    north = flexed[2 * side : 3 * side, :]
    south = flexed[3 * side : 4 * side, :]
    a, b, c, y = in_a[...], in_b[...], in_c[...], in_y[...]
    last_east = jnp.where(odd_b, a, b)
    next_west = jnp.where(odd_b, b, a)
    last_south = jnp.where(odd_a, c, y)
    next_north = jnp.where(odd_a, y, c)
    balanced[0:side, :] = (west + half_jump(0, last_east, west)).astype(BF16)
    balanced[side : 2 * side, :] = (east - half_jump(1, east, next_west)).astype(BF16)
    balanced[2 * side : 3 * side, :] = (north + half_jump(2, last_south, north)).astype(BF16)
    balanced[3 * side : 4 * side, :] = (south - half_jump(3, south, next_north)).astype(BF16)
    values = dot(stiff_top[...], balanced[...])[:corners]
    for k in range(told.shape[0]):
        told[k] = values


def bulk_kernel(steps, balanced, stiff, flex, res_top, res_low, dir_top, dir_low, sol_top, sol_low, *outs):
    stiffed = dot(stiff[...], balanced[...])
    new_res_top, new_res_low, new_sol_top, new_sol_low, squares = outs[:5]
    top = res_top[...] - stiffed[:TOP]
    low = res_low[...] - stiffed[TOP:]
    new_res_top[...] = top
    new_res_low[...] = low
    new_sol_top[...] = sol_top[...] + dir_top[...]
    new_sol_low[...] = sol_low[...] + dir_low[...]
    squares[...] = jnp.sum(low * low, axis=0, keepdims=True)
    if steps is not None:
        new_dir_low, flex_base = outs[5:]
        new_dir = steps[0] * dir_low[...] + steps[1] * low
        new_dir_low[...] = new_dir
        flex_base[...] = dot(flex[:, TOP:], new_dir.astype(BF16))


def half_product_kernel(block, values, total):
    total[...] = dot(block[...], values[...].reshape(-1, values.shape[2]), precision=lax.Precision.HIGHEST)


def product_kernel(block, values, half, total):
    more = dot(block[...], values[...].reshape(-1, values.shape[2]), precision=lax.Precision.HIGHEST)
    total[...] = (half[...] + more).reshape(total.shape)


def correct_kernel(steps, terms, squares, res_top, *refs):
    corners = terms.shape[1]
    correction = terms[0]
    for k in range(1, terms.shape[0]):
        correction = correction + terms[k]
    if steps is None:
        new_res_top, norm = refs
    else:
        place, dir_top, flex_top, flex_base, new_res_top, norm, new_dir_top, flexed = refs[:8]
    new_res_top[...] = res_top[...]
    new_res_top[:corners, :] = res_top[:corners, :] - correction
    top = new_res_top[...]
    norm[...] = squares[...] + jnp.sum(top * top, axis=0, keepdims=True)
    if steps is not None:
        new_dir = steps[0] * dir_top[...] + steps[1] * top
        new_dir_top[...] = new_dir
        flexed[...] = flex_base[...] + dot(flex_top[...], new_dir.astype(BF16))
        send_sides(place, flexed, *refs[8:])


def local(right_side, flex, stiff, coarse_inv, corner_map, side_rows):
    right = right_side[0, 0]
    flex_block = flex[0, 0]
    stiff_block = stiff[0, 0]
    order = flex_block.shape[0]
    side = order // 4
    loads = right.shape[0]
    corners = corner_map.shape[2]
    n_gx, n_gy = NY * NC, NX * NZ
    rows_held, cols_held = coarse_inv.shape
    my_y, my_c, my_x, my_z = (lax.axis_index(a) for a in ALL)
    row_index = my_y * NC + my_c
    col_index = my_x * NZ + my_z
    half = n_gy * corners

    inv_t = coarse_inv.T
    inv_blocks = [inv_t] + [turned(inv_t, "y", NY, k) for k in range(1, NY)]

    place = jnp.stack([col_index % 2, row_index % 2]).astype(jnp.int32)
    sides = [shape(side, loads)] * 4
    flexed, *sends = call(
        first_kernel, [shape(order, loads)] + sides, [sm(), vm(), vm()], "first"
    )(place, right, flex_block)

    facts = jnp.concatenate([corner_map[0, 0], side_rows[0, 0]]).astype(F32)
    facts = told_to_all(facts[None, :], ALL, n_gx * n_gy)[:, 0, :]

    def number(y, c, x, z):
        return ((y * NC + c) * NX + x) * NZ + z

    places = jnp.arange(n_gy)
    row_ids = jnp.concatenate([number(my_y, my_c, 0, places), number(my_y, 1 - my_c, 0, places)])
    ys, xs = places // NX, places % NX
    src_ids = jnp.concatenate([number(ys, my_c, xs, my_z), number(ys, 1 - my_c, xs, my_z)])
    own_id = number(my_y, my_c, my_x, my_z)
    west_id = jnp.where(col_index > 0, own_id - 1, own_id)
    north_id = jnp.where(row_index > 0, own_id - n_gy, own_id)
    wanted_ids = jnp.concatenate([row_ids, src_ids, jnp.stack([own_id, west_id, north_id])])
    taken = facts[wanted_ids].astype(jnp.int32)
    lists = taken[: 4 * n_gy, :corners].reshape(2, 1, 2 * half)
    near = taken[4 * n_gy :, corners:]
    live = jnp.stack(
        [
            jnp.where(col_index > 0, near[1, 0], 0),
            jnp.where(col_index < n_gy - 1, near[0, 0], 0),
            jnp.where(row_index > 0, near[2, 1], 0),
            jnp.where(row_index < n_gx - 1, near[0, 1], 0),
        ]
    )

    turns = jnp.arange(NY)
    row_base = (((my_y - turns) % NY) * NC + my_c) * rows_held
    picked = [shape(cols_held, half)] * 2
    own_rows, other_rows = call(rows_kernel, picked, [sm()] + [vm()] * (1 + NY), "rows")(
        row_base.astype(jnp.int32), lists[0], *inv_blocks
    )
    own_rows = own_rows + turned(other_rows, "c", NC, 1)

    row_parts = [own_rows] + [turned(own_rows, "z", NZ, k) for k in range(1, NZ)]
    col_base = (my_x * NZ + (my_z - turns) % NZ) * cols_held
    block_own, block_other = call(
        cols_kernel, [shape(half, half)] * 2, [sm()] + [vm()] * (1 + NZ), "cols"
    )(col_base.astype(jnp.int32), lists[1], *row_parts)

    stiff_top = stiff_block[:32]
    flex_top = flex_block[:, :TOP]
    right_t = right.T
    res_top, res_low = right_t[:TOP], right_t[TOP:]
    dir_top, dir_low = res_top / cheb_center, res_low / cheb_center
    sol_top, sol_low = jnp.zeros_like(res_top), jnp.zeros_like(res_low)
    tops, lows = shape(TOP, loads), shape(order - TOP, loads)
    rho_prev = 1.0 / cheb_sigma
    norms = []
    for iteration in range(ITERS):
        last = iteration + 1 == ITERS
        in_a = swapped(sends[0], GY, n_gy, 0)
        in_b = swapped(sends[1], GY, n_gy, 1)
        in_c = swapped(sends[2], GX, n_gx, 0)
        in_y = swapped(sends[3], GX, n_gx, 1)
        balanced, told = call(
            balance_kernel,
            [shape(order, loads, dtype=BF16), shape(NY * NX, corners, loads)],
            [sm(), sm()] + [vm()] * 6,
            "balance",
        )(place, live, flexed, in_a, in_b, in_c, in_y, stiff_top)
        values = to_all(told, ("y", "x"))
        steps = None
        if not last:
            rho_next = 1.0 / (2.0 * cheb_sigma - rho_prev)
            steps = (rho_next * rho_prev, 2.0 * rho_next / cheb_half)
            rho_prev = rho_next
        outs = call(
            functools.partial(bulk_kernel, steps),
            [tops, lows, tops, lows, shape(1, loads)] + ([] if last else [lows, shape(order, loads)]),
            [vm()] * 9,
            "bulk",
        )(balanced, stiff_block, flex_block, res_top, res_low, dir_top, dir_low, sol_top, sol_low)
        res_top, res_low, sol_top, sol_low, squares = outs[:5]
        values_other = turned(values, "c", NC, 1)
        partial = call(half_product_kernel, shape(half, loads), [vm()] * 2, "half")(block_own, values)
        partial = call(product_kernel, shape(n_gy, corners, loads), [vm()] * 3, "product")(
            block_other, values_other, partial
        )
        terms = to_all(partial, GY)
        if last:
            res_top, norm = call(
                functools.partial(correct_kernel, None), [tops, shape(1, loads)], [vm()] * 3, "last"
            )(terms, squares, res_top)
        else:
            dir_low, flex_base = outs[5:]
            res_top, norm, dir_top, flexed, *sends = call(
                functools.partial(correct_kernel, steps),
                [tops, shape(1, loads), tops, shape(order, loads)] + sides,
                [vm()] * 3 + [sm()] + [vm()] * 3,
                "correct",
            )(terms, squares, res_top, place, dir_top, flex_top, flex_base)
        norms.append(norm)
    flat = jnp.concatenate(norms).reshape(-1)
    flat = jnp.pad(flat, (0, -flat.size % 128)).reshape(-1, 128)
    totals = told_to_all(flat, ALL, n_gx * n_gy).sum(axis=0).reshape(-1)[: ITERS * loads]
    resid_norm = jnp.sqrt(totals.reshape(ITERS, loads) / (n_gx * n_gy * order))
    solution = jnp.concatenate([sol_top, sol_low]).T
    residual = jnp.concatenate([res_top, res_low]).T
    return (solution[None, None], residual[None, None], resid_norm)


def solution(mesh):
    torus = Mesh(mesh.devices.reshape(NY, NC, NX, NZ), ALL)
    return jax.shard_map(
        local,
        mesh=torus,
        in_specs=(
            P(GX, GY, None, None),
            P(GX, GY, None, None),
            P(GX, GY, None, None),
            P(GX, GY),
            P(GX, GY, None),
            P(GX, GY, None),
        ),
        out_specs=(P(GX, GY, None, None), P(GX, GY, None, None), P()),
        check_vma=False,
    )
```

```python
import functools

import jax
import jax.numpy as jnp
from jax import lax
from jax.experimental import pallas as pl
from jax.experimental.pallas import tpu as pltpu
from jax.sharding import Mesh
from jax.sharding import PartitionSpec as P

ITERS = 3
GX = ("y", "c")
GY = ("x", "z")
ALL = ("y", "c", "x", "z")
NY, NC, NX, NZ = 4, 2, 4, 4
TOP = 128
VMEM_BYTES = 16 * 2**20

cheb_center = 1.15
cheb_half = 0.85
cheb_sigma = cheb_center / cheb_half
F32 = jnp.float32
BF16 = jnp.bfloat16


def turned(array, axes, count, by):
    return lax.ppermute(array, axes, [(i, (i + by) % count) for i in range(count)])


def swapped(array, axes, count, shift):
    pairs = [(i, (((i + shift) ^ 1) - shift) % count) for i in range(count)]
    return lax.ppermute(array, axes, pairs)


def to_all(copies, axes):
    return lax.all_to_all(copies, axes, split_axis=0, concat_axis=0, tiled=True)


def told_to_all(array, axes, count):
    return to_all(jnp.broadcast_to(array, (count, *array.shape)), axes)


def vm():
    return pl.BlockSpec(memory_space=pltpu.VMEM)


def sm():
    return pl.BlockSpec(memory_space=pltpu.SMEM)


def call(body, outs, name):
    def run(*operands, scalars=0):
        held = [pltpu.with_memory_space_constraint(o, pltpu.VMEM) for o in operands[scalars:]]
        specs = [sm()] * scalars + [vm()] * len(held)
        return pl.pallas_call(
            body,
            out_shape=outs,
            in_specs=specs,
            out_specs=[vm() for _ in outs],
            compiler_params=pltpu.CompilerParams(vmem_limit_bytes=VMEM_BYTES),
            name=name,
        )(*operands[:scalars], *held)

    return run


def call_with_scratch(body, outs, scratch, name):
    def run(where, *operands):
        held = [pltpu.with_memory_space_constraint(o, pltpu.VMEM) for o in operands]
        return pl.pallas_call(
            body,
            out_shape=outs,
            in_specs=[sm()] + [vm()] * len(held),
            out_specs=[vm() for _ in outs],
            scratch_shapes=scratch,
            compiler_params=pltpu.CompilerParams(vmem_limit_bytes=VMEM_BYTES),
            name=name,
        )(where, *held)

    return run


def shape(*dims, dtype=F32):
    return pltpu.VMEM(dims, dtype)


def dot(a, b, contract=((1,), (0,)), precision=None):
    return lax.dot_general(a, b, (contract, ((), ())), precision=precision, preferred_element_type=F32)


def thirds(a):
    high = a.astype(BF16)
    rest = a - high.astype(F32)
    mid = rest.astype(BF16)
    low = (rest - mid.astype(F32)).astype(BF16)
    return high, mid, low


def one_hot_rows(ids, base, held):
    at = lax.broadcasted_iota(jnp.int32, (ids.shape[0], held), 1) + base
    return jnp.where(at.astype(F32) == ids, 1.0, 0.0)


def rows_kernel(where, facts, *refs):
    blocks, own, other, pick = refs[:-3], refs[-3], refs[-2], refs[-1]
    my_y, my_c = where[0], where[1]
    held = blocks[0].shape[1]
    targets = NX * NZ
    corners = own.shape[1] // targets
    lists = []
    for core in (my_c, 1 - my_c):
        start = pl.multiple_of((my_y * NC + core) * targets, 8)
        lists.append(facts[pl.ds(start, targets), :].T[:corners])
    total = 0.0
    for k, block in enumerate(blocks):
        base = (((my_y + NY - k) % NY) * NC + my_c) * held
        for n in range(2 * targets):
            ids = lists[n // targets][:, n % targets : n % targets + 1]
            pick[n * corners : (n + 1) * corners, :] = one_hot_rows(ids, base, held)
        chosen = pick[...].astype(BF16)
        for part in thirds(block[...]):
            total = total + dot(part, chosen, ((1,), (1,)))
    own[...] = total[:, : targets * corners]
    other[...] = total[:, targets * corners :]


def cols_kernel(where, facts, *refs):
    blocks, outs, pick, rows = refs[:-6], refs[-6:-2], refs[-2], refs[-1]
    my_c, my_x, my_z = where[1], where[2], where[3]
    held = blocks[0].shape[0]
    sources = NY * NX
    corners = outs[0].shape[1] // sources
    lists = []
    for core in (my_c, 1 - my_c):
        for n in range(sources):
            at = (((n // NX) * NC + core) * NX + n % NX) * NZ + my_z
            rows[n : n + 1, :] = facts[pl.ds(at, 1), :]
        lists.append(rows[...].T[:corners])
    total = 0.0
    for k, block in enumerate(blocks):
        base = (my_x * NZ + (my_z + NZ - k) % NZ) * held
        for n in range(2 * sources):
            ids = lists[n // sources][:, n % sources : n % sources + 1]
            pick[n * corners : (n + 1) * corners, :] = one_hot_rows(ids, base, held)
        chosen = pick[...].astype(BF16)
        for part in thirds(block[...]):
            total = total + dot(chosen, part)
    total = total.T
    for n in range(2):
        half = total[:, n * sources * corners : (n + 1) * sources * corners]
        high = half.astype(BF16)
        outs[2 * n][...] = high
        outs[2 * n + 1][...] = (half - high.astype(F32)).astype(BF16)


def send_sides(where, flexed, out_a, out_b, out_c, out_y):
    side = out_a.shape[0]
    odd_b, odd_a = where[3] % 2, where[1]

    def part(k):
        return flexed[pl.ds(pl.multiple_of(k * side, 32), side), :]

    out_a[...] = part(1 - odd_b)
    out_b[...] = part(odd_b)
    out_c[...] = part(3 - odd_a)
    out_y[...] = part(2 + odd_a)


def first_kernel(where, right, flex, flexed, *sends):
    direction = right[...] / cheb_center
    flexed[...] = dot(flex[...], direction.astype(BF16), ((1,), (1,)))
    send_sides(where, flexed, *sends)


def balance_kernel(where, facts, flexed, in_a, in_b, in_c, in_y, stiff_top, balanced, told):
    side = in_a.shape[0]
    corners = told.shape[1]
    n_gy = NX * NZ
    row = where[0] * NC + where[1]
    col = where[2] * NZ + where[3]
    odd_b, odd_a = where[3] % 2 == 1, where[1] == 1
    at = lax.broadcasted_iota(jnp.int32, in_a.shape, 0).astype(F32)
    own = row * n_gy + col

    def live(subdomain, which, inside):
        count = facts[pl.ds(subdomain, 1), corners + which : corners + which + 1]
        return jnp.logical_and(at < count, inside)

    def half_jump(lives, ahead, behind):
        return jnp.where(lives, 0.5 * (ahead - behind), 0.0)

    west = flexed[0:side, :]
    east = flexed[side : 2 * side, :]
    north = flexed[2 * side : 3 * side, :]
    south = flexed[3 * side : 4 * side, :]
    a, b, c, y = in_a[...], in_b[...], in_c[...], in_y[...]
    last_east = jnp.where(odd_b, a, b)
    next_west = jnp.where(odd_b, b, a)
    last_south = jnp.where(odd_a, c, y)
    next_north = jnp.where(odd_a, y, c)
    live_west = live(jnp.maximum(own - 1, 0), 0, col > 0)
    live_east = live(own, 0, col < n_gy - 1)
    live_north = live(jnp.maximum(own - n_gy, 0), 1, row > 0)
    live_south = live(own, 1, row < NY * NC - 1)
    balanced[0:side, :] = (west + half_jump(live_west, last_east, west)).astype(BF16)
    balanced[side : 2 * side, :] = (east - half_jump(live_east, east, next_west)).astype(BF16)
    balanced[2 * side : 3 * side, :] = (north + half_jump(live_north, last_south, north)).astype(BF16)
    balanced[3 * side : 4 * side, :] = (south - half_jump(live_south, south, next_north)).astype(BF16)
    values = dot(stiff_top[...], balanced[...])[:corners]
    for k in range(told.shape[0]):
        told[k] = values


def step_on(steps, flex, dir_low, low, new_dir_low, flex_base):
    new_dir = steps[0] * dir_low + steps[1] * low
    new_dir_low[...] = new_dir
    flex_base[...] = dot(flex[:, TOP:], new_dir.astype(BF16))


def first_bulk_kernel(steps, balanced, stiff, flex, right, *outs):
    res_top, res_low, sol_top, sol_low, squares = outs[:5]
    stiffed = dot(stiff[...], balanced[...])
    direction = right[...] / cheb_center
    low = right[TOP:, :] - stiffed[TOP:]
    res_top[...] = right[:TOP, :] - stiffed[:TOP]
    res_low[...] = low
    sol_top[...] = direction[:TOP]
    sol_low[...] = direction[TOP:]
    squares[...] = jnp.sum(low * low, axis=0, keepdims=True)
    step_on(steps, flex, direction[TOP:], low, *outs[5:])


def bulk_kernel(steps, balanced, stiff, flex, res_top, res_low, dir_top, dir_low, sol_top, sol_low, *outs):
    new_res_top, new_res_low, new_sol_top, new_sol_low, squares = outs[:5]
    stiffed = dot(stiff[...], balanced[...])
    low = res_low[...] - stiffed[TOP:]
    new_res_top[...] = res_top[...] - stiffed[:TOP]
    new_res_low[...] = low
    new_sol_top[...] = sol_top[...] + dir_top[...]
    new_sol_low[...] = sol_low[...] + dir_low[...]
    squares[...] = jnp.sum(low * low, axis=0, keepdims=True)
    if steps is not None:
        step_on(steps, flex, dir_low[...], low, *outs[5:])


def split_dot(high, low, values):
    values = values[...].reshape(-1, values.shape[2])
    values_high = values.astype(BF16)
    values_low = (values - values_high.astype(F32)).astype(BF16)
    return dot(high[...], values_high) + (dot(high[...], values_low) + dot(low[...], values_high))


def half_product_kernel(high, low, values, total):
    total[...] = split_dot(high, low, values)


def product_kernel(high, low, values, half, total):
    total[...] = (half[...] + split_dot(high, low, values)).reshape(total.shape)


def correction_of(terms, squares, res_top, new_res_top, norm):
    corners = terms.shape[1]
    parts = [terms[k] for k in range(terms.shape[0])]
    while len(parts) > 1:
        parts = [p + q for p, q in zip(parts[::2], parts[1::2])]
    new_res_top[...] = res_top[...]
    new_res_top[:corners, :] = res_top[:corners, :] - parts[0]
    top = new_res_top[...]
    norm[...] = squares[...] + jnp.sum(top * top, axis=0, keepdims=True)
    return top


def last_kernel(*refs):
    correction_of(*refs)


def correct_kernel(steps, where, terms, squares, res_top, dir_top, flex_top, flex_base, *outs):
    new_res_top, norm, new_dir_top, flexed = outs[:4]
    top = correction_of(terms, squares, res_top, new_res_top, norm)
    new_dir = steps[0] * dir_top[...] + steps[1] * top
    new_dir_top[...] = new_dir
    flexed[...] = flex_base[...] + dot(flex_top[...], new_dir.astype(BF16))
    send_sides(where, flexed, *outs[4:])


def local(right_side, flex, stiff, coarse_inv, corner_map, side_rows):
    right = right_side[0, 0]
    flex_block = flex[0, 0]
    stiff_block = stiff[0, 0]
    order = flex_block.shape[0]
    side = order // 4
    loads = right.shape[0]
    corners = corner_map.shape[2]
    n_gx, n_gy = NY * NC, NX * NZ
    rows_held, cols_held = coarse_inv.shape
    where = jnp.stack([lax.axis_index(a) for a in ALL]).astype(jnp.int32)
    half = n_gy * corners

    inv_t = coarse_inv.T
    inv_blocks = [inv_t] + [turned(inv_t, "y", NY, k) for k in range(1, NY)]

    sides = [shape(side, loads)] * 4
    flexed, *sends = call(first_kernel, [shape(order, loads)] + sides, "first")(
        where, right, flex_block, scalars=1
    )

    facts = jnp.concatenate([corner_map[0, 0], side_rows[0, 0]]).astype(F32)
    facts = jnp.pad(facts, (0, -facts.size % 128))
    facts = told_to_all(facts[None, :], ALL, n_gx * n_gy)[:, 0, :]

    own_rows, other_rows = call_with_scratch(
        rows_kernel,
        [shape(cols_held, half)] * 2,
        [pltpu.VMEM((2 * half, rows_held), F32)],
        "rows",
    )(where, facts, *inv_blocks)
    own_rows = own_rows + turned(other_rows, "c", NC, 1)

    row_parts = [own_rows] + [turned(own_rows, "z", NZ, k) for k in range(1, NZ)]
    block_own_high, block_own_low, block_high, block_low = call_with_scratch(
        cols_kernel,
        [shape(half, half, dtype=BF16)] * 4,
        [pltpu.VMEM((2 * half, cols_held), F32), pltpu.VMEM((NY * NX, 128), F32)],
        "cols",
    )(where, facts, *row_parts)

    stiff_top = stiff_block[:32]
    flex_top = flex_block[:, :TOP]
    tops, lows = shape(TOP, loads), shape(order - TOP, loads)
    rho_prev = 1.0 / cheb_sigma
    norms = []
    for iteration in range(ITERS):
        last = iteration + 1 == ITERS
        in_a = swapped(sends[0], GY, n_gy, 0)
        in_b = swapped(sends[1], GY, n_gy, 1)
        in_c = swapped(sends[2], GX, n_gx, 0)
        in_y = swapped(sends[3], GX, n_gx, 1)
        balanced, told = call(
            balance_kernel,
            [shape(order, loads, dtype=BF16), shape(NY * NX, corners, loads)],
            "balance",
        )(where, facts, flexed, in_a, in_b, in_c, in_y, stiff_top, scalars=1)
        values = to_all(told, ("y", "x"))
        steps = None
        if not last:
            rho_next = 1.0 / (2.0 * cheb_sigma - rho_prev)
            steps = (rho_next * rho_prev, 2.0 * rho_next / cheb_half)
            rho_prev = rho_next
        kernel, state = bulk_kernel, None
        if iteration == 0:
            kernel, state = first_bulk_kernel, (right.T,)
        else:
            state = (res_top, res_low, dir_top, dir_low, sol_top, sol_low)
        outs = call(
            functools.partial(kernel, steps),
            [tops, lows, tops, lows, shape(1, loads)] + ([] if last else [lows, shape(order, loads)]),
            "bulk",
        )(balanced, stiff_block, flex_block, *state)
        res_top, res_low, sol_top, sol_low, squares = outs[:5]
        if iteration == 0:
            dir_top = sol_top
        values_other = turned(values, "c", NC, 1)
        (partial,) = call(half_product_kernel, [shape(half, loads)], "half")(
            block_own_high, block_own_low, values
        )
        (partial,) = call(product_kernel, [shape(n_gy, corners, loads)], "product")(
            block_high, block_low, values_other, partial
        )
        terms = to_all(partial, GY)
        if last:
            res_top, norm = call(last_kernel, [tops, shape(1, loads)], "last")(terms, squares, res_top)
        else:
            dir_low, flex_base = outs[5:]
            res_top, norm, dir_top, flexed, *sends = call(
                functools.partial(correct_kernel, steps),
                [tops, shape(1, loads), tops, shape(order, loads)] + sides,
                "correct",
            )(where, terms, squares, res_top, dir_top, flex_top, flex_base, scalars=1)
        norms.append(norm)
    flat = jnp.concatenate(norms).reshape(-1)
    flat = jnp.pad(flat, (0, -flat.size % 128)).reshape(-1, 128)
    totals = told_to_all(flat, ALL, n_gx * n_gy).sum(axis=0).reshape(-1)[: ITERS * loads]
    resid_norm = jnp.sqrt(totals.reshape(ITERS, loads) / (n_gx * n_gy * order))
    solution = jnp.concatenate([sol_top, sol_low]).T
    residual = jnp.concatenate([res_top, res_low]).T
    return (solution[None, None], residual[None, None], resid_norm)


def solution(mesh):
    torus = Mesh(mesh.devices.reshape(NY, NC, NX, NZ), ALL)
    return jax.shard_map(
        local,
        mesh=torus,
        in_specs=(
            P(GX, GY, None, None),
            P(GX, GY, None, None),
            P(GX, GY, None, None),
            P(GX, GY),
            P(GX, GY, None),
            P(GX, GY, None),
        ),
        out_specs=(P(GX, GY, None, None), P(GX, GY, None, None), P()),
        check_vma=False,
    )
```

```python
import functools

import jax
import jax.numpy as jnp
from jax import lax
from jax.experimental import pallas as pl
from jax.experimental.pallas import tpu as pltpu
from jax.sharding import Mesh
from jax.sharding import PartitionSpec as P

ITERS = 3
GX = ("y", "c")
GY = ("x", "z")
ALL = ("y", "c", "x", "z")
NY, NC, NX, NZ = 4, 2, 4, 4
TOP = 128
VMEM_BYTES = 16 * 2**20

cheb_center = 1.15
cheb_half = 0.85
cheb_sigma = cheb_center / cheb_half
F32 = jnp.float32
BF16 = jnp.bfloat16


def turned(array, axes, count, by):
    return lax.ppermute(array, axes, [(i, (i + by) % count) for i in range(count)])


def swapped(array, axes, count, shift):
    pairs = [(i, (((i + shift) ^ 1) - shift) % count) for i in range(count)]
    return lax.ppermute(array, axes, pairs)


def to_all(copies, axes):
    return lax.all_to_all(copies, axes, split_axis=0, concat_axis=0, tiled=True)


def told_to_all(array, axes, count):
    return to_all(jnp.broadcast_to(array, (count, *array.shape)), axes)


def vm():
    return pl.BlockSpec(memory_space=pltpu.VMEM)


def sm():
    return pl.BlockSpec(memory_space=pltpu.SMEM)


def call(body, outs, name):
    def run(*operands, scalars=0):
        held = [pltpu.with_memory_space_constraint(o, pltpu.VMEM) for o in operands[scalars:]]
        specs = [sm()] * scalars + [vm()] * len(held)
        return pl.pallas_call(
            body,
            out_shape=outs,
            in_specs=specs,
            out_specs=[vm() for _ in outs],
            compiler_params=pltpu.CompilerParams(vmem_limit_bytes=VMEM_BYTES),
            name=name,
        )(*operands[:scalars], *held)

    return run


def call_with_scratch(body, outs, scratch, name):
    def run(where, *operands):
        held = [pltpu.with_memory_space_constraint(o, pltpu.VMEM) for o in operands]
        return pl.pallas_call(
            body,
            out_shape=outs,
            in_specs=[sm()] + [vm()] * len(held),
            out_specs=[vm() for _ in outs],
            scratch_shapes=scratch,
            compiler_params=pltpu.CompilerParams(vmem_limit_bytes=VMEM_BYTES),
            name=name,
        )(where, *held)

    return run


def shape(*dims, dtype=F32):
    return pltpu.VMEM(dims, dtype)


def dot(a, b, contract=((1,), (0,)), precision=None):
    return lax.dot_general(a, b, (contract, ((), ())), precision=precision, preferred_element_type=F32)


def thirds(a):
    high = a.astype(BF16)
    rest = a - high.astype(F32)
    mid = rest.astype(BF16)
    low = (rest - mid.astype(F32)).astype(BF16)
    return high, mid, low


def rows_kernel(where, facts, *refs):
    blocks, own, other, pick = refs[:-3], refs[-3], refs[-2], refs[-1]
    my_y, my_c = where[0], where[1]
    held = blocks[0].shape[1]
    targets = NX * NZ
    corners = own.shape[1] // targets
    lists = []
    for core in (my_c, 1 - my_c):
        start = pl.multiple_of((my_y * NC + core) * targets, 8)
        lists.append(facts[pl.ds(start, targets), :].T[:corners])
    at = lax.broadcasted_iota(jnp.int32, (corners, held), 1).astype(F32)
    total = 0.0
    for k, block in enumerate(blocks):
        base = ((((my_y + NY - k) % NY) * NC + my_c) * held).astype(F32)
        shifted = [ids - base for ids in lists]
        for n in range(2 * targets):
            ids = shifted[n // targets][:, n % targets : n % targets + 1]
            pick[n * corners : (n + 1) * corners, :] = jnp.where(at == ids, 1.0, 0.0)
        chosen = pick[...].astype(BF16)
        for part in thirds(block[...]):
            total = total + dot(part, chosen, ((1,), (1,)))
    own[...] = total[:, : targets * corners]
    other[...] = total[:, targets * corners :]


def cols_kernel(where, facts, *refs):
    blocks, outs, pick, rows = refs[:-6], refs[-6:-2], refs[-2], refs[-1]
    my_c, my_x, my_z = where[1], where[2], where[3]
    held = blocks[0].shape[0]
    sources = NY * NX
    corners = outs[0].shape[1] // sources
    lists = []
    for core in (my_c, 1 - my_c):
        for n in range(sources):
            at = (((n // NX) * NC + core) * NX + n % NX) * NZ + my_z
            rows[n : n + 1, :] = facts[pl.ds(at, 1), :]
        lists.append(rows[...].T[:corners])
    at = lax.broadcasted_iota(jnp.int32, (corners, held), 1).astype(F32)
    total = 0.0
    for k, block in enumerate(blocks):
        base = ((my_x * NZ + (my_z + NZ - k) % NZ) * held).astype(F32)
        shifted = [ids - base for ids in lists]
        for n in range(2 * sources):
            ids = shifted[n // sources][:, n % sources : n % sources + 1]
            pick[n * corners : (n + 1) * corners, :] = jnp.where(at == ids, 1.0, 0.0)
        chosen = pick[...].astype(BF16)
        for part in thirds(block[...]):
            total = total + dot(chosen, part)
    total = total.T
    for n in range(2):
        half = total[:, n * sources * corners : (n + 1) * sources * corners]
        high = half.astype(BF16)
        outs[2 * n][...] = high
        outs[2 * n + 1][...] = (half - high.astype(F32)).astype(BF16)


def send_sides(where, flexed, out_a, out_b, out_c, out_y):
    side = out_a.shape[0]
    odd_b, odd_a = where[3] % 2, where[1]

    def part(k):
        return flexed[pl.ds(pl.multiple_of(k * side, 32), side), :]

    out_a[...] = part(1 - odd_b)
    out_b[...] = part(odd_b)
    out_c[...] = part(3 - odd_a)
    out_y[...] = part(2 + odd_a)


def first_kernel(where, right, flex, flexed, *sends):
    direction = right[...] / cheb_center
    flexed[...] = dot(flex[...], direction.astype(BF16), ((1,), (1,)))
    send_sides(where, flexed, *sends)


def balance_kernel(where, facts, flexed, in_a, in_b, in_c, in_y, stiff, balanced, told):
    side = in_a.shape[0]
    corners = told.shape[1]
    n_gy = NX * NZ
    row = where[0] * NC + where[1]
    col = where[2] * NZ + where[3]
    odd_b, odd_a = where[3] % 2 == 1, where[1] == 1
    at = lax.broadcasted_iota(jnp.int32, in_a.shape, 0).astype(F32)
    own = row * n_gy + col

    def live(subdomain, which, inside):
        count = facts[pl.ds(subdomain, 1), corners + which : corners + which + 1]
        return jnp.logical_and(at < count, inside)

    def half_jump(lives, ahead, behind):
        return jnp.where(lives, 0.5 * (ahead - behind), 0.0)

    west = flexed[0:side, :]
    east = flexed[side : 2 * side, :]
    north = flexed[2 * side : 3 * side, :]
    south = flexed[3 * side : 4 * side, :]
    a, b, c, y = in_a[...], in_b[...], in_c[...], in_y[...]
    last_east = jnp.where(odd_b, a, b)
    next_west = jnp.where(odd_b, b, a)
    last_south = jnp.where(odd_a, c, y)
    next_north = jnp.where(odd_a, y, c)
    live_west = live(jnp.maximum(own - 1, 0), 0, col > 0)
    live_east = live(own, 0, col < n_gy - 1)
    live_north = live(jnp.maximum(own - n_gy, 0), 1, row > 0)
    live_south = live(own, 1, row < NY * NC - 1)
    balanced[0:side, :] = (west + half_jump(live_west, last_east, west)).astype(BF16)
    balanced[side : 2 * side, :] = (east - half_jump(live_east, east, next_west)).astype(BF16)
    balanced[2 * side : 3 * side, :] = (north + half_jump(live_north, last_south, north)).astype(BF16)
    balanced[3 * side : 4 * side, :] = (south - half_jump(live_south, south, next_north)).astype(BF16)
    values = dot(stiff[:32, :], balanced[...])[:corners]
    for k in range(told.shape[0]):
        told[k] = values


def step_on(steps, flex, dir_low, low, new_dir_low, flex_base):
    new_dir = steps[0] * dir_low + steps[1] * low
    new_dir_low[...] = new_dir
    flex_base[...] = dot(flex[:, TOP:], new_dir.astype(BF16))


def first_bulk_kernel(steps, after, balanced, stiff, flex, right, *outs):
    right = right[...].T
    res_top, res_low, sol_top, sol_low, squares = outs[:5]
    stiffed = dot(stiff[...], balanced[...])
    direction = right / cheb_center
    low = right[TOP:, :] - stiffed[TOP:]
    res_top[...] = right[:TOP, :] - stiffed[:TOP]
    res_low[...] = low
    sol_top[...] = direction[:TOP]
    sol_low[...] = direction[TOP:]
    squares[...] = jnp.sum(low * low, axis=0, keepdims=True)
    step_on(steps, flex, direction[TOP:], low, *outs[5:])


def bulk_kernel(steps, after, balanced, stiff, flex, res_top, res_low, dir_top, dir_low, sol_top, sol_low, *outs):
    new_res_top, new_res_low, new_sol_top, new_sol_low, squares = outs[:5]
    stiffed = dot(stiff[...], balanced[...])
    low = res_low[...] - stiffed[TOP:]
    new_res_top[...] = res_top[...] - stiffed[:TOP]
    new_res_low[...] = low
    new_sol_top[...] = sol_top[...] + dir_top[...]
    new_sol_low[...] = sol_low[...] + dir_low[...]
    squares[...] = jnp.sum(low * low, axis=0, keepdims=True)
    if steps is not None:
        step_on(steps, flex, dir_low[...], low, *outs[5:])


def split_dot(high, low, values):
    values = values[...].reshape(-1, values.shape[2])
    values_high = values.astype(BF16)
    values_low = (values - values_high.astype(F32)).astype(BF16)
    return dot(high[...], values_high) + (dot(high[...], values_low) + dot(low[...], values_high))


def half_product_kernel(high, low, values, total):
    total[...] = split_dot(high, low, values)


def product_kernel(after, high, low, values, half, total):
    total[...] = (half[...] + split_dot(high, low, values)).reshape(total.shape)


def correction_of(terms, squares, res_top, new_res_top, norm):
    corners = terms.shape[1]
    parts = [terms[k] for k in range(terms.shape[0])]
    while len(parts) > 1:
        parts = [p + q for p, q in zip(parts[::2], parts[1::2])]
    new_res_top[...] = res_top[...]
    new_res_top[:corners, :] = res_top[:corners, :] - parts[0]
    top = new_res_top[...]
    norm[...] = squares[...] + jnp.sum(top * top, axis=0, keepdims=True)
    return top


def last_kernel(*refs):
    correction_of(*refs)


def correct_kernel(steps, where, terms, squares, res_top, dir_top, flex, flex_base, *outs):
    new_res_top, norm, new_dir_top, flexed = outs[:4]
    top = correction_of(terms, squares, res_top, new_res_top, norm)
    new_dir = steps[0] * dir_top[...] + steps[1] * top
    new_dir_top[...] = new_dir
    flexed[...] = flex_base[...] + dot(flex[:, :TOP], new_dir.astype(BF16))
    send_sides(where, flexed, *outs[4:])


def local(right_side, flex, stiff, coarse_inv, corner_map, side_rows):
    right = right_side[0, 0]
    flex_block = flex[0, 0]
    stiff_block = stiff[0, 0]
    order = flex_block.shape[0]
    side = order // 4
    loads = right.shape[0]
    corners = corner_map.shape[2]
    n_gx, n_gy = NY * NC, NX * NZ
    rows_held, cols_held = coarse_inv.shape
    where = jnp.stack([lax.axis_index(a) for a in ALL]).astype(jnp.int32)
    half = n_gy * corners

    inv_t = coarse_inv.T
    inv_blocks = [inv_t] + [turned(inv_t, "y", NY, k) for k in range(1, NY)]

    sides = [shape(side, loads)] * 4
    flexed, *sends = call(first_kernel, [shape(order, loads)] + sides, "first")(
        where, right, flex_block, scalars=1
    )

    facts = jnp.concatenate([corner_map[0, 0], side_rows[0, 0]]).astype(F32)
    facts = jnp.pad(facts, (0, -facts.size % 128))
    facts, *sends = lax.optimization_barrier((facts, *sends))
    facts = told_to_all(facts[None, :], ALL, n_gx * n_gy)[:, 0, :]

    own_rows, other_rows = call_with_scratch(
        rows_kernel,
        [shape(cols_held, half)] * 2,
        [pltpu.VMEM((2 * half, rows_held), F32)],
        "rows",
    )(where, facts, *inv_blocks)
    own_rows = own_rows + turned(other_rows, "c", NC, 1)

    row_parts = [own_rows] + [turned(own_rows, "z", NZ, k) for k in range(1, NZ)]
    block_own_high, block_own_low, block_high, block_low = call_with_scratch(
        cols_kernel,
        [shape(half, half, dtype=BF16)] * 4,
        [pltpu.VMEM((2 * half, cols_held), F32), pltpu.VMEM((NY * NX, 128), F32)],
        "cols",
    )(where, facts, *row_parts)

    tops, lows = shape(TOP, loads), shape(order - TOP, loads)
    rho_prev = 1.0 / cheb_sigma
    norms = []
    for iteration in range(ITERS):
        last = iteration + 1 == ITERS
        in_a = swapped(sends[0], GY, n_gy, 0)
        in_b = swapped(sends[1], GY, n_gy, 1)
        in_c = swapped(sends[2], GX, n_gx, 0)
        in_y = swapped(sends[3], GX, n_gx, 1)
        balanced, told = call(
            balance_kernel,
            [shape(order, loads, dtype=BF16), shape(NY * NX, corners, loads)],
            "balance",
        )(where, facts, flexed, in_a, in_b, in_c, in_y, stiff_block, scalars=1)
        values = to_all(told, ("y", "x"))
        steps = None
        if not last:
            rho_next = 1.0 / (2.0 * cheb_sigma - rho_prev)
            steps = (rho_next * rho_prev, 2.0 * rho_next / cheb_half)
            rho_prev = rho_next
        kernel, state = bulk_kernel, None
        if iteration == 0:
            kernel, state = first_bulk_kernel, (right,)
        else:
            state = (res_top, res_low, dir_top, dir_low, sol_top, sol_low)
        outs = call(
            functools.partial(kernel, steps),
            [tops, lows, tops, lows, shape(1, loads)] + ([] if last else [lows, shape(order, loads)]),
            "bulk",
        )(values, balanced, stiff_block, flex_block, *state)
        res_top, res_low, sol_top, sol_low, squares = outs[:5]
        if iteration == 0:
            dir_top = sol_top
        values_other = turned(values, "c", NC, 1)
        (partial,) = call(half_product_kernel, [shape(half, loads)], "half")(
            block_own_high, block_own_low, values
        )
        (partial,) = call(product_kernel, [shape(n_gy, corners, loads)], "product")(
            squares, block_high, block_low, values_other, partial
        )
        terms = to_all(partial, GY)
        if last:
            res_top, norm = call(last_kernel, [tops, shape(1, loads)], "last")(terms, squares, res_top)
        else:
            dir_low, flex_base = outs[5:]
            res_top, norm, dir_top, flexed, *sends = call(
                functools.partial(correct_kernel, steps),
                [tops, shape(1, loads), tops, shape(order, loads)] + sides,
                "correct",
            )(where, terms, squares, res_top, dir_top, flex_block, flex_base, scalars=1)
        norms.append(norm)
    flat = jnp.concatenate(norms).reshape(-1)
    flat = jnp.pad(flat, (0, -flat.size % 128)).reshape(-1, 128)
    totals = told_to_all(flat, ALL, n_gx * n_gy).sum(axis=0).reshape(-1)[: ITERS * loads]
    resid_norm = jnp.sqrt(totals.reshape(ITERS, loads) / (n_gx * n_gy * order))
    solution = jnp.concatenate([sol_top, sol_low]).T
    residual = jnp.concatenate([res_top, res_low]).T
    return (solution[None, None], residual[None, None], resid_norm)


def solution(mesh):
    torus = Mesh(mesh.devices.reshape(NY, NC, NX, NZ), ALL)
    return jax.shard_map(
        local,
        mesh=torus,
        in_specs=(
            P(GX, GY, None, None),
            P(GX, GY, None, None),
            P(GX, GY, None, None),
            P(GX, GY),
            P(GX, GY, None),
            P(GX, GY, None),
        ),
        out_specs=(P(GX, GY, None, None), P(GX, GY, None, None), P()),
        check_vma=False,
    )
```

```python
import functools

import jax
import jax.numpy as jnp
from jax import lax
from jax.experimental import pallas as pl
from jax.experimental.pallas import tpu as pltpu
from jax.sharding import Mesh
from jax.sharding import PartitionSpec as P

ITERS = 3
GX = ("y", "c")
GY = ("x", "z")
ALL = ("y", "c", "x", "z")
NY, NC, NX, NZ = 4, 2, 4, 4
N_GX, N_GY = NY * NC, NX * NZ
SIDES = 4
TOP = 128
LANES = 128
TILE = 8
VMEM_BYTES = 16 * 2**20

cheb_center = 1.15
cheb_half = 0.85
cheb_sigma = cheb_center / cheb_half
F32 = jnp.float32
BF16 = jnp.bfloat16


def turned(array, axes, count, by):
    return lax.ppermute(array, axes, [(i, (i + by) % count) for i in range(count)])


def swapped(array, axes, count, shift):
    pairs = [(i, (((i + shift) ^ 1) - shift) % count) for i in range(count)]
    return lax.ppermute(array, axes, pairs)


def to_all(copies, axes):
    return lax.all_to_all(copies, axes, split_axis=0, concat_axis=0, tiled=True)


def vm():
    return pl.BlockSpec(memory_space=pltpu.VMEM)


def sm():
    return pl.BlockSpec(memory_space=pltpu.SMEM)


def call(body, outs, scalars=0, scratch=()):
    def run(*operands):
        held = [pltpu.with_memory_space_constraint(o, pltpu.VMEM) for o in operands[scalars:]]
        return pl.pallas_call(
            body,
            out_shape=outs,
            in_specs=[sm()] * scalars + [vm()] * len(held),
            out_specs=[vm() for _ in outs],
            scratch_shapes=scratch,
            compiler_params=pltpu.CompilerParams(vmem_limit_bytes=VMEM_BYTES),
        )(*operands[:scalars], *held)

    return run


def shape(*dims, dtype=F32):
    return pltpu.VMEM(dims, dtype)


def dot(a, b, contract=((1,), (0,))):
    return lax.dot_general(a, b, (contract, ((), ())), preferred_element_type=F32)


def split(a):
    high = a.astype(BF16)
    return high, (a - high.astype(F32)).astype(BF16)


def mark(pick, columns, held):
    corners = columns[0].shape[0]
    at = lax.broadcasted_iota(jnp.int32, (2 * corners, held), 1).astype(F32)
    for n in range(0, len(columns), 2):
        ids = jnp.concatenate(columns[n : n + 2], axis=0)
        pick[n * corners : (n + 2) * corners, :] = jnp.where(at == ids, 1.0, 0.0).astype(BF16)


def rows_kernel(where, ids_own, ids_other, *refs):
    blocks, own, other, pick = refs[:-3], refs[-3], refs[-2], refs[-1]
    my_y, my_c = where[0], where[1]
    held = blocks[0].shape[1]
    half = own.shape[1]
    corners = half // N_GY
    lists = [ids[...].T[:corners] for ids in (ids_own, ids_other)]
    total = 0.0
    for k, block in enumerate(blocks):
        base = ((((my_y + NY - k) % NY) * NC + my_c) * held).astype(F32)
        shifted = [ids - base for ids in lists]
        mark(pick, [ids[:, n : n + 1] for ids in shifted for n in range(N_GY)], held)
        for part in split(block[...]):
            total = total + dot(part, pick[...], ((1,), (1,)))
    own[...] = total[:, :half]
    other[...] = total[:, half:]


def cols_kernel(where, own, other, *refs):
    blocks, outs, pick = refs[:-5], refs[-5:-1], refs[-1]
    my_x, my_z = where[2], where[3]
    held = blocks[0].shape[0]
    half = outs[0].shape[1]
    last = own.shape[2] - 1
    columns = [v[n, :, last:] for v in (own, other) for n in range(v.shape[0])]
    total = 0.0
    for k, block in enumerate(blocks):
        base = ((my_x * NZ + (my_z + NZ - k) % NZ) * held).astype(F32)
        mark(pick, [ids - base for ids in columns], held)
        for part in split(block[...]):
            total = total + dot(pick[...], part)
    total = total.T
    for n in range(2):
        outs[2 * n][...], outs[2 * n + 1][...] = split(total[:, n * half : (n + 1) * half])


def pack(out, main, rest, count):
    side, wide = main.shape[0], rest.shape[1]
    half = side // 2
    out[0:side, :] = main
    out[side : side + half, 0:wide] = rest[:half]
    out[side : side + half, wide : 2 * wide] = rest[half:]
    out[side : side + half, 2 * wide :] = jnp.full((half, LANES - 2 * wide), count.astype(F32))


def first_kernel(where, ids, right, flex, flexed, extra, *sends):
    step = pl.program_id(0)

    @pl.when(step == 0)
    def _():
        column = jnp.broadcast_to(ids[...], (LANES, LANES)).T
        extra[...] = jnp.zeros_like(extra)
        extra[:, extra.shape[1] - LANES :] = column[: extra.shape[0]]

    side = flex.shape[0]
    odd_b, odd_a = where[3] % 2, where[1]
    direction = (right[...] / cheb_center).astype(BF16)
    part = dot(flex[...], direction, ((1,), (1,)))
    flexed[pl.ds(pl.multiple_of(step * side, side), side), :] = part
    for k, wanted in enumerate((1 - odd_b, odd_b, 3 - odd_a, 2 + odd_a)):

        @pl.when(step == wanted)
        def _():
            pack(sends[k], part[:, :LANES], part[:, LANES:], where[4 + k // 2])


def send_sides(where, flexed, *sends):
    side = flexed.shape[0] // SIDES
    odd_b, odd_a = where[3] % 2, where[1]
    for k, wanted in enumerate((1 - odd_b, odd_b, 3 - odd_a, 2 + odd_a)):
        rows = pl.ds(pl.multiple_of(wanted * side, 32), side)
        pack(sends[k], flexed[rows, 0:LANES], flexed[rows, LANES:], where[4 + k // 2])


def balance_kernel(where, flexed, in_a, in_b, in_c, in_y, stiff, extra, *refs):
    balanced, told, message = refs[-3:]
    side = flexed.shape[0] // SIDES
    loads = flexed.shape[1]
    wide = loads - LANES
    half = side // 2
    row = where[0] * NC + where[1]
    col = where[2] * NZ + where[3]
    odd_b, odd_a = where[3] % 2 == 1, where[1] == 1
    spot = (slice(side, side + 1), slice(2 * wide, 2 * wide + 1))
    count_west = jnp.where(odd_b, in_a[spot], in_b[spot])
    count_north = jnp.where(odd_a, in_c[spot], in_y[spot])
    count_east = jnp.full((1, 1), where[4].astype(F32))
    count_south = jnp.full((1, 1), where[5].astype(F32))

    for rows, lanes, there in (
        ((0, side), (0, LANES), ((0, side), (0, LANES))),
        ((0, half), (LANES, loads), ((side, side + half), (0, wide))),
        ((half, side), (LANES, loads), ((side, side + half), (wide, 2 * wide))),
    ):
        size = (rows[1] - rows[0], lanes[1] - lanes[0])
        at = (lax.broadcasted_iota(jnp.int32, size, 0) + rows[0]).astype(F32)
        a, b, c, y = (m[there[0][0] : there[0][1], there[1][0] : there[1][1]] for m in (in_a, in_b, in_c, in_y))
        west, east, north, south = (
            flexed[k * side + rows[0] : k * side + rows[1], lanes[0] : lanes[1]] for k in range(SIDES)
        )

        def half_jump(count, inside, ahead, behind):
            return jnp.where(jnp.logical_and(at < count, inside), 0.5 * (ahead - behind), 0.0)

        results = (
            west + half_jump(count_west, col > 0, jnp.where(odd_b, a, b), west),
            east - half_jump(count_east, col < N_GY - 1, east, jnp.where(odd_b, b, a)),
            north + half_jump(count_north, row > 0, jnp.where(odd_a, c, y), north),
            south - half_jump(count_south, row < N_GX - 1, south, jnp.where(odd_a, y, c)),
        )
        for k, result in enumerate(results):
            balanced[k * side + rows[0] : k * side + rows[1], lanes[0] : lanes[1]] = result.astype(BF16)
    corners = told.shape[1]
    message[...] = extra[...]
    message[:, 0:loads] = dot(stiff[0:32, :], balanced[...])[:corners]
    for k in range(told.shape[0]):
        told[k] = message[...]


def step_on(steps, flex, dir_low, low, new_dir_low, flex_base):
    new_dir = steps[0] * dir_low + steps[1] * low
    new_dir_low[...] = new_dir
    flex_base[...] = dot(flex[:, TOP:], new_dir.astype(BF16))


def first_bulk_kernel(steps, after, balanced, stiff, flex, right, *outs):
    right = right[...].T
    res_top, res_low, sol_top, sol_low, squares = outs[:5]
    stiffed = dot(stiff[...], balanced[...])
    direction = right / cheb_center
    low = right[TOP:, :] - stiffed[TOP:]
    res_top[...] = right[:TOP, :] - stiffed[:TOP]
    res_low[...] = low
    sol_top[...] = direction[:TOP]
    sol_low[...] = direction[TOP:]
    squares[...] = jnp.sum(low * low, axis=0, keepdims=True)
    step_on(steps, flex, direction[TOP:], low, *outs[5:])


def bulk_kernel(steps, after, balanced, stiff, flex, res_top, res_low, dir_top, dir_low, sol_top, sol_low, *outs):
    new_res_top, new_res_low, new_sol_top, new_sol_low, squares = outs[:5]
    stiffed = dot(stiff[...], balanced[...])
    low = res_low[...] - stiffed[TOP:]
    new_res_top[...] = res_top[...] - stiffed[:TOP]
    new_res_low[...] = low
    new_sol_top[...] = sol_top[...] + dir_top[...]
    new_sol_low[...] = sol_low[...] + dir_low[...]
    squares[...] = jnp.sum(low * low, axis=0, keepdims=True)
    if steps is not None:
        step_on(steps, flex, dir_low[...], low, *outs[5:])


def split_dot(high, low, values):
    values_high, values_low = split(values[...].reshape(-1, values.shape[2]))
    return dot(high[...], values_high) + (dot(high[...], values_low) + dot(low[...], values_high))


def tree_sum(parts):
    while len(parts) > 1:
        parts = [p + q for p, q in zip(parts[::2], parts[1::2])]
    return parts[0]


def riders(values):
    return tree_sum([values[k, 0:TILE, :] for k in range(values.shape[0])])


def half_product_kernel(high, low, values, total, ride):
    total[...] = split_dot(high, low, values)
    ride[...] = riders(values)


def product_kernel(loads, after, high, low, values, half, ride, total):
    result = (half[...] + split_dot(high, low, values)).reshape(total.shape)
    both = ride[...] + riders(values)
    lane = lax.broadcasted_iota(jnp.int32, both.shape, 1)
    for k in range(total.shape[0]):
        total[k] = result[k]
        total[k, 0:TILE, :] = jnp.where(lane < loads, result[k, 0:TILE, :], both)


def correction_of(terms, squares, res_top, new_res_top, earlier):
    corners = terms.shape[1]
    total = tree_sum([terms[k] for k in range(terms.shape[0])])
    earlier[...] = total[0:TILE, :] * (1.0 / NX)
    new_res_top[...] = res_top[...]
    new_res_top[:corners, :] = res_top[:corners, :] - total[:, : res_top.shape[1]]
    top = new_res_top[...]
    return top, squares[...] + jnp.sum(top * top, axis=0, keepdims=True)


def last_kernel(terms, squares, res_top, new_res_top, earlier, told):
    _, norm = correction_of(terms, squares, res_top, new_res_top, earlier)
    padded = jnp.concatenate([norm, jnp.zeros((1, told.shape[2] - norm.shape[1]), F32)], axis=1)
    told[...] = jnp.broadcast_to(padded[None], told.shape)


def correct_kernel(steps, where, terms, squares, res_top, dir_top, flex, flex_base, *outs):
    new_res_top, earlier, extra, new_dir_top, flexed = outs[:5]
    top, norm = correction_of(terms, squares, res_top, new_res_top, earlier)
    new_dir = steps[0] * dir_top[...] + steps[1] * top
    new_dir_top[...] = new_dir
    flexed[...] = flex_base[...] + dot(flex[:, :TOP], new_dir.astype(BF16))
    send_sides(where, flexed, *outs[5:])
    loads, width = norm.shape[1], extra.shape[1]
    spare = width - loads
    padded = jnp.concatenate([norm, jnp.zeros((1, spare), F32)], axis=1)
    padded = jnp.broadcast_to(padded, (TILE, width))
    line = lax.broadcasted_iota(jnp.int32, padded.shape, 0)
    ride = jnp.zeros_like(padded)
    for n in range(-(-loads // spare)):
        ride = jnp.where(line == n, pltpu.roll(padded, (loads - n * spare) % width, 1), ride)
    extra[...] = jnp.zeros_like(extra)
    extra[0:TILE, :] = ride


def rider_values(earlier, loads):
    spare = earlier.shape[1] - loads
    lines = -(-loads // spare)
    return earlier[:lines, loads:].reshape(-1)[:loads]


def local(right_side, flex, stiff, coarse_inv, corner_map, side_rows):
    right = right_side[0, 0]
    flex_block = flex[0, 0]
    stiff_block = stiff[0, 0]
    order = flex_block.shape[0]
    side = order // SIDES
    loads = right.shape[0]
    width = -(-loads // LANES) * LANES
    corners = corner_map.shape[2]
    rows_held, cols_held = coarse_inv.shape
    half = N_GY * corners
    ids = corner_map[0, 0]
    where = jnp.concatenate([jnp.stack([lax.axis_index(a) for a in ALL]), side_rows[0, 0]])
    where = where.astype(jnp.int32)

    inv_t = coarse_inv.T
    inv_blocks = [inv_t]
    for k in range(1, NY):
        inv_blocks.append(turned(inv_t, "y", NY, k))

    sides = [shape(side + side // 2, LANES)] * SIDES
    ids_line = jnp.pad(ids.astype(F32), (0, LANES - corners))[None]
    from_hbm = [pltpu.with_memory_space_constraint(a, pltpu.HBM) for a in (right, flex_block)]
    flexed, extra, *sends = pl.pallas_call(
        first_kernel,
        grid=(SIDES,),
        out_shape=[shape(order, loads), shape(corners, width)] + sides,
        in_specs=[
            sm(),
            vm(),
            pl.BlockSpec((loads, order), lambda i: (0, 0)),
            pl.BlockSpec((side, order), lambda i: (i, 0)),
        ],
        out_specs=[vm() for _ in range(2 + SIDES)],
        compiler_params=pltpu.CompilerParams(vmem_limit_bytes=VMEM_BYTES),
        name="first",
    )(where, ids_line, *from_hbm)

    own_ids, *sends = lax.optimization_barrier((ids_line, *sends))
    own_ids = jnp.broadcast_to(own_ids[None], (N_GY, 1, LANES))
    own_ids = to_all(own_ids, GY).reshape(N_GY, LANES)
    other_ids = turned(own_ids, "c", NC, 1)
    own_rows, other_rows = call(
        rows_kernel,
        [shape(cols_held, half)] * 2,
        scalars=1,
        scratch=[pltpu.VMEM((2 * half, rows_held), BF16)],
    )(where, own_ids, other_ids, *inv_blocks)
    own_rows = own_rows + turned(other_rows, "c", NC, 1)

    row_parts = [own_rows]
    for k in range(1, NZ):
        row_parts.append(turned(own_rows, "z", NZ, k))

    tops, lows = shape(TOP, loads), shape(order - TOP, loads)
    told_shape = shape(NY * NX, corners, width)
    ride_shape = shape(TILE, width)
    ordering = (own_rows,)
    rho_prev = 1.0 / cheb_sigma
    norms = []
    for iteration in range(ITERS):
        last = iteration + 1 == ITERS
        ins = []
        for k in range(SIDES):
            axes, count = (GY, N_GY) if k < 2 else (GX, N_GX)
            ins.append(swapped(sends[k], axes, count, k % 2))
        balanced, told = call(
            balance_kernel,
            [shape(order, loads, dtype=BF16), told_shape],
            scalars=1,
            scratch=[pltpu.VMEM((corners, width), F32)],
        )(where, flexed, *ins, stiff_block, extra, *ordering)
        ordering = ()
        values = to_all(told, ("y", "x"))
        steps = None
        if not last:
            rho_next = 1.0 / (2.0 * cheb_sigma - rho_prev)
            steps = (rho_next * rho_prev, 2.0 * rho_next / cheb_half)
            rho_prev = rho_next
        if iteration == 0:
            kernel, state = first_bulk_kernel, (right,)
        else:
            kernel, state = bulk_kernel, (res_top, res_low, dir_top, dir_low, sol_top, sol_low)
        outs = call(
            functools.partial(kernel, steps),
            [tops, lows, tops, lows, shape(1, loads)] + ([] if last else [lows, shape(order, loads)]),
        )(values, balanced, stiff_block, flex_block, *state)
        res_top, res_low, sol_top, sol_low, squares = outs[:5]
        values_other = turned(values, "c", NC, 1)
        if iteration == 0:
            dir_top = sol_top
            own_high, own_low, other_high, other_low = call(
                cols_kernel,
                [shape(half, half, dtype=BF16)] * 4,
                scalars=1,
                scratch=[pltpu.VMEM((2 * half, cols_held), BF16)],
            )(where, values, values_other, *row_parts)
        partial, ride = call(half_product_kernel, [shape(half, width), ride_shape])(
            own_high, own_low, values
        )
        (partial,) = call(
            functools.partial(product_kernel, loads), [shape(N_GY, corners, width)]
        )(squares, other_high, other_low, values_other, partial, ride)
        terms = to_all(partial, GY)
        if last:
            res_top, earlier, told = call(
                last_kernel, [tops, ride_shape, shape(N_GX * N_GY, 1, width)]
            )(terms, squares, res_top)
        else:
            dir_low, flex_base = outs[5:]
            res_top, earlier, extra, dir_top, flexed, *sends = call(
                functools.partial(correct_kernel, steps),
                [tops, ride_shape, shape(corners, width), tops, shape(order, loads)] + sides,
                scalars=1,
            )(where, terms, squares, res_top, dir_top, flex_block, flex_base)
        if iteration > 0:
            norms.append(rider_values(earlier, loads))
    norms.append(to_all(told, ALL).sum(axis=0)[0, :loads])
    resid_norm = jnp.sqrt(jnp.stack(norms) / (N_GX * N_GY * order))
    solution = jnp.concatenate([sol_top, sol_low]).T
    residual = jnp.concatenate([res_top, res_low]).T
    return (solution[None, None], residual[None, None], resid_norm)


def solution(mesh):
    torus = Mesh(mesh.devices.reshape(NY, NC, NX, NZ), ALL)
    return jax.shard_map(
        local,
        mesh=torus,
        in_specs=(
            P(GX, GY, None, None),
            P(GX, GY, None, None),
            P(GX, GY, None, None),
            P(GX, GY),
            P(GX, GY, None),
            P(GX, GY, None),
        ),
        out_specs=(P(GX, GY, None, None), P(GX, GY, None, None), P()),
        check_vma=False,
    )
```

```python
import functools

import jax
import jax.numpy as jnp
from jax import lax
from jax.experimental import pallas as pl
from jax.experimental.pallas import tpu as pltpu
from jax.sharding import Mesh
from jax.sharding import PartitionSpec as P

ITERS = 3
GX = ("y", "c")
GY = ("x", "z")
ALL = ("y", "c", "x", "z")
NY, NC, NX, NZ = 4, 2, 4, 4
N_GX, N_GY = NY * NC, NX * NZ
SIDES = 4
TOP = 128
LANES = 128
TILE = 8
VMEM_BYTES = 16 * 2**20

cheb_center = 1.15
cheb_half = 0.85
cheb_sigma = cheb_center / cheb_half
F32 = jnp.float32
BF16 = jnp.bfloat16


def turned(array, axes, count, by):
    return lax.ppermute(array, axes, [(i, (i + by) % count) for i in range(count)])


def swapped(array, axes, count, shift):
    pairs = [(i, (((i + shift) ^ 1) - shift) % count) for i in range(count)]
    return lax.ppermute(array, axes, pairs)


def to_all(copies, axes):
    return lax.all_to_all(copies, axes, split_axis=0, concat_axis=0, tiled=True)


def vm():
    return pl.BlockSpec(memory_space=pltpu.VMEM)


def sm():
    return pl.BlockSpec(memory_space=pltpu.SMEM)


def call(body, outs, scalars=0, scratch=()):
    def run(*operands):
        held = [pltpu.with_memory_space_constraint(o, pltpu.VMEM) for o in operands[scalars:]]
        return pl.pallas_call(
            body,
            out_shape=outs,
            in_specs=[sm()] * scalars + [vm()] * len(held),
            out_specs=[vm() for _ in outs],
            scratch_shapes=scratch,
            compiler_params=pltpu.CompilerParams(vmem_limit_bytes=VMEM_BYTES),
        )(*operands[:scalars], *held)

    return run


def shape(*dims, dtype=F32):
    return pltpu.VMEM(dims, dtype)


def dot(a, b, contract=((1,), (0,))):
    return lax.dot_general(a, b, (contract, ((), ())), preferred_element_type=F32)


def split(a):
    high = a.astype(BF16)
    return high, (a - high.astype(F32)).astype(BF16)


def mark(pick, columns, held):
    corners = columns[0].shape[0]
    at = lax.broadcasted_iota(jnp.int32, (2 * corners, held), 1).astype(F32)
    for n in range(0, len(columns), 2):
        ids = jnp.concatenate(columns[n : n + 2], axis=0)
        pick[n * corners : (n + 2) * corners, :] = jnp.where(at == ids, 1.0, 0.0).astype(BF16)


def rows_kernel(where, ids_own, ids_other, *refs):
    blocks, own, other, pick = refs[:-3], refs[-3], refs[-2], refs[-1]
    my_y, my_c = where[0], where[1]
    held = blocks[0].shape[1]
    half = own.shape[1]
    corners = half // N_GY
    lists = [ids[...].T[:corners] for ids in (ids_own, ids_other)]
    total = 0.0
    for k, block in enumerate(blocks):
        base = ((((my_y + NY - k) % NY) * NC + my_c) * held).astype(F32)
        shifted = [ids - base for ids in lists]
        mark(pick, [ids[:, n : n + 1] for ids in shifted for n in range(N_GY)], held)
        for part in split(block[...]):
            total = total + dot(part, pick[...], ((1,), (1,)))
    own[...] = total[:, :half]
    other[...] = total[:, half:]


def cols_kernel(where, own, other, *refs):
    blocks, outs, sends, pick, total = refs[:NZ], refs[NZ : NZ + 4], refs[NZ + 4 : -2], refs[-2], refs[-1]
    my_x, my_z = where[2], where[3]
    held = blocks[0].shape[0]
    half = outs[0].shape[1]
    last = own.shape[2] - 1
    corners = own.shape[1]
    columns = [v[n, :, last:] for v in (own, other) for n in range(v.shape[0])]
    summed = 0.0
    for k, block in enumerate(blocks):
        base = ((my_x * NZ + (my_z + NZ - k) % NZ) * held).astype(F32)
        mark(pick, [ids - base for ids in columns], held)
        for part in split(block[...]):
            summed = summed + dot(pick[...], part)
    total[...] = summed
    for n in range(2):
        outs[2 * n][...], outs[2 * n + 1][...] = split(summed[n * half : (n + 1) * half].T)
    for k, send in enumerate(sends):
        for n in range(NC * NY):
            start = pl.multiple_of((n * NX + (my_x + k) % NX) * corners, TILE)
            send[n * corners : (n + 1) * corners, :] = total[pl.ds(start, corners), :]


def block_kernel(*refs):
    parts, outs = refs[:NX], refs[NX:]
    block = ((parts[0][...] + parts[1][...]) + (parts[2][...] + parts[3][...])).T
    half = block.shape[1] // 2
    for n in range(2):
        outs[2 * n][...], outs[2 * n + 1][...] = split(block[:, n * half : (n + 1) * half])


def pack(out, main, rest, count):
    side, wide = main.shape[0], rest.shape[1]
    half = side // 2
    out[0:side, :] = main
    out[side : side + half, 0:wide] = rest[:half]
    out[side : side + half, wide : 2 * wide] = rest[half:]
    out[side : side + half, 2 * wide :] = jnp.full((half, LANES - 2 * wide), count.astype(F32))


def first_kernel(where, ids, right, flex, flexed, extra, *sends):
    step = pl.program_id(0)

    @pl.when(step == 0)
    def _():
        column = jnp.broadcast_to(ids[...], (LANES, LANES)).T
        extra[...] = jnp.zeros_like(extra)
        extra[:, extra.shape[1] - LANES :] = column[: extra.shape[0]]

    side = flex.shape[0]
    odd_b, odd_a = where[3] % 2, where[1]
    direction = (right[...] / cheb_center).astype(BF16)
    part = dot(flex[...], direction, ((1,), (1,)))
    flexed[pl.ds(pl.multiple_of(step * side, side), side), :] = part
    for k, wanted in enumerate((1 - odd_b, odd_b, 3 - odd_a, 2 + odd_a)):

        @pl.when(step == wanted)
        def _():
            pack(sends[k], part[:, :LANES], part[:, LANES:], where[4 + k // 2])


def send_sides(where, flexed, *sends):
    side = flexed.shape[0] // SIDES
    odd_b, odd_a = where[3] % 2, where[1]
    for k, wanted in enumerate((1 - odd_b, odd_b, 3 - odd_a, 2 + odd_a)):
        rows = pl.ds(pl.multiple_of(wanted * side, 32), side)
        pack(sends[k], flexed[rows, 0:LANES], flexed[rows, LANES:], where[4 + k // 2])


def balance_kernel(where, flexed, in_a, in_b, in_c, in_y, stiff, extra, *refs):
    balanced, told, message = refs[-3:]
    side = flexed.shape[0] // SIDES
    loads = flexed.shape[1]
    wide = loads - LANES
    half = side // 2
    row = where[0] * NC + where[1]
    col = where[2] * NZ + where[3]
    odd_b, odd_a = where[3] % 2 == 1, where[1] == 1
    spot = (slice(side, side + 1), slice(2 * wide, 2 * wide + 1))
    count_west = jnp.where(odd_b, in_a[spot], in_b[spot])
    count_north = jnp.where(odd_a, in_c[spot], in_y[spot])
    count_east = jnp.full((1, 1), where[4].astype(F32))
    count_south = jnp.full((1, 1), where[5].astype(F32))

    for rows, lanes, there in (
        ((0, side), (0, LANES), ((0, side), (0, LANES))),
        ((0, half), (LANES, loads), ((side, side + half), (0, wide))),
        ((half, side), (LANES, loads), ((side, side + half), (wide, 2 * wide))),
    ):
        size = (rows[1] - rows[0], lanes[1] - lanes[0])
        at = (lax.broadcasted_iota(jnp.int32, size, 0) + rows[0]).astype(F32)
        a, b, c, y = (m[there[0][0] : there[0][1], there[1][0] : there[1][1]] for m in (in_a, in_b, in_c, in_y))
        west, east, north, south = (
            flexed[k * side + rows[0] : k * side + rows[1], lanes[0] : lanes[1]] for k in range(SIDES)
        )

        def half_jump(count, inside, ahead, behind):
            return jnp.where(jnp.logical_and(at < count, inside), 0.5 * (ahead - behind), 0.0)

        results = (
            west + half_jump(count_west, col > 0, jnp.where(odd_b, a, b), west),
            east - half_jump(count_east, col < N_GY - 1, east, jnp.where(odd_b, b, a)),
            north + half_jump(count_north, row > 0, jnp.where(odd_a, c, y), north),
            south - half_jump(count_south, row < N_GX - 1, south, jnp.where(odd_a, y, c)),
        )
        for k, result in enumerate(results):
            balanced[k * side + rows[0] : k * side + rows[1], lanes[0] : lanes[1]] = result.astype(BF16)
    corners = told.shape[1]
    message[...] = extra[...]
    message[:, 0:loads] = dot(stiff[0:32, :], balanced[...])[:corners]
    for k in range(told.shape[0]):
        told[k] = message[...]


def step_on(steps, flex, dir_low, low, new_dir_low, flex_base):
    new_dir = steps[0] * dir_low + steps[1] * low
    new_dir_low[...] = new_dir
    flex_base[...] = dot(flex[:, TOP:], new_dir.astype(BF16))


def first_bulk_kernel(steps, after, balanced, stiff, flex, right, *outs):
    right = right[...].T
    res_top, res_low, sol_top, sol_low, squares = outs[:5]
    stiffed = dot(stiff[...], balanced[...])
    direction = right / cheb_center
    low = right[TOP:, :] - stiffed[TOP:]
    res_top[...] = right[:TOP, :] - stiffed[:TOP]
    res_low[...] = low
    sol_top[...] = direction[:TOP]
    sol_low[...] = direction[TOP:]
    squares[...] = jnp.sum(low * low, axis=0, keepdims=True)
    step_on(steps, flex, direction[TOP:], low, *outs[5:])


def bulk_kernel(steps, balanced, stiff, flex, res_top, res_low, dir_top, dir_low, sol_top, sol_low, *outs):
    new_res_top, new_res_low, new_sol_top, new_sol_low, squares = outs[:5]
    stiffed = dot(stiff[...], balanced[...])
    low = res_low[...] - stiffed[TOP:]
    new_res_top[...] = res_top[...] - stiffed[:TOP]
    new_res_low[...] = low
    new_sol_top[...] = sol_top[...] + dir_top[...]
    new_sol_low[...] = sol_low[...] + dir_low[...]
    squares[...] = jnp.sum(low * low, axis=0, keepdims=True)
    if steps is not None:
        step_on(steps, flex, dir_low[...], low, *outs[5:])


def split_dot(high, low, values):
    values_high, values_low = split(values)
    return dot(high[...], values_high) + (dot(high[...], values_low) + dot(low[...], values_high))


def tree_sum(parts):
    while len(parts) > 1:
        parts = [p + q for p, q in zip(parts[::2], parts[1::2])]
    return parts[0]


def first_half_kernel(high, low, values, total):
    total[...] = split_dot(high, low, values[...].reshape(-1, values.shape[2]))


def first_product_kernel(after, high, low, values, half, total):
    more = split_dot(high, low, values[...].reshape(-1, values.shape[2]))
    total[...] = (half[...] + more).reshape(total.shape)


def gathered(where, blocks, stack):
    corners = blocks[0].shape[1]
    for k, block in enumerate(blocks):
        at = pl.multiple_of(((where[0] + NY - k) % NY) * corners, TILE)
        stack[pl.ds(at, corners), :] = block[0]
    b = [block[0, 0:TILE, :] for block in blocks]
    return (b[0] + b[2]) + (b[1] + b[3])


def half_product_kernel(where, high, low, *refs):
    blocks, total, ride, stack = refs[:NY], refs[NY], refs[NY + 1], refs[NY + 2]
    ride[...] = gathered(where, blocks, stack)
    total[...] = split_dot(high, low, stack[...])


def product_kernel(loads, where, after, high, low, half, ride, *refs):
    blocks, total, stack = refs[:NY], refs[NY], refs[NY + 1]
    both = ride[...] + gathered(where, blocks, stack)
    result = (half[...] + split_dot(high, low, stack[...])).reshape(total.shape)
    lane = lax.broadcasted_iota(jnp.int32, both.shape, 1)
    for k in range(total.shape[0]):
        total[k] = result[k]
        total[k, 0:TILE, :] = jnp.where(lane < loads, result[k, 0:TILE, :], both)


def correction_of(terms, squares, res_top, new_res_top, earlier):
    corners = terms.shape[1]
    total = tree_sum([terms[k] for k in range(terms.shape[0])])
    earlier[...] = total[0:TILE, :]
    new_res_top[...] = res_top[...]
    new_res_top[:corners, :] = res_top[:corners, :] - total[:, : res_top.shape[1]]
    top = new_res_top[...]
    return top, squares[...] + jnp.sum(top * top, axis=0, keepdims=True)


def last_kernel(terms, squares, res_top, new_res_top, earlier, told):
    _, norm = correction_of(terms, squares, res_top, new_res_top, earlier)
    padded = jnp.concatenate([norm, jnp.zeros((1, told.shape[2] - norm.shape[1]), F32)], axis=1)
    told[...] = jnp.broadcast_to(padded[None], told.shape)


def correct_kernel(steps, where, terms, squares, res_top, dir_top, flex, flex_base, *outs):
    new_res_top, earlier, extra, new_dir_top, flexed = outs[:5]
    top, norm = correction_of(terms, squares, res_top, new_res_top, earlier)
    new_dir = steps[0] * dir_top[...] + steps[1] * top
    new_dir_top[...] = new_dir
    flexed[...] = flex_base[...] + dot(flex[:, :TOP], new_dir.astype(BF16))
    send_sides(where, flexed, *outs[5:])
    loads, width = norm.shape[1], extra.shape[1]
    spare = width - loads
    padded = jnp.concatenate([norm, jnp.zeros((1, spare), F32)], axis=1)
    padded = jnp.broadcast_to(padded, (TILE, width))
    line = lax.broadcasted_iota(jnp.int32, padded.shape, 0)
    ride = jnp.zeros_like(padded)
    for n in range(-(-loads // spare)):
        ride = jnp.where(line == n, pltpu.roll(padded, (loads - n * spare) % width, 1), ride)
    extra[...] = jnp.zeros_like(extra)
    extra[0:TILE, :] = ride


def rider_values(earlier, loads):
    spare = earlier.shape[1] - loads
    lines = -(-loads // spare)
    return earlier[:lines, loads:].reshape(-1)[:loads]


def local(right_side, flex, stiff, coarse_inv, corner_map, side_rows):
    right = right_side[0, 0]
    flex_block = flex[0, 0]
    stiff_block = stiff[0, 0]
    order = flex_block.shape[0]
    side = order // SIDES
    loads = right.shape[0]
    width = -(-loads // LANES) * LANES
    corners = corner_map.shape[2]
    rows_held, cols_held = coarse_inv.shape
    half = N_GY * corners
    ids = corner_map[0, 0]
    where = jnp.concatenate([jnp.stack([lax.axis_index(a) for a in ALL]), side_rows[0, 0]])
    where = where.astype(jnp.int32)

    inv_t = coarse_inv.T
    inv_blocks = [inv_t]
    for k in range(1, NY):
        inv_blocks.append(turned(inv_t, "y", NY, k))

    sides = [shape(side + side // 2, LANES)] * SIDES
    ids_line = jnp.pad(ids.astype(F32), (0, LANES - corners))[None]
    from_hbm = [pltpu.with_memory_space_constraint(a, pltpu.HBM) for a in (right, flex_block)]
    flexed, extra, *sends = pl.pallas_call(
        first_kernel,
        grid=(SIDES,),
        out_shape=[shape(order, loads), shape(corners, width)] + sides,
        in_specs=[
            sm(),
            vm(),
            pl.BlockSpec((loads, order), lambda i: (0, 0)),
            pl.BlockSpec((side, order), lambda i: (i, 0)),
        ],
        out_specs=[vm() for _ in range(2 + SIDES)],
        compiler_params=pltpu.CompilerParams(vmem_limit_bytes=VMEM_BYTES),
        name="first",
    )(where, ids_line, *from_hbm)

    own_ids, *sends = lax.optimization_barrier((ids_line, *sends))
    own_ids = jnp.broadcast_to(own_ids[None], (N_GY, 1, LANES))
    own_ids = to_all(own_ids, GY).reshape(N_GY, LANES)
    other_ids = turned(own_ids, "c", NC, 1)
    own_rows, other_rows = call(
        rows_kernel, [shape(cols_held, half)] * 2, scalars=1, scratch=[pltpu.VMEM((2 * half, rows_held), BF16)]
    )(where, own_ids, other_ids, *inv_blocks)
    own_rows = own_rows + turned(other_rows, "c", NC, 1)

    row_parts = [own_rows]
    for k in range(1, NZ):
        row_parts.append(turned(own_rows, "z", NZ, k))

    tops, lows = shape(TOP, loads), shape(order - TOP, loads)
    ride_shape = shape(TILE, width)
    corner_scratch = [pltpu.VMEM((NY * corners, width), F32)]
    ordering = (own_rows,)
    rho_prev = 1.0 / cheb_sigma
    norms = []
    for iteration in range(ITERS):
        last = iteration + 1 == ITERS
        ins = []
        for k in range(SIDES):
            axes, count = (GY, N_GY) if k < 2 else (GX, N_GX)
            ins.append(swapped(sends[k], axes, count, k % 2))
        balanced, told = call(
            balance_kernel,
            [shape(order, loads, dtype=BF16), shape(NY * NX if iteration == 0 else 1, corners, width)],
            scalars=1,
            scratch=[pltpu.VMEM((corners, width), F32)],
        )(where, flexed, *ins, stiff_block, extra, *ordering)
        ordering = ()
        steps = None
        if not last:
            rho_next = 1.0 / (2.0 * cheb_sigma - rho_prev)
            steps = (rho_next * rho_prev, 2.0 * rho_next / cheb_half)
            rho_prev = rho_next
        if iteration == 0:
            values = to_all(told, ("y", "x"))
            kernel, state = first_bulk_kernel, (right,)
            order_after = (values,)
        else:
            values = [told]
            for k in range(1, NY):
                values.append(turned(told, "y", NY, k))
            kernel, state = bulk_kernel, (res_top, res_low, dir_top, dir_low, sol_top, sol_low)
            order_after = ()
        outs = call(
            functools.partial(kernel, steps),
            [tops, lows, tops, lows, shape(1, loads)] + ([] if last else [lows, shape(order, loads)]),
        )(*order_after, balanced, stiff_block, flex_block, *state)
        res_top, res_low, sol_top, sol_low, squares = outs[:5]
        if iteration == 0:
            dir_top = sol_top
            values_other = turned(values, "c", NC, 1)
            own_high, own_low, other_high, other_low, *shares = call(
                cols_kernel,
                [shape(half, half, dtype=BF16)] * 4 + [shape(half // NX * 2, half)] * NX,
                scalars=1,
                scratch=[pltpu.VMEM((2 * half, cols_held), BF16), pltpu.VMEM((2 * half, half), F32)],
            )(where, values, values_other, *row_parts)
            (partial,) = call(first_half_kernel, [shape(half, width)])(own_high, own_low, values)
            (partial,) = call(first_product_kernel, [shape(N_GY, corners, width)])(
                squares, other_high, other_low, values_other, partial
            )
            for k in range(1, NX):
                shares[k] = turned(shares[k], "x", NX, k)
            block = call(block_kernel, [shape(half, NY * corners, dtype=BF16)] * 4)(*shares)
        else:
            others = []
            for k in range(NY):
                others.append(turned(values[k], "c", NC, 1))
            partial, ride = call(
                half_product_kernel, [shape(half, width), ride_shape], scalars=1, scratch=corner_scratch
            )(where, *block[:2], *values)
            (partial,) = call(
                functools.partial(product_kernel, loads),
                [shape(N_GY, corners, width)],
                scalars=1,
                scratch=corner_scratch,
            )(where, squares, *block[2:], partial, ride, *others)
        terms = to_all(partial, GY)
        if last:
            res_top, earlier, told = call(
                last_kernel, [tops, ride_shape, shape(N_GX * N_GY, 1, width)]
            )(terms, squares, res_top)
        else:
            dir_low, flex_base = outs[5:]
            res_top, earlier, extra, dir_top, flexed, *sends = call(
                functools.partial(correct_kernel, steps),
                [tops, ride_shape, shape(corners, width), tops, shape(order, loads)] + sides,
                scalars=1,
            )(where, terms, squares, res_top, dir_top, flex_block, flex_base)
        if iteration > 0:
            norms.append(rider_values(earlier, loads))
    norms.append(to_all(told, ALL).sum(axis=0)[0, :loads])
    resid_norm = jnp.sqrt(jnp.stack(norms) / (N_GX * N_GY * order))
    solution = jnp.concatenate([sol_top, sol_low]).T
    residual = jnp.concatenate([res_top, res_low]).T
    return (solution[None, None], residual[None, None], resid_norm)


def solution(mesh):
    torus = Mesh(mesh.devices.reshape(NY, NC, NX, NZ), ALL)
    return jax.shard_map(
        local,
        mesh=torus,
        in_specs=(
            P(GX, GY, None, None),
            P(GX, GY, None, None),
            P(GX, GY, None, None),
            P(GX, GY),
            P(GX, GY, None),
            P(GX, GY, None),
        ),
        out_specs=(P(GX, GY, None, None), P(GX, GY, None, None), P()),
        check_vma=False,
    )
```

```python
import functools

import jax
import jax.numpy as jnp
from jax import lax
from jax.experimental import pallas as pl
from jax.experimental.pallas import tpu as pltpu
from jax.sharding import Mesh
from jax.sharding import PartitionSpec as P

ITERS = 3
GX = ("y", "c")
GY = ("x", "z")
ALL = ("y", "c", "x", "z")
NY, NC, NX, NZ = 4, 2, 4, 4
N_GX, N_GY = NY * NC, NX * NZ
SIDES = 4
TOP = 128
LANES = 128
TILE = 8
VMEM_BYTES = 16 * 2**20

cheb_center = 1.15
cheb_half = 0.85
cheb_sigma = cheb_center / cheb_half
F32 = jnp.float32
BF16 = jnp.bfloat16


def turned(array, axes, count, by):
    return lax.ppermute(array, axes, [(i, (i + by) % count) for i in range(count)])


def swapped(array, axes, count, shift):
    pairs = [(i, (((i + shift) ^ 1) - shift) % count) for i in range(count)]
    return lax.ppermute(array, axes, pairs)


def to_all(copies, axes):
    return lax.all_to_all(copies, axes, split_axis=0, concat_axis=0, tiled=True)


def vm():
    return pl.BlockSpec(memory_space=pltpu.VMEM)


def sm():
    return pl.BlockSpec(memory_space=pltpu.SMEM)


def call(body, outs, scratch=()):
    def run(*operands):
        return pl.pallas_call(
            body,
            out_shape=outs,
            in_specs=[vm() for _ in operands],
            out_specs=[vm() for _ in outs],
            scratch_shapes=scratch,
            compiler_params=pltpu.CompilerParams(vmem_limit_bytes=VMEM_BYTES),
        )(*[pltpu.with_memory_space_constraint(o, pltpu.VMEM) for o in operands])

    return run


def shape(*dims, dtype=F32):
    return pltpu.VMEM(dims, dtype)


def dot(a, b, contract=((1,), (0,))):
    return lax.dot_general(a, b, (contract, ((), ())), preferred_element_type=F32)


def split(a):
    high = a.astype(BF16)
    return high, (a - high.astype(F32)).astype(BF16)


def mark(pick, columns, held):
    corners = columns[0].shape[0]
    at = lax.broadcasted_iota(jnp.int32, (2 * corners, held), 1).astype(F32)
    for n in range(0, len(columns), 2):
        ids = jnp.concatenate(columns[n : n + 2], axis=0)
        pick[n * corners : (n + 2) * corners, :] = jnp.where(at == ids, 1.0, 0.0).astype(BF16)


def rows_kernel(facts, *refs):
    blocks, own, other, pick = refs[:-3], refs[-3], refs[-2], refs[-1]
    my_y, my_c = lax.axis_index("y"), lax.axis_index("c")
    held = blocks[0].shape[1]
    half = own.shape[1]
    corners = half // N_GY
    lists = []
    for core in (my_c, 1 - my_c):
        start = pl.multiple_of((my_y * NC + core) * N_GY, TILE)
        lists.append(facts[pl.ds(start, N_GY), :].T[:corners])
    total = 0.0
    for k, block in enumerate(blocks):
        base = ((((my_y + NY - k) % NY) * NC + my_c) * held).astype(F32)
        shifted = [ids - base for ids in lists]
        mark(pick, [ids[:, n : n + 1] for ids in shifted for n in range(N_GY)], held)
        for part in split(block[...]):
            total = total + dot(part, pick[...], ((1,), (1,)))
    own[...] = total[:, :half]
    other[...] = total[:, half:]


def cols_kernel(facts, *refs):
    blocks, sends, pick, total, lines = refs[:NZ], refs[NZ:-3], refs[-3], refs[-2], refs[-1]
    my_c, my_x, my_z = (lax.axis_index(a) for a in ("c", "x", "z"))
    held = blocks[0].shape[0]
    corners = sends[0].shape[0] // (NC * NY)
    columns = []
    for core in (my_c, 1 - my_c):
        for n in range(NY * NX):
            at = (((n // NX) * NC + core) * NX + n % NX) * NZ + my_z
            lines[n : n + 1, :] = facts[pl.ds(at, 1), :]
        turned_lines = lines[...].T[:corners]
        columns += [turned_lines[:, n : n + 1] for n in range(NY * NX)]
    summed = 0.0
    for k, block in enumerate(blocks):
        base = ((my_x * NZ + (my_z + NZ - k) % NZ) * held).astype(F32)
        mark(pick, [ids - base for ids in columns], held)
        for part in split(block[...]):
            summed = summed + dot(pick[...], part)
    total[...] = summed
    for k, send in enumerate(sends):
        for n in range(NC * NY):
            start = pl.multiple_of((n * NX + (my_x + k) % NX) * corners, TILE)
            send[n * corners : (n + 1) * corners, :] = total[pl.ds(start, corners), :]


def block_kernel(*refs):
    parts, outs = refs[:NX], refs[NX:]
    block = ((parts[0][...] + parts[1][...]) + (parts[2][...] + parts[3][...])).T
    half = block.shape[1] // 2
    for n in range(2):
        outs[2 * n][...], outs[2 * n + 1][...] = split(block[:, n * half : (n + 1) * half])


def pack(out, main, rest, count):
    side, wide = main.shape[0], rest.shape[1]
    half = side // 2
    out[0:side, :] = main
    out[side : side + half, 0:wide] = rest[:half]
    out[side : side + half, wide : 2 * wide] = rest[half:]
    out[side : side + half, 2 * wide :] = jnp.broadcast_to(count[:, 2 * wide :], (half, LANES - 2 * wide))


def sent_sides():
    odd_b, odd_a = lax.axis_index("z") % 2, lax.axis_index("c")
    return (1 - odd_b, odd_b, 3 - odd_a, 2 + odd_a)


def first_kernel(side_rows, after, right, flex, flexed, extra, counts, *refs):
    sends, direction = refs[:-1], refs[-1]
    step = pl.program_id(0)
    side = flex.shape[0]

    @pl.when(step == 0)
    def _():
        direction[...] = (right[...] / cheb_center).astype(BF16).T
        extra[...] = jnp.zeros_like(extra)
        line = lax.broadcasted_iota(jnp.int32, counts.shape, 0)
        east, south = side_rows[0].astype(F32), side_rows[1].astype(F32)
        counts[...] = jnp.where(line == 0, east, south)

    part = dot(flex[...], direction[...])
    flexed[pl.ds(pl.multiple_of(step * side, side), side), :] = part
    for k, wanted in enumerate(sent_sides()):

        @pl.when(step == wanted)
        def _():
            pack(sends[k], part[:, :LANES], part[:, LANES:], counts[k // 2 : k // 2 + 1, :])


def send_sides(counts, flexed, *sends):
    side = flexed.shape[0] // SIDES
    for k, wanted in enumerate(sent_sides()):
        rows = pl.ds(pl.multiple_of(wanted * side, 32), side)
        pack(sends[k], flexed[rows, 0:LANES], flexed[rows, LANES:], counts[k // 2 : k // 2 + 1, :])


def balance_kernel(counts, flexed, in_a, in_b, in_c, in_y, stiff, extra, balanced, told):
    side = flexed.shape[0] // SIDES
    loads = flexed.shape[1]
    wide = loads - LANES
    half = side // 2
    my_y, my_c, my_x, my_z = (lax.axis_index(a) for a in ALL)
    row = my_y * NC + my_c
    col = my_x * NZ + my_z
    odd_b, odd_a = my_z % 2 == 1, my_c == 1
    spot = (slice(side, side + 1), slice(2 * wide, 2 * wide + 1))
    count_west = jnp.where(odd_b, in_a[spot], in_b[spot])
    count_north = jnp.where(odd_a, in_c[spot], in_y[spot])
    count_east = counts[0:1, 0:1]
    count_south = counts[1:2, 0:1]

    for rows, lanes, there in (
        ((0, side), (0, LANES), ((0, side), (0, LANES))),
        ((0, half), (LANES, loads), ((side, side + half), (0, wide))),
        ((half, side), (LANES, loads), ((side, side + half), (wide, 2 * wide))),
    ):
        size = (rows[1] - rows[0], lanes[1] - lanes[0])
        at = (lax.broadcasted_iota(jnp.int32, size, 0) + rows[0]).astype(F32)
        a, b, c, y = (m[there[0][0] : there[0][1], there[1][0] : there[1][1]] for m in (in_a, in_b, in_c, in_y))
        west, east, north, south = (
            flexed[k * side + rows[0] : k * side + rows[1], lanes[0] : lanes[1]] for k in range(SIDES)
        )

        def half_jump(count, inside, ahead, behind):
            return jnp.where(jnp.logical_and(at < count, inside), 0.5 * (ahead - behind), 0.0)

        results = (
            west + half_jump(count_west, col > 0, jnp.where(odd_b, a, b), west),
            east - half_jump(count_east, col < N_GY - 1, east, jnp.where(odd_b, b, a)),
            north + half_jump(count_north, row > 0, jnp.where(odd_a, c, y), north),
            south - half_jump(count_south, row < N_GX - 1, south, jnp.where(odd_a, y, c)),
        )
        for k, result in enumerate(results):
            balanced[k * side + rows[0] : k * side + rows[1], lanes[0] : lanes[1]] = result.astype(BF16)
    corners = told.shape[1]
    told[0] = extra[...]
    told[0, :, 0:loads] = dot(stiff[0:32, :], balanced[...])[:corners]


def step_on(steps, flex, dir_low, low, new_dir_low, flex_base):
    new_dir = steps[0] * dir_low + steps[1] * low
    new_dir_low[...] = new_dir
    flex_base[...] = dot(flex[:, TOP:], new_dir.astype(BF16))


def first_bulk_kernel(steps, balanced, stiff, flex, right, *outs):
    right = right[...].T
    res_top, res_low, sol_top, sol_low, squares = outs[:5]
    stiffed = dot(stiff[...], balanced[...])
    direction = right / cheb_center
    low = right[TOP:, :] - stiffed[TOP:]
    res_top[...] = right[:TOP, :] - stiffed[:TOP]
    res_low[...] = low
    sol_top[...] = direction[:TOP]
    sol_low[...] = direction[TOP:]
    squares[...] = jnp.sum(low * low, axis=0, keepdims=True)
    step_on(steps, flex, direction[TOP:], low, *outs[5:])


def bulk_kernel(steps, balanced, stiff, flex, res_top, res_low, dir_top, dir_low, sol_top, sol_low, *outs):
    new_res_top, new_res_low, new_sol_top, new_sol_low, squares = outs[:5]
    stiffed = dot(stiff[...], balanced[...])
    low = res_low[...] - stiffed[TOP:]
    new_res_top[...] = res_top[...] - stiffed[:TOP]
    new_res_low[...] = low
    new_sol_top[...] = sol_top[...] + dir_top[...]
    new_sol_low[...] = sol_low[...] + dir_low[...]
    squares[...] = jnp.sum(low * low, axis=0, keepdims=True)
    if steps is not None:
        step_on(steps, flex, dir_low[...], low, *outs[5:])


def split_dot(high, low, values):
    values_high, values_low = split(values)
    return dot(high[...], values_high) + (dot(high[...], values_low) + dot(low[...], values_high))


def tree_sum(parts):
    while len(parts) > 1:
        parts = [p + q for p, q in zip(parts[::2], parts[1::2])]
    return parts[0]


def gathered(blocks, stack):
    my_y = lax.axis_index("y")
    corners = blocks[0].shape[1]
    for k, block in enumerate(blocks):
        at = pl.multiple_of(((my_y + NY - k) % NY) * corners, TILE)
        stack[pl.ds(at, corners), :] = block[0]
    b = [block[0, 0:TILE, :] for block in blocks]
    return (b[0] + b[2]) + (b[1] + b[3])


def half_product_kernel(high, low, *refs):
    blocks, total, ride, stack = refs[:NY], refs[NY], refs[NY + 1], refs[NY + 2]
    ride[...] = gathered(blocks, stack)
    total[...] = split_dot(high, low, stack[...])


def product_kernel(loads, after, high, low, half, ride, *refs):
    blocks, total, stack = refs[:NY], refs[NY], refs[NY + 1]
    both = ride[...] + gathered(blocks, stack)
    result = (half[...] + split_dot(high, low, stack[...])).reshape(total.shape)
    lane = lax.broadcasted_iota(jnp.int32, both.shape, 1)
    for k in range(total.shape[0]):
        total[k] = result[k]
        total[k, 0:TILE, :] = jnp.where(lane < loads, result[k, 0:TILE, :], both)


def correction_of(terms, squares, res_top, new_res_top, earlier):
    corners = terms.shape[1]
    total = tree_sum([terms[k] for k in range(terms.shape[0])])
    earlier[...] = total[0:TILE, :]
    new_res_top[...] = res_top[...]
    new_res_top[:corners, :] = res_top[:corners, :] - total[:, : res_top.shape[1]]
    top = new_res_top[...]
    return top, squares[...] + jnp.sum(top * top, axis=0, keepdims=True)


def last_kernel(terms, squares, res_top, new_res_top, earlier, told):
    _, norm = correction_of(terms, squares, res_top, new_res_top, earlier)
    padded = jnp.concatenate([norm, jnp.zeros((1, told.shape[2] - norm.shape[1]), F32)], axis=1)
    told[...] = jnp.broadcast_to(padded[None], told.shape)


def correct_kernel(steps, counts, terms, squares, res_top, dir_top, flex, flex_base, *outs):
    new_res_top, earlier, extra, new_dir_top, flexed = outs[:5]
    top, norm = correction_of(terms, squares, res_top, new_res_top, earlier)
    new_dir = steps[0] * dir_top[...] + steps[1] * top
    new_dir_top[...] = new_dir
    flexed[...] = flex_base[...] + dot(flex[:, :TOP], new_dir.astype(BF16))
    send_sides(counts, flexed, *outs[5:])
    loads, width = norm.shape[1], extra.shape[1]
    spare = width - loads
    padded = jnp.concatenate([norm, jnp.zeros((1, spare), F32)], axis=1)
    padded = jnp.broadcast_to(padded, (TILE, width))
    line = lax.broadcasted_iota(jnp.int32, padded.shape, 0)
    ride = jnp.zeros_like(padded)
    for n in range(-(-loads // spare)):
        ride = jnp.where(line == n, pltpu.roll(padded, (loads - n * spare) % width, 1), ride)
    extra[...] = jnp.zeros_like(extra)
    extra[0:TILE, :] = ride


def rider_values(earlier, loads):
    spare = earlier.shape[1] - loads
    lines = -(-loads // spare)
    return earlier[:lines, loads:].reshape(-1)[:loads]


def local(right_side, flex, stiff, coarse_inv, corner_map, side_rows):
    right = right_side[0, 0]
    flex_block = flex[0, 0]
    stiff_block = stiff[0, 0]
    order = flex_block.shape[0]
    side = order // SIDES
    loads = right.shape[0]
    width = -(-loads // LANES) * LANES
    corners = corner_map.shape[2]
    rows_held, cols_held = coarse_inv.shape
    half = N_GY * corners
    inv_t = coarse_inv.T
    inv_blocks = [inv_t]
    for k in range(1, NY):
        inv_blocks.append(turned(inv_t, "y", NY, k))

    facts = jnp.pad(corner_map[0, 0].astype(F32), (0, LANES - corners))
    facts = jnp.broadcast_to(facts[None, None], (N_GX * N_GY, 1, LANES))
    facts = to_all(facts, ALL).reshape(N_GX * N_GY, LANES)

    own_rows, other_rows = call(
        rows_kernel, [shape(cols_held, half)] * 2, scratch=[pltpu.VMEM((2 * half, rows_held), BF16)]
    )(facts, *inv_blocks)
    own_rows = own_rows + turned(other_rows, "c", NC, 1)

    row_parts = [own_rows]
    for k in range(1, NZ):
        row_parts.append(turned(own_rows, "z", NZ, k))

    sides = [shape(side + side // 2, LANES)] * SIDES
    from_hbm = [pltpu.with_memory_space_constraint(a, pltpu.HBM) for a in (right, flex_block)]
    flexed, extra, counts, *sends = pl.pallas_call(
        first_kernel,
        grid=(SIDES,),
        out_shape=[shape(order, loads), shape(corners, width), shape(TILE, LANES)] + sides,
        in_specs=[
            sm(),
            vm(),
            pl.BlockSpec((loads, order), lambda i: (0, 0)),
            pl.BlockSpec((side, order), lambda i: (i, 0)),
        ],
        out_specs=[vm() for _ in range(3 + SIDES)],
        scratch_shapes=[pltpu.VMEM((order, loads), BF16)],
        compiler_params=pltpu.CompilerParams(vmem_limit_bytes=VMEM_BYTES),
        name="first",
    )(side_rows[0, 0], pltpu.with_memory_space_constraint(facts, pltpu.VMEM), *from_hbm)

    shares = list(call(
        cols_kernel,
        [shape(half // NX * 2, half)] * NX,
        scratch=[
            pltpu.VMEM((2 * half, cols_held), BF16),
            pltpu.VMEM((2 * half, half), F32),
            pltpu.VMEM((NY * NX, LANES), F32),
        ],
    )(facts, *row_parts))
    for k in range(1, NX):
        shares[k] = turned(shares[k], "x", NX, k)
    block = call(block_kernel, [shape(half, NY * corners, dtype=BF16)] * 4)(*shares)

    tops, lows = shape(TOP, loads), shape(order - TOP, loads)
    ride_shape = shape(TILE, width)
    corner_scratch = [pltpu.VMEM((NY * corners, width), F32)]
    rho_prev = 1.0 / cheb_sigma
    norms = []
    for iteration in range(ITERS):
        last = iteration + 1 == ITERS
        ins = []
        for k in range(SIDES):
            axes, count = (GY, N_GY) if k < 2 else (GX, N_GX)
            ins.append(swapped(sends[k], axes, count, k % 2))
        balanced, told = call(
            balance_kernel, [shape(order, loads, dtype=BF16), shape(1, corners, width)]
        )(counts, flexed, *ins, stiff_block, extra)
        values = [told]
        for k in range(1, NY):
            values.append(turned(told, "y", NY, k))
        steps = None
        if not last:
            rho_next = 1.0 / (2.0 * cheb_sigma - rho_prev)
            steps = (rho_next * rho_prev, 2.0 * rho_next / cheb_half)
            rho_prev = rho_next
        if iteration == 0:
            kernel, state = first_bulk_kernel, (right,)
        else:
            kernel, state = bulk_kernel, (res_top, res_low, dir_top, dir_low, sol_top, sol_low)
        outs = call(
            functools.partial(kernel, steps),
            [tops, lows, tops, lows, shape(1, loads)] + ([] if last else [lows, shape(order, loads)]),
        )(balanced, stiff_block, flex_block, *state)
        res_top, res_low, sol_top, sol_low, squares = outs[:5]
        if iteration == 0:
            dir_top = sol_top
        others = []
        for k in range(NY):
            others.append(turned(values[k], "c", NC, 1))
        partial, ride = call(
            half_product_kernel, [shape(half, width), ride_shape], scratch=corner_scratch
        )(*block[:2], *values)
        (partial,) = call(
            functools.partial(product_kernel, loads),
            [shape(N_GY, corners, width)],
            scratch=corner_scratch,
        )(squares, *block[2:], partial, ride, *others)
        terms = to_all(partial, GY)
        if last:
            res_top, earlier, told = call(
                last_kernel, [tops, ride_shape, shape(N_GX * N_GY, 1, width)]
            )(terms, squares, res_top)
        else:
            dir_low, flex_base = outs[5:]
            res_top, earlier, extra, dir_top, flexed, *sends = call(
                functools.partial(correct_kernel, steps),
                [tops, ride_shape, shape(corners, width), tops, shape(order, loads)] + sides,
            )(counts, terms, squares, res_top, dir_top, flex_block, flex_base)
        if iteration > 0:
            norms.append(rider_values(earlier, loads))
    norms.append(to_all(told, ALL).sum(axis=0)[0, :loads])
    resid_norm = jnp.sqrt(jnp.stack(norms) / (N_GX * N_GY * order))
    solution = jnp.concatenate([sol_top, sol_low]).T
    residual = jnp.concatenate([res_top, res_low]).T
    return (solution[None, None], residual[None, None], resid_norm)


def solution(mesh):
    torus = Mesh(mesh.devices.reshape(NY, NC, NX, NZ), ALL)
    return jax.shard_map(
        local,
        mesh=torus,
        in_specs=(
            P(GX, GY, None, None),
            P(GX, GY, None, None),
            P(GX, GY, None, None),
            P(GX, GY),
            P(GX, GY, None),
            P(GX, GY, None),
        ),
        out_specs=(P(GX, GY, None, None), P(GX, GY, None, None), P()),
        check_vma=False,
    )
```

```python
import functools

import jax
import jax.numpy as jnp
from jax import lax
from jax.experimental import pallas as pl
from jax.experimental.pallas import tpu as pltpu
from jax.sharding import Mesh
from jax.sharding import PartitionSpec as P

ITERS = 3
GX = ("y", "c")
GY = ("x", "z")
ALL = ("y", "c", "x", "z")
NY, NC, NX, NZ = 4, 2, 4, 4
N_GX, N_GY = NY * NC, NX * NZ
SIDES = 4
TOP = 128
LANES = 128
TILE = 8
VMEM_BYTES = 16 * 2**20

cheb_center = 1.15
cheb_half = 0.85
cheb_sigma = cheb_center / cheb_half
F32 = jnp.float32
BF16 = jnp.bfloat16


def turned(array, axes, count, by):
    return lax.ppermute(array, axes, [(i, (i + by) % count) for i in range(count)])


def swapped(array, axes, count, shift):
    pairs = [(i, (((i + shift) ^ 1) - shift) % count) for i in range(count)]
    return lax.ppermute(array, axes, pairs)


def to_all(copies, axes):
    return lax.all_to_all(copies, axes, split_axis=0, concat_axis=0, tiled=True)


def vm():
    return pl.BlockSpec(memory_space=pltpu.VMEM)


def call(body, outs, scratch=()):
    def run(*operands):
        return pl.pallas_call(
            body,
            out_shape=outs,
            in_specs=[vm() for _ in operands],
            out_specs=[vm() for _ in outs],
            scratch_shapes=scratch,
            compiler_params=pltpu.CompilerParams(vmem_limit_bytes=VMEM_BYTES),
        )(*[pltpu.with_memory_space_constraint(o, pltpu.VMEM) for o in operands])

    return run


def shape(*dims, dtype=F32):
    return pltpu.VMEM(dims, dtype)


def dot(a, b, contract=((1,), (0,))):
    return lax.dot_general(a, b, (contract, ((), ())), preferred_element_type=F32)


def split(a):
    high = a.astype(BF16)
    return high, (a - high.astype(F32)).astype(BF16)


def mark(pick, columns, held):
    corners = columns[0].shape[0]
    at = lax.broadcasted_iota(jnp.int32, (2 * corners, held), 1).astype(F32)
    for n in range(0, len(columns), 2):
        ids = jnp.concatenate(columns[n : n + 2], axis=0)
        pick[n * corners : (n + 2) * corners, :] = jnp.where(at == ids, 1.0, 0.0).astype(BF16)


def rows_kernel(ids_own, ids_other, *refs):
    blocks, own, other, pick = refs[:-3], refs[-3], refs[-2], refs[-1]
    my_y, my_c = lax.axis_index("y"), lax.axis_index("c")
    held = blocks[0].shape[1]
    half = own.shape[1]
    corners = half // N_GY
    lists = [ids[...].T[:corners] for ids in (ids_own, ids_other)]
    total = 0.0
    for k, block in enumerate(blocks):
        base = ((((my_y + NY - k) % NY) * NC + my_c) * held).astype(F32)
        shifted = [ids - base for ids in lists]
        mark(pick, [ids[:, n : n + 1] for ids in shifted for n in range(N_GY)], held)
        for part in split(block[...]):
            total = total + dot(part, pick[...], ((1,), (1,)))
    own[...] = total[:, :half]
    other[...] = total[:, half:]


def cols_kernel(own, other, *refs):
    blocks, outs, sends, pick, total = refs[:NZ], refs[NZ : NZ + 4], refs[NZ + 4 : -2], refs[-2], refs[-1]
    my_x, my_z = lax.axis_index("x"), lax.axis_index("z")
    held = blocks[0].shape[0]
    half = outs[0].shape[1]
    last = own.shape[2] - 1
    corners = own.shape[1]
    columns = [v[n, :, last:] for v in (own, other) for n in range(v.shape[0])]
    summed = 0.0
    for k, block in enumerate(blocks):
        base = ((my_x * NZ + (my_z + NZ - k) % NZ) * held).astype(F32)
        mark(pick, [ids - base for ids in columns], held)
        for part in split(block[...]):
            summed = summed + dot(pick[...], part)
    total[...] = summed
    for n in range(2):
        outs[2 * n][...], outs[2 * n + 1][...] = split(summed[n * half : (n + 1) * half].T)
    for k, send in enumerate(sends):
        for n in range(NC * NY):
            start = pl.multiple_of((n * NX + (my_x + k) % NX) * corners, TILE)
            send[n * corners : (n + 1) * corners, :] = total[pl.ds(start, corners), :]


def block_kernel(*refs):
    parts, outs = refs[:NX], refs[NX:]
    block = ((parts[0][...] + parts[1][...]) + (parts[2][...] + parts[3][...])).T
    half = block.shape[1] // 2
    for n in range(2):
        outs[2 * n][...], outs[2 * n + 1][...] = split(block[:, n * half : (n + 1) * half])


def pack(out, main, rest, count):
    side, wide = main.shape[0], rest.shape[1]
    half = side // 2
    out[0:side, :] = main
    out[side : side + half, 0:wide] = rest[:half]
    out[side : side + half, wide : 2 * wide] = rest[half:]
    out[side : side + half, 2 * wide :] = jnp.broadcast_to(count[:, 2 * wide :], (half, LANES - 2 * wide))


def sent_sides():
    odd_b, odd_a = lax.axis_index("z") % 2, lax.axis_index("c")
    return (1 - odd_b, odd_b, 3 - odd_a, 2 + odd_a)


def first_kernel(after, ids, live, right, flex, flexed, extra, counts, *sends):
    direction = (right[...] / cheb_center).astype(BF16)
    flexed[...] = dot(flex[...], direction, ((1,), (1,)))
    counts[0:1, :] = jnp.broadcast_to(live[0:1, 0:1], (1, LANES))
    counts[1:2, :] = jnp.broadcast_to(live[0:1, 1:2], (1, LANES))
    send_sides(counts, flexed, *sends)
    column = jnp.broadcast_to(ids[...], (LANES, LANES)).T
    extra[...] = jnp.zeros_like(extra)
    extra[:, extra.shape[1] - LANES :] = column[: extra.shape[0]]


def send_sides(counts, flexed, *sends):
    side = flexed.shape[0] // SIDES
    for k, wanted in enumerate(sent_sides()):
        rows = pl.ds(pl.multiple_of(wanted * side, 32), side)
        pack(sends[k], flexed[rows, 0:LANES], flexed[rows, LANES:], counts[k // 2 : k // 2 + 1, :])


def balance_kernel(counts, flexed, in_a, in_b, in_c, in_y, stiff, extra, balanced, told):
    side = flexed.shape[0] // SIDES
    loads = flexed.shape[1]
    wide = loads - LANES
    half = side // 2
    my_y, my_c, my_x, my_z = (lax.axis_index(a) for a in ALL)
    row = my_y * NC + my_c
    col = my_x * NZ + my_z
    odd_b, odd_a = my_z % 2 == 1, my_c == 1
    spot = (slice(side, side + 1), slice(2 * wide, 2 * wide + 1))
    count_west = jnp.where(odd_b, in_a[spot], in_b[spot])
    count_north = jnp.where(odd_a, in_c[spot], in_y[spot])
    count_east = counts[0:1, 0:1]
    count_south = counts[1:2, 0:1]

    for rows, lanes, there in (
        ((0, side), (0, LANES), ((0, side), (0, LANES))),
        ((0, half), (LANES, loads), ((side, side + half), (0, wide))),
        ((half, side), (LANES, loads), ((side, side + half), (wide, 2 * wide))),
    ):
        size = (rows[1] - rows[0], lanes[1] - lanes[0])
        at = (lax.broadcasted_iota(jnp.int32, size, 0) + rows[0]).astype(F32)
        a, b, c, y = (m[there[0][0] : there[0][1], there[1][0] : there[1][1]] for m in (in_a, in_b, in_c, in_y))
        west, east, north, south = (
            flexed[k * side + rows[0] : k * side + rows[1], lanes[0] : lanes[1]] for k in range(SIDES)
        )

        def half_jump(count, inside, ahead, behind):
            return jnp.where(jnp.logical_and(at < count, inside), 0.5 * (ahead - behind), 0.0)

        results = (
            west + half_jump(count_west, col > 0, jnp.where(odd_b, a, b), west),
            east - half_jump(count_east, col < N_GY - 1, east, jnp.where(odd_b, b, a)),
            north + half_jump(count_north, row > 0, jnp.where(odd_a, c, y), north),
            south - half_jump(count_south, row < N_GX - 1, south, jnp.where(odd_a, y, c)),
        )
        for k, result in enumerate(results):
            balanced[k * side + rows[0] : k * side + rows[1], lanes[0] : lanes[1]] = result.astype(BF16)
    corners = told.shape[1]
    told[0] = extra[...]
    told[0, :, 0:loads] = dot(stiff[0:32, :], balanced[...])[:corners]
    for k in range(1, told.shape[0]):
        told[k] = told[0]


def step_on(steps, flex, dir_low, low, new_dir_low, flex_base):
    new_dir = steps[0] * dir_low + steps[1] * low
    new_dir_low[...] = new_dir
    flex_base[...] = dot(flex[:, TOP:], new_dir.astype(BF16))


def first_bulk_kernel(steps, after, balanced, stiff, flex, right, *outs):
    right = right[...].T
    res_top, res_low, sol_top, sol_low, squares = outs[:5]
    stiffed = dot(stiff[...], balanced[...])
    direction = right / cheb_center
    low = right[TOP:, :] - stiffed[TOP:]
    res_top[...] = right[:TOP, :] - stiffed[:TOP]
    res_low[...] = low
    sol_top[...] = direction[:TOP]
    sol_low[...] = direction[TOP:]
    squares[...] = jnp.sum(low * low, axis=0, keepdims=True)
    step_on(steps, flex, direction[TOP:], low, *outs[5:])


def bulk_kernel(steps, balanced, stiff, flex, res_top, res_low, dir_top, dir_low, sol_top, sol_low, *outs):
    new_res_top, new_res_low, new_sol_top, new_sol_low, squares = outs[:5]
    stiffed = dot(stiff[...], balanced[...])
    low = res_low[...] - stiffed[TOP:]
    new_res_top[...] = res_top[...] - stiffed[:TOP]
    new_res_low[...] = low
    new_sol_top[...] = sol_top[...] + dir_top[...]
    new_sol_low[...] = sol_low[...] + dir_low[...]
    squares[...] = jnp.sum(low * low, axis=0, keepdims=True)
    if steps is not None:
        step_on(steps, flex, dir_low[...], low, *outs[5:])


def split_dot(high, low, values):
    values_high, values_low = split(values)
    return dot(high[...], values_high) + (dot(high[...], values_low) + dot(low[...], values_high))


def tree_sum(parts):
    while len(parts) > 1:
        parts = [p + q for p, q in zip(parts[::2], parts[1::2])]
    return parts[0]


def first_half_kernel(high, low, values, total):
    total[...] = split_dot(high, low, values[...].reshape(-1, values.shape[2]))


def first_product_kernel(after, high, low, values, half, total):
    more = split_dot(high, low, values[...].reshape(-1, values.shape[2]))
    total[...] = (half[...] + more).reshape(total.shape)


def gathered(blocks, stack):
    my_y = lax.axis_index("y")
    corners = blocks[0].shape[1]
    for k, block in enumerate(blocks):
        at = pl.multiple_of(((my_y + NY - k) % NY) * corners, TILE)
        stack[pl.ds(at, corners), :] = block[0]
    b = [block[0, 0:TILE, :] for block in blocks]
    return (b[0] + b[2]) + (b[1] + b[3])


def half_product_kernel(high, low, *refs):
    blocks, total, ride, stack = refs[:NY], refs[NY], refs[NY + 1], refs[NY + 2]
    ride[...] = gathered(blocks, stack)
    total[...] = split_dot(high, low, stack[...])


def product_kernel(loads, after, high, low, half, ride, *refs):
    blocks, total, stack = refs[:NY], refs[NY], refs[NY + 1]
    both = ride[...] + gathered(blocks, stack)
    result = (half[...] + split_dot(high, low, stack[...])).reshape(total.shape)
    lane = lax.broadcasted_iota(jnp.int32, both.shape, 1)
    for k in range(total.shape[0]):
        total[k] = result[k]
        total[k, 0:TILE, :] = jnp.where(lane < loads, result[k, 0:TILE, :], both)


def correction_of(terms, squares, res_top, new_res_top, earlier):
    corners = terms.shape[1]
    total = tree_sum([terms[k] for k in range(terms.shape[0])])
    earlier[...] = total[0:TILE, :]
    new_res_top[...] = res_top[...]
    new_res_top[:corners, :] = res_top[:corners, :] - total[:, : res_top.shape[1]]
    top = new_res_top[...]
    return top, squares[...] + jnp.sum(top * top, axis=0, keepdims=True)


def last_kernel(terms, squares, res_top, new_res_top, earlier, told):
    _, norm = correction_of(terms, squares, res_top, new_res_top, earlier)
    padded = jnp.concatenate([norm, jnp.zeros((1, told.shape[2] - norm.shape[1]), F32)], axis=1)
    told[...] = jnp.broadcast_to(padded[None], told.shape)


def correct_kernel(steps, counts, terms, squares, res_top, dir_top, flex, flex_base, *outs):
    new_res_top, earlier, extra, new_dir_top, flexed = outs[:5]
    top, norm = correction_of(terms, squares, res_top, new_res_top, earlier)
    new_dir = steps[0] * dir_top[...] + steps[1] * top
    new_dir_top[...] = new_dir
    flexed[...] = flex_base[...] + dot(flex[:, :TOP], new_dir.astype(BF16))
    send_sides(counts, flexed, *outs[5:])
    loads, width = norm.shape[1], extra.shape[1]
    spare = width - loads
    padded = jnp.concatenate([norm, jnp.zeros((1, spare), F32)], axis=1)
    padded = jnp.broadcast_to(padded, (TILE, width))
    line = lax.broadcasted_iota(jnp.int32, padded.shape, 0)
    ride = jnp.zeros_like(padded)
    for n in range(-(-loads // spare)):
        ride = jnp.where(line == n, pltpu.roll(padded, (loads - n * spare) % width, 1), ride)
    extra[...] = jnp.zeros_like(extra)
    extra[0:TILE, :] = ride


def rider_values(earlier, loads):
    spare = earlier.shape[1] - loads
    lines = -(-loads // spare)
    return earlier[:lines, loads:].reshape(-1)[:loads]


def local(right_side, flex, stiff, coarse_inv, corner_map, side_rows):
    right = right_side[0, 0]
    flex_block = flex[0, 0]
    stiff_block = stiff[0, 0]
    order = flex_block.shape[0]
    side = order // SIDES
    loads = right.shape[0]
    width = -(-loads // LANES) * LANES
    corners = corner_map.shape[2]
    rows_held, cols_held = coarse_inv.shape
    half = N_GY * corners
    inv_t = coarse_inv.T
    inv_blocks = [inv_t]
    for k in range(1, NY):
        inv_blocks.append(turned(inv_t, "y", NY, k))

    ids_line = jnp.pad(corner_map[0, 0].astype(F32), (0, LANES - corners))[None]
    own_ids = jnp.broadcast_to(ids_line[None], (N_GY, 1, LANES))
    own_ids = to_all(own_ids, GY).reshape(N_GY, LANES)

    sides = [shape(side + side // 2, LANES)] * SIDES
    flexed, extra, counts, *sends = call(
        first_kernel, [shape(order, loads), shape(corners, width), shape(TILE, LANES)] + sides
    )(own_ids, ids_line, side_rows[0].astype(F32), right, flex_block)

    other_ids = turned(own_ids, "c", NC, 1)
    own_rows, other_rows = call(
        rows_kernel, [shape(cols_held, half)] * 2, scratch=[pltpu.VMEM((2 * half, rows_held), BF16)]
    )(own_ids, other_ids, *inv_blocks)
    own_rows = own_rows + turned(other_rows, "c", NC, 1)

    row_parts = [own_rows]
    for k in range(1, NZ):
        row_parts.append(turned(own_rows, "z", NZ, k))

    tops, lows = shape(TOP, loads), shape(order - TOP, loads)
    ride_shape = shape(TILE, width)
    corner_scratch = [pltpu.VMEM((NY * corners, width), F32)]
    rho_prev = 1.0 / cheb_sigma
    norms = []
    for iteration in range(ITERS):
        last = iteration + 1 == ITERS
        ins = []
        for k in range(SIDES):
            axes, count = (GY, N_GY) if k < 2 else (GX, N_GX)
            ins.append(swapped(sends[k], axes, count, k % 2))
        balanced, told = call(
            balance_kernel, [shape(order, loads, dtype=BF16), shape(NY * NX if iteration == 0 else 1, corners, width)]
        )(counts, flexed, *ins, stiff_block, extra)
        steps = None
        if not last:
            rho_next = 1.0 / (2.0 * cheb_sigma - rho_prev)
            steps = (rho_next * rho_prev, 2.0 * rho_next / cheb_half)
            rho_prev = rho_next
        if iteration == 0:
            values = to_all(told, ("y", "x"))
            kernel, state = first_bulk_kernel, (right,)
            order_after = (values,)
        else:
            values = [told]
            for k in range(1, NY):
                values.append(turned(told, "y", NY, k))
            kernel, state = bulk_kernel, (res_top, res_low, dir_top, dir_low, sol_top, sol_low)
            order_after = ()
        outs = call(
            functools.partial(kernel, steps),
            [tops, lows, tops, lows, shape(1, loads)] + ([] if last else [lows, shape(order, loads)]),
        )(*order_after, balanced, stiff_block, flex_block, *state)
        res_top, res_low, sol_top, sol_low, squares = outs[:5]
        if iteration == 0:
            dir_top = sol_top
            values_other = turned(values, "c", NC, 1)
            own_high, own_low, other_high, other_low, *shares = call(
                cols_kernel,
                [shape(half, half, dtype=BF16)] * 4 + [shape(half // NX * 2, half)] * NX,
                scratch=[pltpu.VMEM((2 * half, cols_held), BF16), pltpu.VMEM((2 * half, half), F32)],
            )(values, values_other, *row_parts)
            (partial,) = call(first_half_kernel, [shape(half, width)])(own_high, own_low, values)
            (partial,) = call(first_product_kernel, [shape(N_GY, corners, width)])(
                squares, other_high, other_low, values_other, partial
            )
            for k in range(1, NX):
                shares[k] = turned(shares[k], "x", NX, k)
            block = call(block_kernel, [shape(half, NY * corners, dtype=BF16)] * 4)(*shares)
        else:
            others = []
            for k in range(NY):
                others.append(turned(values[k], "c", NC, 1))
            partial, ride = call(
                half_product_kernel, [shape(half, width), ride_shape], scratch=corner_scratch
            )(*block[:2], *values)
            (partial,) = call(
                functools.partial(product_kernel, loads), [shape(N_GY, corners, width)], scratch=corner_scratch
            )(squares, *block[2:], partial, ride, *others)
        terms = to_all(partial, GY)
        if last:
            res_top, earlier, told = call(
                last_kernel, [tops, ride_shape, shape(N_GX * N_GY, 1, width)]
            )(terms, squares, res_top)
        else:
            dir_low, flex_base = outs[5:]
            res_top, earlier, extra, dir_top, flexed, *sends = call(
                functools.partial(correct_kernel, steps),
                [tops, ride_shape, shape(corners, width), tops, shape(order, loads)] + sides,
            )(counts, terms, squares, res_top, dir_top, flex_block, flex_base)
        if iteration > 0:
            norms.append(rider_values(earlier, loads))
    norms.append(to_all(told, ALL).sum(axis=0)[0, :loads])
    resid_norm = jnp.sqrt(jnp.stack(norms) / (N_GX * N_GY * order))
    solution = jnp.concatenate([sol_top, sol_low]).T
    residual = jnp.concatenate([res_top, res_low]).T
    return (solution[None, None], residual[None, None], resid_norm)


def solution(mesh):
    torus = Mesh(mesh.devices.reshape(NY, NC, NX, NZ), ALL)
    return jax.shard_map(
        local,
        mesh=torus,
        in_specs=(
            P(GX, GY, None, None),
            P(GX, GY, None, None),
            P(GX, GY, None, None),
            P(GX, GY),
            P(GX, GY, None),
            P(GX, GY, None),
        ),
        out_specs=(P(GX, GY, None, None), P(GX, GY, None, None), P()),
        check_vma=False,
    )
```

```python
import functools

import jax
import jax.numpy as jnp
from jax import lax
from jax.experimental import pallas as pl
from jax.experimental.pallas import tpu as pltpu
from jax.sharding import Mesh
from jax.sharding import PartitionSpec as P

ITERS = 3
GX = ("y", "c")
GY = ("x", "z")
ALL = ("y", "c", "x", "z")
NY, NC, NX, NZ = 4, 2, 4, 4
N_GX, N_GY = NY * NC, NX * NZ
SIDES = 4
TOP = 128
LANES = 128
TILE = 8
VMEM_BYTES = 16 * 2**20

cheb_center = 1.15
cheb_half = 0.85
cheb_sigma = cheb_center / cheb_half
F32 = jnp.float32
BF16 = jnp.bfloat16


def turned(array, axes, count, by):
    return lax.ppermute(array, axes, [(i, (i + by) % count) for i in range(count)])


def swapped(array, axes, count, shift):
    pairs = [(i, (((i + shift) ^ 1) - shift) % count) for i in range(count)]
    return lax.ppermute(array, axes, pairs)


def to_all(copies, axes):
    return lax.all_to_all(copies, axes, split_axis=0, concat_axis=0, tiled=True)


def vm():
    return pl.BlockSpec(memory_space=pltpu.VMEM)


def call(body, outs, scratch=()):
    def run(*operands):
        return pl.pallas_call(
            body,
            out_shape=outs,
            in_specs=[vm() for _ in operands],
            out_specs=[vm() for _ in outs],
            scratch_shapes=scratch,
            compiler_params=pltpu.CompilerParams(vmem_limit_bytes=VMEM_BYTES),
        )(*[pltpu.with_memory_space_constraint(o, pltpu.VMEM) for o in operands])

    return run


def shape(*dims, dtype=F32):
    return pltpu.VMEM(dims, dtype)


def dot(a, b, contract=((1,), (0,))):
    return lax.dot_general(a, b, (contract, ((), ())), preferred_element_type=F32)


def split(a):
    high = a.astype(BF16)
    return high, (a - high.astype(F32)).astype(BF16)


def mark(pick, columns, held):
    corners = columns[0].shape[0]
    at = lax.broadcasted_iota(jnp.int32, (2 * corners, held), 1).astype(F32)
    for n in range(0, len(columns), 2):
        ids = jnp.concatenate(columns[n : n + 2], axis=0)
        pick[n * corners : (n + 2) * corners, :] = jnp.where(at == ids, 1.0, 0.0).astype(BF16)


def rows_kernel(ids_own, ids_other, *refs):
    blocks, own, other, pick = refs[:-3], refs[-3], refs[-2], refs[-1]
    my_y, my_c = lax.axis_index("y"), lax.axis_index("c")
    held = blocks[0].shape[1]
    half = own.shape[1]
    corners = half // N_GY
    lists = [ids[...].T[:corners] for ids in (ids_own, ids_other)]
    total = 0.0
    for k, block in enumerate(blocks):
        base = ((((my_y + NY - k) % NY) * NC + my_c) * held).astype(F32)
        shifted = [ids - base for ids in lists]
        mark(pick, [ids[:, n : n + 1] for ids in shifted for n in range(N_GY)], held)
        for part in split(block[...]):
            total = total + dot(part, pick[...], ((1,), (1,)))
    own[...] = total[:, :half]
    other[...] = total[:, half:]


def cols_kernel(own, other, *refs):
    blocks, outs, sends, pick, total = refs[:NZ], refs[NZ : NZ + 4], refs[NZ + 4 : -2], refs[-2], refs[-1]
    my_x, my_z = lax.axis_index("x"), lax.axis_index("z")
    held = blocks[0].shape[0]
    half = outs[0].shape[1]
    last = own.shape[2] - 1
    corners = own.shape[1]
    columns = [v[n, :, last:] for v in (own, other) for n in range(v.shape[0])]
    summed = 0.0
    for k, block in enumerate(blocks):
        base = ((my_x * NZ + (my_z + NZ - k) % NZ) * held).astype(F32)
        mark(pick, [ids - base for ids in columns], held)
        for part in split(block[...]):
            summed = summed + dot(pick[...], part)
    total[...] = summed
    for n in range(2):
        outs[2 * n][...], outs[2 * n + 1][...] = split(summed[n * half : (n + 1) * half].T)
    for k, send in enumerate(sends):
        for n in range(NC * NY):
            start = pl.multiple_of((n * NX + (my_x + k) % NX) * corners, TILE)
            send[n * corners : (n + 1) * corners, :] = total[pl.ds(start, corners), :]


def block_kernel(*refs):
    parts, outs = refs[:NX], refs[NX:]
    block = ((parts[0][...] + parts[1][...]) + (parts[2][...] + parts[3][...])).T
    half = block.shape[1] // 2
    for n in range(2):
        outs[2 * n][...], outs[2 * n + 1][...] = split(block[:, n * half : (n + 1) * half])


def pack(out, main, rest, count):
    side, wide = main.shape[0], rest.shape[1]
    half = side // 2
    out[0:side, :] = main
    out[side : side + half, 0:wide] = rest[:half]
    out[side : side + half, wide : 2 * wide] = rest[half:]
    out[side : side + half, 2 * wide :] = jnp.broadcast_to(count[:, 2 * wide :], (half, LANES - 2 * wide))


def sent_sides():
    odd_b, odd_a = lax.axis_index("z") % 2, lax.axis_index("c")
    return (1 - odd_b, odd_b, 3 - odd_a, 2 + odd_a)


def first_kernel(after, ids, live, right, flex, flexed, extra, counts, *sends):
    direction = (right[...] / cheb_center).astype(BF16)
    flexed[...] = dot(flex[...], direction, ((1,), (1,)))
    counts[0:1, :] = jnp.broadcast_to(live[0:1, 0:1], (1, LANES))
    counts[1:2, :] = jnp.broadcast_to(live[0:1, 1:2], (1, LANES))
    send_sides(counts, flexed, *sends)
    column = jnp.broadcast_to(ids[...], (LANES, LANES)).T
    extra[...] = jnp.zeros_like(extra)
    extra[:, extra.shape[1] - LANES :] = column[: extra.shape[0]]


def send_sides(counts, flexed, *sends):
    side = flexed.shape[0] // SIDES
    for k, wanted in enumerate(sent_sides()):
        rows = pl.ds(pl.multiple_of(wanted * side, 32), side)
        pack(sends[k], flexed[rows, 0:LANES], flexed[rows, LANES:], counts[k // 2 : k // 2 + 1, :])


def balance_kernel(counts, flexed, in_a, in_b, in_c, in_y, stiff, extra, balanced, told):
    side = flexed.shape[0] // SIDES
    loads = flexed.shape[1]
    wide = loads - LANES
    half = side // 2
    my_y, my_c, my_x, my_z = (lax.axis_index(a) for a in ALL)
    row = my_y * NC + my_c
    col = my_x * NZ + my_z
    odd_b, odd_a = my_z % 2 == 1, my_c == 1
    spot = (slice(side, side + 1), slice(2 * wide, 2 * wide + 1))
    count_west = jnp.where(odd_b, in_a[spot], in_b[spot])
    count_north = jnp.where(odd_a, in_c[spot], in_y[spot])
    count_east = counts[0:1, 0:1]
    count_south = counts[1:2, 0:1]

    for rows, lanes, there in (
        ((0, side), (0, LANES), ((0, side), (0, LANES))),
        ((0, half), (LANES, loads), ((side, side + half), (0, wide))),
        ((half, side), (LANES, loads), ((side, side + half), (wide, 2 * wide))),
    ):
        size = (rows[1] - rows[0], lanes[1] - lanes[0])
        at = (lax.broadcasted_iota(jnp.int32, size, 0) + rows[0]).astype(F32)
        a, b, c, y = (m[there[0][0] : there[0][1], there[1][0] : there[1][1]] for m in (in_a, in_b, in_c, in_y))
        west, east, north, south = (
            flexed[k * side + rows[0] : k * side + rows[1], lanes[0] : lanes[1]] for k in range(SIDES)
        )

        def half_jump(count, inside, ahead, behind):
            return jnp.where(jnp.logical_and(at < count, inside), 0.5 * (ahead - behind), 0.0)

        results = (
            west + half_jump(count_west, col > 0, jnp.where(odd_b, a, b), west),
            east - half_jump(count_east, col < N_GY - 1, east, jnp.where(odd_b, b, a)),
            north + half_jump(count_north, row > 0, jnp.where(odd_a, c, y), north),
            south - half_jump(count_south, row < N_GX - 1, south, jnp.where(odd_a, y, c)),
        )
        for k, result in enumerate(results):
            balanced[k * side + rows[0] : k * side + rows[1], lanes[0] : lanes[1]] = result.astype(BF16)
    corners = told.shape[1]
    told[0] = extra[...]
    told[0, :, 0:loads] = dot(stiff[0:32, :], balanced[...])[:corners]
    for k in range(1, told.shape[0]):
        told[k] = told[0]


def step_on(steps, flex, dir_low, low, new_dir_low, flex_base):
    new_dir = steps[0] * dir_low + steps[1] * low
    new_dir_low[...] = new_dir
    flex_base[...] = dot(flex[:, TOP:], new_dir.astype(BF16))


def first_bulk_kernel(steps, after, balanced, stiff, flex, right, *outs):
    right = right[...].T
    res_top, res_low, sol_top, sol_low, squares = outs[:5]
    stiffed = dot(stiff[...], balanced[...])
    direction = right / cheb_center
    low = right[TOP:, :] - stiffed[TOP:]
    res_top[...] = right[:TOP, :] - stiffed[:TOP]
    res_low[...] = low
    sol_top[...] = direction[:TOP]
    sol_low[...] = direction[TOP:]
    squares[...] = jnp.sum(low * low, axis=0, keepdims=True)
    step_on(steps, flex, direction[TOP:], low, *outs[5:])


def bulk_kernel(steps, balanced, stiff, flex, res_top, res_low, dir_top, dir_low, sol_top, sol_low, *outs):
    new_res_top, new_res_low, new_sol_top, new_sol_low, squares = outs[:5]
    stiffed = dot(stiff[...], balanced[...])
    low = res_low[...] - stiffed[TOP:]
    new_res_top[...] = res_top[...] - stiffed[:TOP]
    new_res_low[...] = low
    new_sol_top[...] = sol_top[...] + dir_top[...]
    new_sol_low[...] = sol_low[...] + dir_low[...]
    squares[...] = jnp.sum(low * low, axis=0, keepdims=True)
    if steps is not None:
        step_on(steps, flex, dir_low[...], low, *outs[5:])


def split_dot(high, low, values):
    values_high, values_low = split(values)
    return dot(high[...], values_high) + (dot(high[...], values_low) + dot(low[...], values_high))


def first_half_kernel(high, low, values, total):
    total[...] = split_dot(high, low, values[...].reshape(-1, values.shape[2]))


def dealt(total, outs):
    my_x, my_z = lax.axis_index("x"), lax.axis_index("z")
    for k, out in enumerate(outs):
        for j in range(NX):
            out[j] = total[((my_x + j) % NX) * NZ + (my_z + k) % NZ]


def first_product_kernel(high, low, values, half, *refs):
    outs, total = refs[:-1], refs[-1]
    more = split_dot(high, low, values[...].reshape(-1, values.shape[2]))
    total[...] = (half[...] + more).reshape(total.shape)
    dealt(total, outs)


def ring_sum(parts):
    return (parts[0] + parts[2]) + (parts[1] + parts[3])


def sum_kernel(*refs):
    parts, outs = refs[:NZ], refs[NZ:]
    for j, out in enumerate(outs):
        out[...] = ring_sum([p[j] for p in parts])


def gathered(blocks, stack):
    my_y = lax.axis_index("y")
    corners = blocks[0].shape[1]
    for k, block in enumerate(blocks):
        at = pl.multiple_of(((my_y + NY - k) % NY) * corners, TILE)
        stack[pl.ds(at, corners), :] = block[0]
    return ring_sum([block[0, 0:TILE, :] for block in blocks])


def half_product_kernel(high, low, *refs):
    blocks, total, ride, stack = refs[:NY], refs[NY], refs[NY + 1], refs[NY + 2]
    ride[...] = gathered(blocks, stack)
    total[...] = split_dot(high, low, stack[...])


def product_kernel(loads, high, low, half, ride, *refs):
    blocks, outs, stack, total = refs[:NY], refs[NY:-2], refs[-2], refs[-1]
    both = ride[...] + gathered(blocks, stack)
    result = (half[...] + split_dot(high, low, stack[...])).reshape(total.shape)
    lane = lax.broadcasted_iota(jnp.int32, both.shape, 1)
    for k in range(total.shape[0]):
        total[k] = result[k]
        total[k, 0:TILE, :] = jnp.where(lane < loads, result[k, 0:TILE, :], both)
    dealt(total, outs)


def correction_of(squares, res_top, terms, new_res_top, earlier):
    corners = terms[0].shape[0]
    total = ring_sum([t[...] for t in terms])
    earlier[...] = total[0:TILE, :]
    new_res_top[...] = res_top[...]
    new_res_top[:corners, :] = res_top[:corners, :] - total[:, : res_top.shape[1]]
    top = new_res_top[...]
    return top, squares[...] + jnp.sum(top * top, axis=0, keepdims=True)


def last_kernel(squares, res_top, *refs):
    terms, (new_res_top, earlier, told) = refs[:NX], refs[NX:]
    _, norm = correction_of(squares, res_top, terms, new_res_top, earlier)
    padded = jnp.concatenate([norm, jnp.zeros((1, told.shape[2] - norm.shape[1]), F32)], axis=1)
    told[...] = jnp.broadcast_to(padded[None], told.shape)


def correct_kernel(steps, squares, res_top, counts, dir_top, flex, flex_base, *refs):
    terms, outs = refs[:NX], refs[NX:]
    new_res_top, earlier, extra, new_dir_top, flexed = outs[:5]
    top, norm = correction_of(squares, res_top, terms, new_res_top, earlier)
    new_dir = steps[0] * dir_top[...] + steps[1] * top
    new_dir_top[...] = new_dir
    flexed[...] = flex_base[...] + dot(flex[:, :TOP], new_dir.astype(BF16))
    send_sides(counts, flexed, *outs[5:])
    loads, width = norm.shape[1], extra.shape[1]
    spare = width - loads
    padded = jnp.concatenate([norm, jnp.zeros((1, spare), F32)], axis=1)
    padded = jnp.broadcast_to(padded, (TILE, width))
    line = lax.broadcasted_iota(jnp.int32, padded.shape, 0)
    ride = jnp.zeros_like(padded)
    for n in range(-(-loads // spare)):
        ride = jnp.where(line == n, pltpu.roll(padded, (loads - n * spare) % width, 1), ride)
    extra[...] = jnp.zeros_like(extra)
    extra[0:TILE, :] = ride


def rider_values(earlier, loads):
    spare = earlier.shape[1] - loads
    lines = -(-loads // spare)
    return earlier[:lines, loads:].reshape(-1)[:loads]


def local(right_side, flex, stiff, coarse_inv, corner_map, side_rows):
    right = right_side[0, 0]
    flex_block = flex[0, 0]
    stiff_block = stiff[0, 0]
    order = flex_block.shape[0]
    side = order // SIDES
    loads = right.shape[0]
    width = -(-loads // LANES) * LANES
    corners = corner_map.shape[2]
    rows_held, cols_held = coarse_inv.shape
    half = N_GY * corners
    inv_t = coarse_inv.T
    inv_blocks = [inv_t]
    for k in range(1, NY):
        inv_blocks.append(turned(inv_t, "y", NY, k))

    ids_line = jnp.pad(corner_map[0, 0].astype(F32), (0, LANES - corners))[None]
    own_ids = jnp.broadcast_to(ids_line[None], (N_GY, 1, LANES))
    own_ids = to_all(own_ids, GY).reshape(N_GY, LANES)

    sides = [shape(side + side // 2, LANES)] * SIDES
    flexed, extra, counts, *sends = call(
        first_kernel, [shape(order, loads), shape(corners, width), shape(TILE, LANES)] + sides
    )(own_ids, ids_line, side_rows[0].astype(F32), right, flex_block)

    other_ids = turned(own_ids, "c", NC, 1)
    own_rows, other_rows = call(
        rows_kernel, [shape(cols_held, half)] * 2, scratch=[pltpu.VMEM((2 * half, rows_held), BF16)]
    )(own_ids, other_ids, *inv_blocks)
    own_rows = own_rows + turned(other_rows, "c", NC, 1)

    row_parts = [own_rows]
    for k in range(1, NZ):
        row_parts.append(turned(own_rows, "z", NZ, k))

    tops, lows = shape(TOP, loads), shape(order - TOP, loads)
    ride_shape = shape(TILE, width)
    corner_scratch = [pltpu.VMEM((NY * corners, width), F32)]
    dealt_shapes = [shape(NX, corners, width)] * NZ
    dealt_scratch = pltpu.VMEM((N_GY, corners, width), F32)
    rho_prev = 1.0 / cheb_sigma
    norms = []
    for iteration in range(ITERS):
        last = iteration + 1 == ITERS
        ins = []
        for k in range(SIDES):
            axes, count = (GY, N_GY) if k < 2 else (GX, N_GX)
            ins.append(swapped(sends[k], axes, count, k % 2))
        balanced, told = call(
            balance_kernel, [shape(order, loads, dtype=BF16), shape(NY * NX if iteration == 0 else 1, corners, width)]
        )(counts, flexed, *ins, stiff_block, extra)
        steps = None
        if not last:
            rho_next = 1.0 / (2.0 * cheb_sigma - rho_prev)
            steps = (rho_next * rho_prev, 2.0 * rho_next / cheb_half)
            rho_prev = rho_next
        if iteration == 0:
            values = to_all(told, ("y", "x"))
            kernel, state = first_bulk_kernel, (right,)
            order_after = (values,)
        else:
            values = [told]
            for k in range(1, NY):
                values.append(turned(told, "y", NY, k))
            kernel, state = bulk_kernel, (res_top, res_low, dir_top, dir_low, sol_top, sol_low)
            order_after = ()
        outs = call(
            functools.partial(kernel, steps),
            [tops, lows, tops, lows, shape(1, loads)] + ([] if last else [lows, shape(order, loads)]),
        )(*order_after, balanced, stiff_block, flex_block, *state)
        res_top, res_low, sol_top, sol_low, squares = outs[:5]
        if iteration == 0:
            dir_top = sol_top
            values_other = turned(values, "c", NC, 1)
            own_high, own_low, other_high, other_low, *shares = call(
                cols_kernel,
                [shape(half, half, dtype=BF16)] * 4 + [shape(half // NX * 2, half)] * NX,
                scratch=[pltpu.VMEM((2 * half, cols_held), BF16), pltpu.VMEM((2 * half, half), F32)],
            )(values, values_other, *row_parts)
            (partial,) = call(first_half_kernel, [shape(half, width)])(own_high, own_low, values)
            shared = call(first_product_kernel, dealt_shapes, scratch=[dealt_scratch])(
                other_high, other_low, values_other, partial
            )
            for k in range(1, NX):
                shares[k] = turned(shares[k], "x", NX, k)
            block = call(block_kernel, [shape(half, NY * corners, dtype=BF16)] * 4)(*shares)
        else:
            others = []
            for k in range(NY):
                others.append(turned(values[k], "c", NC, 1))
            partial, ride = call(
                half_product_kernel, [shape(half, width), ride_shape], scratch=corner_scratch
            )(*block[:2], *values)
            shared = call(
                functools.partial(product_kernel, loads), dealt_shapes, scratch=corner_scratch + [dealt_scratch]
            )(*block[2:], partial, ride, *others)
        shared = list(shared)
        for k in range(1, NZ):
            shared[k] = turned(shared[k], "z", NZ, k)
        terms = list(call(sum_kernel, [shape(corners, width)] * NX)(*shared))
        for k in range(1, NX):
            terms[k] = turned(terms[k], "x", NX, k)
        if last:
            res_top, earlier, told = call(
                last_kernel, [tops, ride_shape, shape(N_GX * N_GY, 1, width)]
            )(squares, res_top, *terms)
        else:
            dir_low, flex_base = outs[5:]
            res_top, earlier, extra, dir_top, flexed, *sends = call(
                functools.partial(correct_kernel, steps),
                [tops, ride_shape, shape(corners, width), tops, shape(order, loads)] + sides,
            )(squares, res_top, counts, dir_top, flex_block, flex_base, *terms)
        if iteration > 0:
            norms.append(rider_values(earlier, loads))
    norms.append(to_all(told, ALL).sum(axis=0)[0, :loads])
    resid_norm = jnp.sqrt(jnp.stack(norms) / (N_GX * N_GY * order))
    solution = jnp.concatenate([sol_top, sol_low]).T
    residual = jnp.concatenate([res_top, res_low]).T
    return (solution[None, None], residual[None, None], resid_norm)


def solution(mesh):
    torus = Mesh(mesh.devices.reshape(NY, NC, NX, NZ), ALL)
    return jax.shard_map(
        local,
        mesh=torus,
        in_specs=(
            P(GX, GY, None, None),
            P(GX, GY, None, None),
            P(GX, GY, None, None),
            P(GX, GY),
            P(GX, GY, None),
            P(GX, GY, None),
        ),
        out_specs=(P(GX, GY, None, None), P(GX, GY, None, None), P()),
        check_vma=False,
    )
```

```python
import functools

import jax
import jax.numpy as jnp
from jax import lax
from jax.experimental import pallas as pl
from jax.experimental.pallas import tpu as pltpu
from jax.sharding import Mesh
from jax.sharding import PartitionSpec as P

ITERS = 3
GX = ("y", "c")
GY = ("x", "z")
ALL = ("y", "c", "x", "z")
NY, NC, NX, NZ = 4, 2, 4, 4
N_GX, N_GY = NY * NC, NX * NZ
SIDES = 4
TOP = 128
LANES = 128
TILE = 8
VMEM_BYTES = 16 * 2**20

cheb_center = 1.15
cheb_half = 0.85
cheb_sigma = cheb_center / cheb_half
F32 = jnp.float32
BF16 = jnp.bfloat16


def turned(array, axes, count, by):
    return lax.ppermute(array, axes, [(i, (i + by) % count) for i in range(count)])


def swapped(array, axes, count, shift):
    pairs = [(i, (((i + shift) ^ 1) - shift) % count) for i in range(count)]
    return lax.ppermute(array, axes, pairs)


def to_all(copies, axes):
    return lax.all_to_all(copies, axes, split_axis=0, concat_axis=0, tiled=True)


def vm():
    return pl.BlockSpec(memory_space=pltpu.VMEM)


def call(body, outs, scratch=(), unread=()):
    def run(*operands):
        return pl.pallas_call(
            body,
            out_shape=outs,
            in_specs=[vm() for _ in operands] + [pl.BlockSpec(memory_space=pltpu.HBM) for _ in unread],
            out_specs=[vm() for _ in outs],
            scratch_shapes=scratch,
            compiler_params=pltpu.CompilerParams(vmem_limit_bytes=VMEM_BYTES),
        )(
            *[pltpu.with_memory_space_constraint(o, pltpu.VMEM) for o in operands],
            *[pltpu.with_memory_space_constraint(o, pltpu.HBM) for o in unread],
        )

    return run


def shape(*dims, dtype=F32):
    return pltpu.VMEM(dims, dtype)


def dot(a, b, contract=((1,), (0,))):
    return lax.dot_general(a, b, (contract, ((), ())), preferred_element_type=F32)


def split(a):
    high = a.astype(BF16)
    return high, (a - high.astype(F32)).astype(BF16)


def mark(pick, columns, held):
    corners = columns[0].shape[0]
    at = lax.broadcasted_iota(jnp.int32, (2 * corners, held), 1).astype(F32)
    for n in range(0, len(columns), 2):
        ids = jnp.concatenate(columns[n : n + 2], axis=0)
        pick[n * corners : (n + 2) * corners, :] = jnp.where(at == ids, 1.0, 0.0).astype(BF16)


def rows_kernel(ids_own, ids_other, *refs):
    blocks, own, other, pick = refs[:-3], refs[-3], refs[-2], refs[-1]
    my_y, my_c = lax.axis_index("y"), lax.axis_index("c")
    held = blocks[0].shape[1]
    half = own.shape[1]
    corners = half // N_GY
    lists = [ids[...].T[:corners] for ids in (ids_own, ids_other)]
    total = 0.0
    for k, block in enumerate(blocks):
        base = ((((my_y + NY - k) % NY) * NC + my_c) * held).astype(F32)
        shifted = [ids - base for ids in lists]
        mark(pick, [ids[:, n : n + 1] for ids in shifted for n in range(N_GY)], held)
        for part in split(block[...]):
            total = total + dot(part, pick[...], ((1,), (1,)))
    own[...] = total[:, :half]
    other[...] = total[:, half:]


def cols_kernel(own, other, *refs):
    blocks, outs, sends, pick, total = refs[:NZ], refs[NZ : NZ + 4], refs[NZ + 4 : -2], refs[-2], refs[-1]
    my_x, my_z = lax.axis_index("x"), lax.axis_index("z")
    held = blocks[0].shape[0]
    half = outs[0].shape[1]
    last = own.shape[2] - 1
    corners = own.shape[1]
    columns = [v[n, :, last:] for v in (own, other) for n in range(v.shape[0])]
    summed = 0.0
    for k, block in enumerate(blocks):
        base = ((my_x * NZ + (my_z + NZ - k) % NZ) * held).astype(F32)
        mark(pick, [ids - base for ids in columns], held)
        for part in split(block[...]):
            summed = summed + dot(pick[...], part)
    total[...] = summed
    for n in range(2):
        outs[2 * n][...], outs[2 * n + 1][...] = split(summed[n * half : (n + 1) * half].T)
    for k, send in enumerate(sends):
        for n in range(NC * NY):
            start = pl.multiple_of((n * NX + (my_x + k) % NX) * corners, TILE)
            send[n * corners : (n + 1) * corners, :] = total[pl.ds(start, corners), :]


def block_kernel(*refs):
    parts, outs = refs[:NX], refs[NX:]
    block = ((parts[0][...] + parts[1][...]) + (parts[2][...] + parts[3][...])).T
    half = block.shape[1] // 2
    for n in range(2):
        outs[2 * n][...], outs[2 * n + 1][...] = split(block[:, n * half : (n + 1) * half])


def pack(out, main, rest, count):
    side, wide = main.shape[0], rest.shape[1]
    half = side // 2
    out[0:side, :] = main
    out[side : side + half, 0:wide] = rest[:half]
    out[side : side + half, wide : 2 * wide] = rest[half:]
    out[side : side + half, 2 * wide :] = jnp.broadcast_to(count[:, 2 * wide :], (half, LANES - 2 * wide))


def sent_sides():
    odd_b, odd_a = lax.axis_index("z") % 2, lax.axis_index("c")
    return (1 - odd_b, odd_b, 3 - odd_a, 2 + odd_a)


def ids_kernel(ids, side_rows, right, flex, told, line, counts):
    line[...] = jnp.zeros_like(line)
    line[:, 0 : ids.shape[1]] = ids[...].astype(F32)
    told[...] = jnp.broadcast_to(line[...][None], told.shape)
    live = side_rows[...].astype(F32)
    which = lax.broadcasted_iota(jnp.int32, counts.shape, 0)
    counts[...] = jnp.where(which == 0, live[:, 0:1], live[:, 1:2])


def first_kernel(after, ids, counts, right, flex, flexed, extra, *sends):
    direction = (right[...] / cheb_center).astype(BF16)
    flexed[...] = dot(flex[...], direction, ((1,), (1,)))
    send_sides(counts, flexed, *sends)
    column = jnp.broadcast_to(ids[...], (LANES, LANES)).T
    extra[...] = jnp.zeros_like(extra)
    extra[:, extra.shape[1] - LANES :] = column[: extra.shape[0]]


def send_sides(counts, flexed, *sends):
    side = flexed.shape[0] // SIDES
    for k, wanted in enumerate(sent_sides()):
        rows = pl.ds(pl.multiple_of(wanted * side, 32), side)
        pack(sends[k], flexed[rows, 0:LANES], flexed[rows, LANES:], counts[k // 2 : k // 2 + 1, :])


def balance_kernel(counts, flexed, in_a, in_b, in_c, in_y, stiff, extra, balanced, told):
    side = flexed.shape[0] // SIDES
    loads = flexed.shape[1]
    wide = loads - LANES
    half = side // 2
    my_y, my_c, my_x, my_z = (lax.axis_index(a) for a in ALL)
    row = my_y * NC + my_c
    col = my_x * NZ + my_z
    odd_b, odd_a = my_z % 2 == 1, my_c == 1
    spot = (slice(side, side + 1), slice(2 * wide, 2 * wide + 1))
    count_west = jnp.where(odd_b, in_a[spot], in_b[spot])
    count_north = jnp.where(odd_a, in_c[spot], in_y[spot])
    count_east = counts[0:1, 0:1]
    count_south = counts[1:2, 0:1]

    for rows, lanes, there in (
        ((0, side), (0, LANES), ((0, side), (0, LANES))),
        ((0, half), (LANES, loads), ((side, side + half), (0, wide))),
        ((half, side), (LANES, loads), ((side, side + half), (wide, 2 * wide))),
    ):
        size = (rows[1] - rows[0], lanes[1] - lanes[0])
        at = (lax.broadcasted_iota(jnp.int32, size, 0) + rows[0]).astype(F32)
        a, b, c, y = (m[there[0][0] : there[0][1], there[1][0] : there[1][1]] for m in (in_a, in_b, in_c, in_y))
        west, east, north, south = (
            flexed[k * side + rows[0] : k * side + rows[1], lanes[0] : lanes[1]] for k in range(SIDES)
        )

        def half_jump(count, inside, ahead, behind):
            return jnp.where(jnp.logical_and(at < count, inside), 0.5 * (ahead - behind), 0.0)

        results = (
            west + half_jump(count_west, col > 0, jnp.where(odd_b, a, b), west),
            east - half_jump(count_east, col < N_GY - 1, east, jnp.where(odd_b, b, a)),
            north + half_jump(count_north, row > 0, jnp.where(odd_a, c, y), north),
            south - half_jump(count_south, row < N_GX - 1, south, jnp.where(odd_a, y, c)),
        )
        for k, result in enumerate(results):
            balanced[k * side + rows[0] : k * side + rows[1], lanes[0] : lanes[1]] = result.astype(BF16)
    corners = told.shape[1]
    told[0] = extra[...]
    told[0, :, 0:loads] = dot(stiff[0:32, :], balanced[...])[:corners]
    for k in range(1, told.shape[0]):
        told[k] = told[0]


def step_on(steps, flex, dir_low, low, new_dir_low, flex_base, rounded):
    new_dir = steps[0] * dir_low + steps[1] * low
    new_dir_low[...] = new_dir
    rounded[0:TOP, :] = jnp.zeros((TOP, rounded.shape[1]), BF16)
    rounded[TOP:, :] = new_dir.astype(BF16)
    flex_base[...] = dot(flex[...], rounded[...])


def first_bulk_kernel(steps, after, balanced, stiff, flex, right, *outs):
    right = right[...].T
    res_top, res_low, sol_top, sol_low, squares = outs[:5]
    stiffed = dot(stiff[...], balanced[...])
    direction = right / cheb_center
    low = right[TOP:, :] - stiffed[TOP:]
    res_top[...] = right[:TOP, :] - stiffed[:TOP]
    res_low[...] = low
    sol_top[...] = direction[:TOP]
    sol_low[...] = direction[TOP:]
    squares[...] = jnp.sum(low * low, axis=0, keepdims=True)
    step_on(steps, flex, direction[TOP:], low, *outs[5:])


def bulk_kernel(steps, balanced, stiff, flex, res_top, res_low, dir_top, dir_low, sol_top, sol_low, *outs):
    new_res_top, new_res_low, new_sol_top, new_sol_low, squares = outs[:5]
    stiffed = dot(stiff[...], balanced[...])
    low = res_low[...] - stiffed[TOP:]
    new_res_top[...] = res_top[...] - stiffed[:TOP]
    new_res_low[...] = low
    new_sol_top[...] = sol_top[...] + dir_top[...]
    new_sol_low[...] = sol_low[...] + dir_low[...]
    squares[...] = jnp.sum(low * low, axis=0, keepdims=True)
    if steps is not None:
        step_on(steps, flex, dir_low[...], low, *outs[5:])


def split_dot(high, low, values):
    values_high, values_low = split(values)
    return dot(high[...], values_high) + (dot(high[...], values_low) + dot(low[...], values_high))


def tree_sum(parts):
    while len(parts) > 1:
        parts = [p + q for p, q in zip(parts[::2], parts[1::2])]
    return parts[0]


def first_half_kernel(high, low, values, total):
    total[...] = split_dot(high, low, values[...].reshape(-1, values.shape[2]))


def first_product_kernel(after, high, low, values, half, total):
    more = split_dot(high, low, values[...].reshape(-1, values.shape[2]))
    total[...] = (half[...] + more).reshape(total.shape)


def gathered(blocks, stack):
    my_y = lax.axis_index("y")
    corners = blocks[0].shape[1]
    for k, block in enumerate(blocks):
        at = pl.multiple_of(((my_y + NY - k) % NY) * corners, TILE)
        stack[pl.ds(at, corners), :] = block[0]
    b = [block[0, 0:TILE, :] for block in blocks]
    return (b[0] + b[2]) + (b[1] + b[3])


def half_product_kernel(high, low, *refs):
    blocks, total, ride, stack = refs[:NY], refs[NY], refs[NY + 1], refs[NY + 2]
    ride[...] = gathered(blocks, stack)
    total[...] = split_dot(high, low, stack[...])


def product_kernel(loads, after, high, low, half, ride, *refs):
    blocks, total, stack = refs[:NY], refs[NY], refs[NY + 1]
    both = ride[...] + gathered(blocks, stack)
    result = (half[...] + split_dot(high, low, stack[...])).reshape(total.shape)
    lane = lax.broadcasted_iota(jnp.int32, both.shape, 1)
    for k in range(total.shape[0]):
        total[k] = result[k]
        total[k, 0:TILE, :] = jnp.where(lane < loads, result[k, 0:TILE, :], both)


def correction_of(terms, squares, res_top, new_res_top, earlier):
    corners = terms.shape[1]
    total = tree_sum([terms[k] for k in range(terms.shape[0])])
    if earlier is not None:
        earlier[...] = total[0:TILE, :]
    new_res_top[...] = res_top[...]
    new_res_top[:corners, :] = res_top[:corners, :] - total[:, : res_top.shape[1]]
    top = new_res_top[...]
    return top, squares[...] + jnp.sum(top * top, axis=0, keepdims=True)


def last_kernel(terms, squares, res_top, new_res_top, earlier, told):
    _, norm = correction_of(terms, squares, res_top, new_res_top, earlier)
    padded = jnp.concatenate([norm, jnp.zeros((1, told.shape[2] - norm.shape[1]), F32)], axis=1)
    told[...] = jnp.broadcast_to(padded[None], told.shape)


def correct_kernel(steps, first, counts, terms, squares, res_top, dir_top, flex, flex_base, *outs):
    earlier, outs = (None, outs) if first else (outs[0], outs[1:])
    new_res_top, extra, new_dir_top, flexed = outs[:4]
    top, norm = correction_of(terms, squares, res_top, new_res_top, earlier)
    new_dir = steps[0] * dir_top[...] + steps[1] * top
    new_dir_top[...] = new_dir
    flexed[...] = flex_base[...] + dot(flex[:, :TOP], new_dir.astype(BF16))
    send_sides(counts, flexed, *outs[4:])
    loads, width = norm.shape[1], extra.shape[1]
    spare = width - loads
    padded = jnp.concatenate([norm, jnp.zeros((1, spare), F32)], axis=1)
    padded = jnp.broadcast_to(padded, (TILE, width))
    line = lax.broadcasted_iota(jnp.int32, padded.shape, 0)
    ride = jnp.zeros_like(padded)
    for n in range(-(-loads // spare)):
        ride = jnp.where(line == n, pltpu.roll(padded, (loads - n * spare) % width, 1), ride)
    extra[...] = jnp.zeros_like(extra)
    extra[0:TILE, :] = ride


def rider_values(earlier, loads):
    spare = earlier.shape[1] - loads
    lines = -(-loads // spare)
    return earlier[:lines, loads:].reshape(-1)[:loads]


def local(right_side, flex, stiff, coarse_inv, corner_map, side_rows):
    right = right_side[0, 0]
    flex_block = flex[0, 0]
    stiff_block = stiff[0, 0]
    order = flex_block.shape[0]
    side = order // SIDES
    loads = right.shape[0]
    width = -(-loads // LANES) * LANES
    corners = corner_map.shape[2]
    rows_held, cols_held = coarse_inv.shape
    half = N_GY * corners
    inv_t = coarse_inv.T
    inv_blocks = [inv_t]
    for k in range(1, NY):
        inv_blocks.append(turned(inv_t, "y", NY, k))

    own_ids, ids_line, counts = call(
        ids_kernel, [shape(N_GY, 1, LANES), shape(1, LANES), shape(TILE, LANES)], unread=(right, flex_block)
    )(corner_map[0], side_rows[0])
    own_ids = to_all(own_ids, GY).reshape(N_GY, LANES)

    sides = [shape(side + side // 2, LANES)] * SIDES
    flexed, extra, *sends = call(
        first_kernel, [shape(order, loads), shape(corners, width)] + sides
    )(own_ids, ids_line, counts, right, flex_block)

    other_ids = turned(own_ids, "c", NC, 1)
    own_rows, other_rows = call(
        rows_kernel, [shape(cols_held, half)] * 2, scratch=[pltpu.VMEM((2 * half, rows_held), BF16)]
    )(own_ids, other_ids, *inv_blocks)
    own_rows = own_rows + turned(other_rows, "c", NC, 1)

    row_parts = [own_rows]
    for k in range(1, NZ):
        row_parts.append(turned(own_rows, "z", NZ, k))

    tops, lows = shape(TOP, loads), shape(order - TOP, loads)
    ride_shape = shape(TILE, width)
    corner_scratch = [pltpu.VMEM((NY * corners, width), F32)]
    rho_prev = 1.0 / cheb_sigma
    norms = []
    for iteration in range(ITERS):
        last = iteration + 1 == ITERS
        ins = []
        for k in range(SIDES):
            axes, count = (GY, N_GY) if k < 2 else (GX, N_GX)
            ins.append(swapped(sends[k], axes, count, k % 2))
        balanced, told = call(
            balance_kernel, [shape(order, loads, dtype=BF16), shape(NY * NX if iteration == 0 else 1, corners, width)]
        )(counts, flexed, *ins, stiff_block, extra)
        steps = None
        if not last:
            rho_next = 1.0 / (2.0 * cheb_sigma - rho_prev)
            steps = (rho_next * rho_prev, 2.0 * rho_next / cheb_half)
            rho_prev = rho_next
        if iteration == 0:
            values = to_all(told, ("y", "x"))
            kernel, state = first_bulk_kernel, (right,)
            order_after = (values,)
        else:
            values = [told]
            for k in range(1, NY):
                values.append(turned(told, "y", NY, k))
            kernel, state = bulk_kernel, (res_top, res_low, dir_top, dir_low, sol_top, sol_low)
            order_after = ()
        outs = call(
            functools.partial(kernel, steps),
            [tops, lows, tops, lows, shape(1, loads)] + ([] if last else [lows, shape(order, loads)]),
            scratch=[] if last else [pltpu.VMEM((order, loads), BF16)],
        )(*order_after, balanced, stiff_block, flex_block, *state)
        res_top, res_low, sol_top, sol_low, squares = outs[:5]
        if iteration == 0:
            dir_top = sol_top
            values_other = turned(values, "c", NC, 1)
            own_high, own_low, other_high, other_low, *shares = call(
                cols_kernel,
                [shape(half, half, dtype=BF16)] * 4 + [shape(half // NX * 2, half)] * NX,
                scratch=[pltpu.VMEM((2 * half, cols_held), BF16), pltpu.VMEM((2 * half, half), F32)],
            )(values, values_other, *row_parts)
            (partial,) = call(first_half_kernel, [shape(half, width)])(own_high, own_low, values)
            (partial,) = call(first_product_kernel, [shape(N_GY, corners, width)])(
                squares, other_high, other_low, values_other, partial
            )
            for k in range(1, NX):
                shares[k] = turned(shares[k], "x", NX, k)
            block = call(block_kernel, [shape(half, NY * corners, dtype=BF16)] * 4)(*shares)
        else:
            others = []
            for k in range(NY):
                others.append(turned(values[k], "c", NC, 1))
            partial, ride = call(
                half_product_kernel, [shape(half, width), ride_shape], scratch=corner_scratch
            )(*block[:2], *values)
            (partial,) = call(
                functools.partial(product_kernel, loads), [shape(N_GY, corners, width)], scratch=corner_scratch
            )(squares, *block[2:], partial, ride, *others)
        terms = to_all(partial, GY)
        if last:
            res_top, earlier, told = call(
                last_kernel, [tops, ride_shape, shape(N_GX * N_GY, 1, width)]
            )(terms, squares, res_top)
        else:
            dir_low, flex_base = outs[5:]
            outs = call(
                functools.partial(correct_kernel, steps, iteration == 0),
                ([ride_shape] if iteration > 0 else [])
                + [tops, shape(corners, width), tops, shape(order, loads)]
                + sides,
            )(counts, terms, squares, res_top, dir_top, flex_block, flex_base)
            if iteration > 0:
                earlier, *outs = outs
            res_top, extra, dir_top, flexed, *sends = outs
        if iteration > 0:
            norms.append(rider_values(earlier, loads))
    norms.append(to_all(told, ALL).sum(axis=0)[0, :loads])
    resid_norm = jnp.sqrt(jnp.stack(norms) / (N_GX * N_GY * order))
    solution = jnp.concatenate([sol_top, sol_low]).T
    residual = jnp.concatenate([res_top, res_low]).T
    return (solution[None, None], residual[None, None], resid_norm)


def solution(mesh):
    torus = Mesh(mesh.devices.reshape(NY, NC, NX, NZ), ALL)
    return jax.shard_map(
        local,
        mesh=torus,
        in_specs=(
            P(GX, GY, None, None),
            P(GX, GY, None, None),
            P(GX, GY, None, None),
            P(GX, GY),
            P(GX, GY, None),
            P(GX, GY, None),
        ),
        out_specs=(P(GX, GY, None, None), P(GX, GY, None, None), P()),
        check_vma=False,
    )
```

```python
import functools

import jax
import jax.numpy as jnp
from jax import lax
from jax.experimental import pallas as pl
from jax.experimental.pallas import tpu as pltpu
from jax.sharding import Mesh
from jax.sharding import PartitionSpec as P

ITERS = 3
GX = ("y", "c")
GY = ("x", "z")
ALL = ("y", "c", "x", "z")
NY, NC, NX, NZ = 4, 2, 4, 4
N_GX, N_GY = NY * NC, NX * NZ
SIDES = 4
TOP = 128
LANES = 128
TILE = 8
VMEM_BYTES = 16 * 2**20

cheb_center = 1.15
cheb_half = 0.85
cheb_sigma = cheb_center / cheb_half
F32 = jnp.float32
BF16 = jnp.bfloat16


def turned(array, axes, count, by):
    return lax.ppermute(array, axes, [(i, (i + by) % count) for i in range(count)])


def swapped(array, axes, count, shift):
    pairs = [(i, (((i + shift) ^ 1) - shift) % count) for i in range(count)]
    return lax.ppermute(array, axes, pairs)


def to_all(copies, axes):
    return lax.all_to_all(copies, axes, split_axis=0, concat_axis=0, tiled=True)


def vm():
    return pl.BlockSpec(memory_space=pltpu.VMEM)


def call(body, outs, scratch=(), unread=()):
    def run(*operands):
        return pl.pallas_call(
            body,
            out_shape=outs,
            in_specs=[vm() for _ in operands] + [pl.BlockSpec(memory_space=pltpu.HBM) for _ in unread],
            out_specs=[vm() for _ in outs],
            scratch_shapes=scratch,
            compiler_params=pltpu.CompilerParams(vmem_limit_bytes=VMEM_BYTES),
        )(
            *[pltpu.with_memory_space_constraint(o, pltpu.VMEM) for o in operands],
            *[pltpu.with_memory_space_constraint(o, pltpu.HBM) for o in unread],
        )

    return run


def shape(*dims, dtype=F32):
    return pltpu.VMEM(dims, dtype)


def dot(a, b, contract=((1,), (0,))):
    return lax.dot_general(a, b, (contract, ((), ())), preferred_element_type=F32)


def split(a):
    high = a.astype(BF16)
    return high, (a - high.astype(F32)).astype(BF16)


def mark(pick, columns, held):
    corners = columns[0].shape[0]
    at = lax.broadcasted_iota(jnp.int32, (2 * corners, held), 1).astype(F32)
    for n in range(0, len(columns), 2):
        ids = jnp.concatenate(columns[n : n + 2], axis=0)
        pick[n * corners : (n + 2) * corners, :] = jnp.where(at == ids, 1.0, 0.0).astype(BF16)


def rows_kernel(ids_own, ids_other, *refs):
    blocks, own, other, pick = refs[:-3], refs[-3], refs[-2], refs[-1]
    my_y, my_c = lax.axis_index("y"), lax.axis_index("c")
    held = blocks[0].shape[1]
    half = own.shape[1]
    corners = half // N_GY
    lists = [ids[...].T[:corners] for ids in (ids_own, ids_other)]
    total = 0.0
    for k, block in enumerate(blocks):
        base = ((((my_y + NY - k) % NY) * NC + my_c) * held).astype(F32)
        shifted = [ids - base for ids in lists]
        mark(pick, [ids[:, n : n + 1] for ids in shifted for n in range(N_GY)], held)
        for part in split(block[...]):
            total = total + dot(part, pick[...], ((1,), (1,)))
    own[...] = total[:, :half]
    other[...] = total[:, half:]


def cols_kernel(own, other, *refs):
    blocks, outs, sends, pick, total = refs[:NZ], refs[NZ : NZ + 4], refs[NZ + 4 : -2], refs[-2], refs[-1]
    my_x, my_z = lax.axis_index("x"), lax.axis_index("z")
    held = blocks[0].shape[0]
    half = outs[0].shape[1]
    last = own.shape[2] - 1
    corners = own.shape[1]
    columns = [v[n, :, last:] for v in (own, other) for n in range(v.shape[0])]
    summed = 0.0
    for k, block in enumerate(blocks):
        base = ((my_x * NZ + (my_z + NZ - k) % NZ) * held).astype(F32)
        mark(pick, [ids - base for ids in columns], held)
        for part in split(block[...]):
            summed = summed + dot(pick[...], part)
    total[...] = summed
    for n in range(2):
        outs[2 * n][...], outs[2 * n + 1][...] = split(summed[n * half : (n + 1) * half].T)
    for k, send in enumerate(sends):
        for n in range(NC * NY):
            start = pl.multiple_of((n * NX + (my_x + k) % NX) * corners, TILE)
            send[n * corners : (n + 1) * corners, :] = total[pl.ds(start, corners), :]


def block_kernel(*refs):
    parts, outs = refs[:NX], refs[NX:]
    block = ((parts[0][...] + parts[1][...]) + (parts[2][...] + parts[3][...])).T
    half = block.shape[1] // 2
    for n in range(2):
        outs[2 * n][...], outs[2 * n + 1][...] = split(block[:, n * half : (n + 1) * half])


def pack(out, main, rest, count):
    side, wide = main.shape[0], rest.shape[1]
    half = side // 2
    out[0:side, :] = main
    out[side : side + half, 0:wide] = rest[:half]
    out[side : side + half, wide : 2 * wide] = rest[half:]
    out[side : side + half, 2 * wide :] = jnp.broadcast_to(count[:, 2 * wide :], (half, LANES - 2 * wide))


def sent_sides():
    odd_b, odd_a = lax.axis_index("z") % 2, lax.axis_index("c")
    return (1 - odd_b, odd_b, 3 - odd_a, 2 + odd_a)


def ids_kernel(ids, right, flex, line):
    line[...] = jnp.zeros_like(line)
    line[:, 0 : ids.shape[1]] = ids[...].astype(F32)


def line_kernel(*refs):
    for k, line in enumerate(refs[:-1]):
        refs[-1][k : k + 1, :] = line[...]


def table_kernel(*refs):
    my_x, my_z = lax.axis_index("x"), lax.axis_index("z")
    for j, lines in enumerate(refs[:-1]):
        for k in range(NZ):
            at = ((my_x + NX - j) % NX) * NZ + (my_z + NZ - k) % NZ
            refs[-1][pl.ds(at, 1), :] = lines[k : k + 1, :]


def first_kernel(ids, side_rows, right, flex, flexed, extra, counts, *sends):
    live = side_rows[...].astype(F32)
    which = lax.broadcasted_iota(jnp.int32, counts.shape, 0)
    counts[...] = jnp.where(which == 0, live[:, 0:1], live[:, 1:2])
    direction = (right[...] / cheb_center).astype(BF16)
    flexed[...] = dot(flex[...], direction, ((1,), (1,)))
    send_sides(counts, flexed, *sends)
    column = jnp.broadcast_to(ids[...], (LANES, LANES)).T
    extra[...] = jnp.zeros_like(extra)
    extra[:, extra.shape[1] - LANES :] = column[: extra.shape[0]]


def send_sides(counts, flexed, *sends):
    side = flexed.shape[0] // SIDES
    for k, wanted in enumerate(sent_sides()):
        rows = pl.ds(pl.multiple_of(wanted * side, 32), side)
        pack(sends[k], flexed[rows, 0:LANES], flexed[rows, LANES:], counts[k // 2 : k // 2 + 1, :])


def balance_kernel(counts, flexed, in_a, in_b, in_c, in_y, stiff, extra, balanced, told):
    side = flexed.shape[0] // SIDES
    loads = flexed.shape[1]
    wide = loads - LANES
    half = side // 2
    my_y, my_c, my_x, my_z = (lax.axis_index(a) for a in ALL)
    row = my_y * NC + my_c
    col = my_x * NZ + my_z
    odd_b, odd_a = my_z % 2 == 1, my_c == 1
    spot = (slice(side, side + 1), slice(2 * wide, 2 * wide + 1))
    count_west = jnp.where(odd_b, in_a[spot], in_b[spot])
    count_north = jnp.where(odd_a, in_c[spot], in_y[spot])
    count_east = counts[0:1, 0:1]
    count_south = counts[1:2, 0:1]

    for rows, lanes, there in (
        ((0, side), (0, LANES), ((0, side), (0, LANES))),
        ((0, half), (LANES, loads), ((side, side + half), (0, wide))),
        ((half, side), (LANES, loads), ((side, side + half), (wide, 2 * wide))),
    ):
        size = (rows[1] - rows[0], lanes[1] - lanes[0])
        at = (lax.broadcasted_iota(jnp.int32, size, 0) + rows[0]).astype(F32)
        a, b, c, y = (m[there[0][0] : there[0][1], there[1][0] : there[1][1]] for m in (in_a, in_b, in_c, in_y))
        west, east, north, south = (
            flexed[k * side + rows[0] : k * side + rows[1], lanes[0] : lanes[1]] for k in range(SIDES)
        )

        def half_jump(count, inside, ahead, behind):
            return jnp.where(jnp.logical_and(at < count, inside), 0.5 * (ahead - behind), 0.0)

        results = (
            west + half_jump(count_west, col > 0, jnp.where(odd_b, a, b), west),
            east - half_jump(count_east, col < N_GY - 1, east, jnp.where(odd_b, b, a)),
            north + half_jump(count_north, row > 0, jnp.where(odd_a, c, y), north),
            south - half_jump(count_south, row < N_GX - 1, south, jnp.where(odd_a, y, c)),
        )
        for k, result in enumerate(results):
            balanced[k * side + rows[0] : k * side + rows[1], lanes[0] : lanes[1]] = result.astype(BF16)
    corners = told.shape[1]
    told[0] = extra[...]
    told[0, :, 0:loads] = dot(stiff[0:32, :], balanced[...])[:corners]
    for k in range(1, told.shape[0]):
        told[k] = told[0]


def step_on(steps, flex, dir_low, low, new_dir_low, flex_base):
    new_dir = steps[0] * dir_low + steps[1] * low
    new_dir_low[...] = new_dir
    flex_base[...] = dot(flex[:, TOP:], new_dir.astype(BF16))


def first_bulk_kernel(steps, after, balanced, stiff, flex, right, *outs):
    right = right[...].T
    res_top, res_low, sol_top, sol_low, squares = outs[:5]
    stiffed = dot(stiff[...], balanced[...])
    direction = right / cheb_center
    low = right[TOP:, :] - stiffed[TOP:]
    res_top[...] = right[:TOP, :] - stiffed[:TOP]
    res_low[...] = low
    sol_top[...] = direction[:TOP]
    sol_low[...] = direction[TOP:]
    squares[...] = jnp.sum(low * low, axis=0, keepdims=True)
    step_on(steps, flex, direction[TOP:], low, *outs[5:])


def bulk_kernel(steps, balanced, stiff, flex, res_top, res_low, dir_top, dir_low, sol_top, sol_low, *outs):
    new_res_top, new_res_low, new_sol_top, new_sol_low, squares = outs[:5]
    stiffed = dot(stiff[...], balanced[...])
    low = res_low[...] - stiffed[TOP:]
    new_res_top[...] = res_top[...] - stiffed[:TOP]
    new_res_low[...] = low
    new_sol_top[...] = sol_top[...] + dir_top[...]
    new_sol_low[...] = sol_low[...] + dir_low[...]
    squares[...] = jnp.sum(low * low, axis=0, keepdims=True)
    if steps is not None:
        step_on(steps, flex, dir_low[...], low, *outs[5:])


def split_dot(high, low, values):
    values_high, values_low = split(values)
    return dot(high[...], values_high) + (dot(high[...], values_low) + dot(low[...], values_high))


def tree_sum(parts):
    while len(parts) > 1:
        parts = [p + q for p, q in zip(parts[::2], parts[1::2])]
    return parts[0]


def first_half_kernel(high, low, values, total):
    total[...] = split_dot(high, low, values[...].reshape(-1, values.shape[2]))


def first_product_kernel(after, high, low, values, half, total):
    more = split_dot(high, low, values[...].reshape(-1, values.shape[2]))
    total[...] = (half[...] + more).reshape(total.shape)


def gathered(blocks, stack):
    my_y = lax.axis_index("y")
    corners = blocks[0].shape[1]
    for k, block in enumerate(blocks):
        at = pl.multiple_of(((my_y + NY - k) % NY) * corners, TILE)
        stack[pl.ds(at, corners), :] = block[0]
    b = [block[0, 0:TILE, :] for block in blocks]
    return (b[0] + b[2]) + (b[1] + b[3])


def half_product_kernel(high, low, *refs):
    blocks, total, ride, stack = refs[:NY], refs[NY], refs[NY + 1], refs[NY + 2]
    ride[...] = gathered(blocks, stack)
    total[...] = split_dot(high, low, stack[...])


def product_kernel(loads, after, high, low, half, ride, *refs):
    blocks, total, stack = refs[:NY], refs[NY], refs[NY + 1]
    both = ride[...] + gathered(blocks, stack)
    result = (half[...] + split_dot(high, low, stack[...])).reshape(total.shape)
    lane = lax.broadcasted_iota(jnp.int32, both.shape, 1)
    for k in range(total.shape[0]):
        total[k] = result[k]
        total[k, 0:TILE, :] = jnp.where(lane < loads, result[k, 0:TILE, :], both)


def correction_of(terms, squares, res_top, new_res_top, earlier):
    corners = terms.shape[1]
    total = tree_sum([terms[k] for k in range(terms.shape[0])])
    if earlier is not None:
        earlier[...] = total[0:TILE, :]
    new_res_top[...] = res_top[...]
    new_res_top[:corners, :] = res_top[:corners, :] - total[:, : res_top.shape[1]]
    top = new_res_top[...]
    return top, squares[...] + jnp.sum(top * top, axis=0, keepdims=True)


def last_kernel(terms, squares, res_top, new_res_top, earlier, told):
    _, norm = correction_of(terms, squares, res_top, new_res_top, earlier)
    padded = jnp.concatenate([norm, jnp.zeros((1, told.shape[2] - norm.shape[1]), F32)], axis=1)
    told[...] = jnp.broadcast_to(padded[None], told.shape)


def correct_kernel(steps, first, counts, terms, squares, res_top, dir_top, flex, flex_base, *outs):
    earlier, outs = (None, outs) if first else (outs[0], outs[1:])
    new_res_top, extra, new_dir_top, flexed = outs[:4]
    top, norm = correction_of(terms, squares, res_top, new_res_top, earlier)
    new_dir = steps[0] * dir_top[...] + steps[1] * top
    new_dir_top[...] = new_dir
    flexed[...] = flex_base[...] + dot(flex[:, :TOP], new_dir.astype(BF16))
    send_sides(counts, flexed, *outs[4:])
    loads, width = norm.shape[1], extra.shape[1]
    spare = width - loads
    padded = jnp.concatenate([norm, jnp.zeros((1, spare), F32)], axis=1)
    padded = jnp.broadcast_to(padded, (TILE, width))
    line = lax.broadcasted_iota(jnp.int32, padded.shape, 0)
    ride = jnp.zeros_like(padded)
    for n in range(-(-loads // spare)):
        ride = jnp.where(line == n, pltpu.roll(padded, (loads - n * spare) % width, 1), ride)
    extra[...] = jnp.zeros_like(extra)
    extra[0:TILE, :] = ride


def rider_values(earlier, loads):
    spare = earlier.shape[1] - loads
    lines = -(-loads // spare)
    return earlier[:lines, loads:].reshape(-1)[:loads]


def local(right_side, flex, stiff, coarse_inv, corner_map, side_rows):
    right = right_side[0, 0]
    flex_block = flex[0, 0]
    stiff_block = stiff[0, 0]
    order = flex_block.shape[0]
    side = order // SIDES
    loads = right.shape[0]
    width = -(-loads // LANES) * LANES
    corners = corner_map.shape[2]
    rows_held, cols_held = coarse_inv.shape
    half = N_GY * corners
    (ids_line,) = call(ids_kernel, [shape(1, LANES)], unread=(right, flex_block))(corner_map[0])
    lines = [ids_line]
    for k in range(1, NZ):
        lines.append(turned(ids_line, "z", NZ, k))
    (line,) = call(line_kernel, [shape(NZ, LANES)])(*lines)
    tables = [line]
    for k in range(1, NX):
        tables.append(turned(line, "x", NX, k))
    (own_ids,) = call(table_kernel, [shape(N_GY, LANES)])(*tables)
    other_ids = turned(own_ids, "c", NC, 1)

    inv_t = coarse_inv.T
    inv_blocks = [inv_t]
    for k in range(1, NY):
        inv_blocks.append(turned(inv_t, "y", NY, k))

    sides = [shape(side + side // 2, LANES)] * SIDES
    flexed, extra, counts, *sends = call(
        first_kernel, [shape(order, loads), shape(corners, width), shape(TILE, LANES)] + sides
    )(ids_line, side_rows[0], right, flex_block)

    own_rows, other_rows = call(
        rows_kernel, [shape(cols_held, half)] * 2, scratch=[pltpu.VMEM((2 * half, rows_held), BF16)]
    )(own_ids, other_ids, *inv_blocks)
    own_rows = own_rows + turned(other_rows, "c", NC, 1)

    row_parts = [own_rows]
    for k in range(1, NZ):
        row_parts.append(turned(own_rows, "z", NZ, k))

    tops, lows = shape(TOP, loads), shape(order - TOP, loads)
    ride_shape = shape(TILE, width)
    corner_scratch = [pltpu.VMEM((NY * corners, width), F32)]
    rho_prev = 1.0 / cheb_sigma
    norms = []
    for iteration in range(ITERS):
        last = iteration + 1 == ITERS
        ins = []
        for k in range(SIDES):
            axes, count = (GY, N_GY) if k < 2 else (GX, N_GX)
            ins.append(swapped(sends[k], axes, count, k % 2))
        balanced, told = call(
            balance_kernel, [shape(order, loads, dtype=BF16), shape(NY * NX if iteration == 0 else 1, corners, width)]
        )(counts, flexed, *ins, stiff_block, extra)
        steps = None
        if not last:
            rho_next = 1.0 / (2.0 * cheb_sigma - rho_prev)
            steps = (rho_next * rho_prev, 2.0 * rho_next / cheb_half)
            rho_prev = rho_next
        if iteration == 0:
            values = to_all(told, ("y", "x"))
            kernel, state = first_bulk_kernel, (right,)
            order_after = (values,)
        else:
            values = [told]
            for k in range(1, NY):
                values.append(turned(told, "y", NY, k))
            kernel, state = bulk_kernel, (res_top, res_low, dir_top, dir_low, sol_top, sol_low)
            order_after = ()
        outs = call(
            functools.partial(kernel, steps),
            [tops, lows, tops, lows, shape(1, loads)] + ([] if last else [lows, shape(order, loads)]),
        )(*order_after, balanced, stiff_block, flex_block, *state)
        res_top, res_low, sol_top, sol_low, squares = outs[:5]
        if iteration == 0:
            dir_top = sol_top
            values_other = turned(values, "c", NC, 1)
            own_high, own_low, other_high, other_low, *shares = call(
                cols_kernel,
                [shape(half, half, dtype=BF16)] * 4 + [shape(half // NX * 2, half)] * NX,
                scratch=[pltpu.VMEM((2 * half, cols_held), BF16), pltpu.VMEM((2 * half, half), F32)],
            )(values, values_other, *row_parts)
            (partial,) = call(first_half_kernel, [shape(half, width)])(own_high, own_low, values)
            (partial,) = call(first_product_kernel, [shape(N_GY, corners, width)])(
                squares, other_high, other_low, values_other, partial
            )
            for k in range(1, NX):
                shares[k] = turned(shares[k], "x", NX, k)
            block = call(block_kernel, [shape(half, NY * corners, dtype=BF16)] * 4)(*shares)
        else:
            others = []
            for k in range(NY):
                others.append(turned(values[k], "c", NC, 1))
            partial, ride = call(
                half_product_kernel, [shape(half, width), ride_shape], scratch=corner_scratch
            )(*block[:2], *values)
            (partial,) = call(
                functools.partial(product_kernel, loads), [shape(N_GY, corners, width)], scratch=corner_scratch
            )(squares, *block[2:], partial, ride, *others)
        terms = to_all(partial, GY)
        if last:
            res_top, earlier, told = call(
                last_kernel, [tops, ride_shape, shape(N_GX * N_GY, 1, width)]
            )(terms, squares, res_top)
        else:
            dir_low, flex_base = outs[5:]
            outs = call(
                functools.partial(correct_kernel, steps, iteration == 0),
                ([ride_shape] if iteration > 0 else [])
                + [tops, shape(corners, width), tops, shape(order, loads)]
                + sides,
            )(counts, terms, squares, res_top, dir_top, flex_block, flex_base)
            if iteration > 0:
                earlier, *outs = outs
            res_top, extra, dir_top, flexed, *sends = outs
        if iteration > 0:
            norms.append(rider_values(earlier, loads))
    norms.append(to_all(told, ALL).sum(axis=0)[0, :loads])
    resid_norm = jnp.sqrt(jnp.stack(norms) / (N_GX * N_GY * order))
    solution = jnp.concatenate([sol_top, sol_low]).T
    residual = jnp.concatenate([res_top, res_low]).T
    return (solution[None, None], residual[None, None], resid_norm)


def solution(mesh):
    torus = Mesh(mesh.devices.reshape(NY, NC, NX, NZ), ALL)
    return jax.shard_map(
        local,
        mesh=torus,
        in_specs=(
            P(GX, GY, None, None),
            P(GX, GY, None, None),
            P(GX, GY, None, None),
            P(GX, GY),
            P(GX, GY, None),
            P(GX, GY, None),
        ),
        out_specs=(P(GX, GY, None, None), P(GX, GY, None, None), P()),
        check_vma=False,
    )
```

```python
import functools

import jax
import jax.numpy as jnp
from jax import lax
from jax.experimental import pallas as pl
from jax.experimental.pallas import tpu as pltpu
from jax.sharding import Mesh
from jax.sharding import PartitionSpec as P

ITERS = 3
GX = ("y", "c")
GY = ("x", "z")
ALL = ("y", "c", "x", "z")
NY, NC, NX, NZ = 4, 2, 4, 4
N_GX, N_GY = NY * NC, NX * NZ
SIDES = 4
TOP = 128
LANES = 128
TILE = 8
VMEM_BYTES = 16 * 2**20

cheb_center = 1.15
cheb_half = 0.85
cheb_sigma = cheb_center / cheb_half
F32 = jnp.float32
BF16 = jnp.bfloat16


def turned(array, axes, count, by):
    return lax.ppermute(array, axes, [(i, (i + by) % count) for i in range(count)])


def swapped(array, axes, count, shift):
    pairs = [(i, (((i + shift) ^ 1) - shift) % count) for i in range(count)]
    return lax.ppermute(array, axes, pairs)


def to_all(copies, axes):
    return lax.all_to_all(copies, axes, split_axis=0, concat_axis=0, tiled=True)


def vm():
    return pl.BlockSpec(memory_space=pltpu.VMEM)


def call(body, outs, scratch=(), unread=()):
    def run(*operands):
        return pl.pallas_call(
            body,
            out_shape=outs,
            in_specs=[vm() for _ in operands] + [pl.BlockSpec(memory_space=pltpu.HBM) for _ in unread],
            out_specs=[vm() for _ in outs],
            scratch_shapes=scratch,
            compiler_params=pltpu.CompilerParams(vmem_limit_bytes=VMEM_BYTES),
        )(
            *[pltpu.with_memory_space_constraint(o, pltpu.VMEM) for o in operands],
            *[pltpu.with_memory_space_constraint(o, pltpu.HBM) for o in unread],
        )

    return run


def shape(*dims, dtype=F32):
    return pltpu.VMEM(dims, dtype)


def dot(a, b, contract=((1,), (0,))):
    return lax.dot_general(a, b, (contract, ((), ())), preferred_element_type=F32)


def split(a):
    high = a.astype(BF16)
    return high, (a - high.astype(F32)).astype(BF16)


def mark(pick, columns, held):
    corners = columns[0].shape[0]
    at = lax.broadcasted_iota(jnp.int32, (2 * corners, held), 1).astype(F32)
    for n in range(0, len(columns), 2):
        ids = jnp.concatenate(columns[n : n + 2], axis=0)
        pick[n * corners : (n + 2) * corners, :] = jnp.where(at == ids, 1.0, 0.0).astype(BF16)


def rows_kernel(ids_own, ids_other, *refs):
    blocks, own, other, pick = refs[:-3], refs[-3], refs[-2], refs[-1]
    my_y, my_c = lax.axis_index("y"), lax.axis_index("c")
    held = blocks[0].shape[1]
    half = own.shape[1]
    corners = half // N_GY
    lists = [ids[...].T[:corners] for ids in (ids_own, ids_other)]
    total = 0.0
    for k, block in enumerate(blocks):
        base = ((((my_y + NY - k) % NY) * NC + my_c) * held).astype(F32)
        shifted = [ids - base for ids in lists]
        mark(pick, [ids[:, n : n + 1] for ids in shifted for n in range(N_GY)], held)
        for part in split(block[...]):
            total = total + dot(part, pick[...], ((1,), (1,)))
    own[...] = total[:, :half]
    other[...] = total[:, half:]


def cols_kernel(*refs):
    values, refs = refs[: NC * NX], refs[NC * NX :]
    blocks, outs, sends, pick, total = refs[:NZ], refs[NZ : NZ + 4], refs[NZ + 4 : -2], refs[-2], refs[-1]
    my_x, my_z = lax.axis_index("x"), lax.axis_index("z")
    held = blocks[0].shape[0]
    half = outs[0].shape[1]
    share = half // NX
    last = values[0].shape[2] - 1
    columns = [v[n, :, last:] for v in values for n in range(NY)]
    summed = 0.0
    for k, block in enumerate(blocks):
        base = ((my_x * NZ + (my_z + NZ - k) % NZ) * held).astype(F32)
        mark(pick, [ids - base for ids in columns], held)
        for part in split(block[...]):
            summed = summed + dot(pick[...], part)
    total[...] = summed
    for n in range(2):
        outs[2 * n][...], outs[2 * n + 1][...] = split(summed[n * half : (n + 1) * half].T)
    for k, send in enumerate(sends):
        for n in range(NC):
            start = n * half + ((NX - k) % NX) * share
            send[n * share : (n + 1) * share, :] = total[start : start + share, :]


def block_kernel(*refs):
    parts, outs = refs[:NX], refs[NX:]
    block = ((parts[0][...] + parts[1][...]) + (parts[2][...] + parts[3][...])).T
    half = block.shape[1] // 2
    for n in range(2):
        outs[2 * n][...], outs[2 * n + 1][...] = split(block[:, n * half : (n + 1) * half])


def pack(out, main, rest, count):
    side, wide = main.shape[0], rest.shape[1]
    half = side // 2
    out[0:side, :] = main
    out[side : side + half, 0:wide] = rest[:half]
    out[side : side + half, wide : 2 * wide] = rest[half:]
    out[side : side + half, 2 * wide :] = jnp.broadcast_to(count[:, 2 * wide :], (half, LANES - 2 * wide))


def sent_sides():
    odd_b, odd_a = lax.axis_index("z") % 2, lax.axis_index("c")
    return (1 - odd_b, odd_b, 3 - odd_a, 2 + odd_a)


def ids_kernel(ids, right, flex, line):
    line[...] = jnp.zeros_like(line)
    line[:, 0 : ids.shape[1]] = ids[...].astype(F32)


def line_kernel(*refs):
    for k, line in enumerate(refs[:-1]):
        refs[-1][k : k + 1, :] = line[...]


def table_kernel(*refs):
    my_x, my_z = lax.axis_index("x"), lax.axis_index("z")
    for j, lines in enumerate(refs[:-1]):
        for k in range(NZ):
            at = ((my_x + NX - j) % NX) * NZ + (my_z + NZ - k) % NZ
            refs[-1][pl.ds(at, 1), :] = lines[k : k + 1, :]


def first_kernel(ids, side_rows, right, flex, flexed, extra, counts, *sends):
    live = side_rows[...].astype(F32)
    which = lax.broadcasted_iota(jnp.int32, counts.shape, 0)
    counts[...] = jnp.where(which == 0, live[:, 0:1], live[:, 1:2])
    direction = (right[...] / cheb_center).astype(BF16)
    flexed[...] = dot(flex[...], direction, ((1,), (1,)))
    send_sides(counts, flexed, *sends)
    column = jnp.broadcast_to(ids[...], (LANES, LANES)).T
    extra[...] = jnp.zeros_like(extra)
    extra[:, extra.shape[1] - LANES :] = column[: extra.shape[0]]


def send_sides(counts, flexed, *sends):
    side = flexed.shape[0] // SIDES
    for k, wanted in enumerate(sent_sides()):
        rows = pl.ds(pl.multiple_of(wanted * side, 32), side)
        pack(sends[k], flexed[rows, 0:LANES], flexed[rows, LANES:], counts[k // 2 : k // 2 + 1, :])


def balance_kernel(counts, flexed, in_a, in_b, in_c, in_y, stiff, extra, balanced, told):
    side = flexed.shape[0] // SIDES
    loads = flexed.shape[1]
    wide = loads - LANES
    half = side // 2
    my_y, my_c, my_x, my_z = (lax.axis_index(a) for a in ALL)
    row = my_y * NC + my_c
    col = my_x * NZ + my_z
    odd_b, odd_a = my_z % 2 == 1, my_c == 1
    spot = (slice(side, side + 1), slice(2 * wide, 2 * wide + 1))
    count_west = jnp.where(odd_b, in_a[spot], in_b[spot])
    count_north = jnp.where(odd_a, in_c[spot], in_y[spot])
    count_east = counts[0:1, 0:1]
    count_south = counts[1:2, 0:1]

    for rows, lanes, there in (
        ((0, side), (0, LANES), ((0, side), (0, LANES))),
        ((0, half), (LANES, loads), ((side, side + half), (0, wide))),
        ((half, side), (LANES, loads), ((side, side + half), (wide, 2 * wide))),
    ):
        size = (rows[1] - rows[0], lanes[1] - lanes[0])
        at = (lax.broadcasted_iota(jnp.int32, size, 0) + rows[0]).astype(F32)
        a, b, c, y = (m[there[0][0] : there[0][1], there[1][0] : there[1][1]] for m in (in_a, in_b, in_c, in_y))
        west, east, north, south = (
            flexed[k * side + rows[0] : k * side + rows[1], lanes[0] : lanes[1]] for k in range(SIDES)
        )

        def half_jump(count, inside, ahead, behind):
            return jnp.where(jnp.logical_and(at < count, inside), 0.5 * (ahead - behind), 0.0)

        results = (
            west + half_jump(count_west, col > 0, jnp.where(odd_b, a, b), west),
            east - half_jump(count_east, col < N_GY - 1, east, jnp.where(odd_b, b, a)),
            north + half_jump(count_north, row > 0, jnp.where(odd_a, c, y), north),
            south - half_jump(count_south, row < N_GX - 1, south, jnp.where(odd_a, y, c)),
        )
        for k, result in enumerate(results):
            balanced[k * side + rows[0] : k * side + rows[1], lanes[0] : lanes[1]] = result.astype(BF16)
    corners = told.shape[1]
    told[0] = extra[...]
    told[0, :, 0:loads] = dot(stiff[0:32, :], balanced[...])[:corners]


def step_on(steps, flex, dir_low, low, new_dir_low, flex_base):
    new_dir = steps[0] * dir_low + steps[1] * low
    new_dir_low[...] = new_dir
    flex_base[...] = dot(flex[:, TOP:], new_dir.astype(BF16))


def first_bulk_kernel(steps, balanced, stiff, flex, right, *outs):
    right = right[...].T
    res_top, res_low, sol_top, sol_low, squares = outs[:5]
    stiffed = dot(stiff[...], balanced[...])
    direction = right / cheb_center
    low = right[TOP:, :] - stiffed[TOP:]
    res_top[...] = right[:TOP, :] - stiffed[:TOP]
    res_low[...] = low
    sol_top[...] = direction[:TOP]
    sol_low[...] = direction[TOP:]
    squares[...] = jnp.sum(low * low, axis=0, keepdims=True)
    step_on(steps, flex, direction[TOP:], low, *outs[5:])


def bulk_kernel(steps, balanced, stiff, flex, res_top, res_low, dir_top, dir_low, sol_top, sol_low, *outs):
    new_res_top, new_res_low, new_sol_top, new_sol_low, squares = outs[:5]
    stiffed = dot(stiff[...], balanced[...])
    low = res_low[...] - stiffed[TOP:]
    new_res_top[...] = res_top[...] - stiffed[:TOP]
    new_res_low[...] = low
    new_sol_top[...] = sol_top[...] + dir_top[...]
    new_sol_low[...] = sol_low[...] + dir_low[...]
    squares[...] = jnp.sum(low * low, axis=0, keepdims=True)
    if steps is not None:
        step_on(steps, flex, dir_low[...], low, *outs[5:])


def split_dot(high, low, values):
    values_high, values_low = split(values)
    return dot(high[...], values_high) + (dot(high[...], values_low) + dot(low[...], values_high))


def tree_sum(parts):
    while len(parts) > 1:
        parts = [p + q for p, q in zip(parts[::2], parts[1::2])]
    return parts[0]


def rows_of(values):
    return jnp.concatenate([v[...].reshape(-1, v.shape[2]) for v in values], axis=0)


def stack_kernel(*refs):
    for k, block in enumerate(refs[:-1]):
        refs[-1][k] = block[0]


def first_half_kernel(high, low, *refs):
    refs[-1][...] = split_dot(high, low, rows_of(refs[:-1]))


def first_product_kernel(high, low, half, *refs):
    total = refs[-1]
    total[...] = (half[...] + split_dot(high, low, rows_of(refs[:-1]))).reshape(total.shape)


def gathered(blocks, stack):
    corners = blocks[0].shape[1]
    for k, block in enumerate(blocks):
        stack[k * corners : (k + 1) * corners, :] = block[0]
    b = [block[0, 0:TILE, :] for block in blocks]
    return (b[0] + b[2]) + (b[1] + b[3])


def half_product_kernel(high, low, *refs):
    blocks, total, ride, stack = refs[:NY], refs[NY], refs[NY + 1], refs[NY + 2]
    ride[...] = gathered(blocks, stack)
    total[...] = split_dot(high, low, stack[...])


def product_kernel(loads, after, high, low, half, ride, *refs):
    blocks, total, stack = refs[:NY], refs[NY], refs[NY + 1]
    both = ride[...] + gathered(blocks, stack)
    result = (half[...] + split_dot(high, low, stack[...])).reshape(total.shape)
    lane = lax.broadcasted_iota(jnp.int32, both.shape, 1)
    for k in range(total.shape[0]):
        total[k] = result[k]
        total[k, 0:TILE, :] = jnp.where(lane < loads, result[k, 0:TILE, :], both)


def correction_of(terms, squares, res_top, new_res_top, earlier):
    corners = terms.shape[1]
    total = tree_sum([terms[k] for k in range(terms.shape[0])])
    if earlier is not None:
        earlier[...] = total[0:TILE, :]
    new_res_top[...] = res_top[...]
    new_res_top[:corners, :] = res_top[:corners, :] - total[:, : res_top.shape[1]]
    top = new_res_top[...]
    return top, squares[...] + jnp.sum(top * top, axis=0, keepdims=True)


def last_kernel(terms, squares, res_top, new_res_top, earlier, told):
    _, norm = correction_of(terms, squares, res_top, new_res_top, earlier)
    padded = jnp.concatenate([norm, jnp.zeros((1, told.shape[2] - norm.shape[1]), F32)], axis=1)
    told[...] = jnp.broadcast_to(padded[None], told.shape)


def correct_kernel(steps, first, counts, terms, squares, res_top, dir_top, flex, flex_base, *outs):
    earlier, outs = (None, outs) if first else (outs[0], outs[1:])
    new_res_top, extra, new_dir_top, flexed = outs[:4]
    top, norm = correction_of(terms, squares, res_top, new_res_top, earlier)
    new_dir = steps[0] * dir_top[...] + steps[1] * top
    new_dir_top[...] = new_dir
    flexed[...] = flex_base[...] + dot(flex[:, :TOP], new_dir.astype(BF16))
    send_sides(counts, flexed, *outs[4:])
    loads, width = norm.shape[1], extra.shape[1]
    spare = width - loads
    padded = jnp.concatenate([norm, jnp.zeros((1, spare), F32)], axis=1)
    padded = jnp.broadcast_to(padded, (TILE, width))
    line = lax.broadcasted_iota(jnp.int32, padded.shape, 0)
    ride = jnp.zeros_like(padded)
    for n in range(-(-loads // spare)):
        ride = jnp.where(line == n, pltpu.roll(padded, (loads - n * spare) % width, 1), ride)
    extra[...] = jnp.zeros_like(extra)
    extra[0:TILE, :] = ride


def rider_values(earlier, loads):
    spare = earlier.shape[1] - loads
    lines = -(-loads // spare)
    return earlier[:lines, loads:].reshape(-1)[:loads]


def local(right_side, flex, stiff, coarse_inv, corner_map, side_rows):
    right = right_side[0, 0]
    flex_block = flex[0, 0]
    stiff_block = stiff[0, 0]
    order = flex_block.shape[0]
    side = order // SIDES
    loads = right.shape[0]
    width = -(-loads // LANES) * LANES
    corners = corner_map.shape[2]
    rows_held, cols_held = coarse_inv.shape
    half = N_GY * corners
    (ids_line,) = call(ids_kernel, [shape(1, LANES)], unread=(right, flex_block))(corner_map[0])
    lines = [ids_line]
    for k in range(1, NZ):
        lines.append(turned(ids_line, "z", NZ, k))
    (line,) = call(line_kernel, [shape(NZ, LANES)])(*lines)
    tables = [line]
    for k in range(1, NX):
        tables.append(turned(line, "x", NX, k))
    (own_ids,) = call(table_kernel, [shape(N_GY, LANES)])(*tables)
    other_ids = turned(own_ids, "c", NC, 1)

    inv_t = coarse_inv.T
    inv_blocks = [inv_t]
    for k in range(1, NY):
        inv_blocks.append(turned(inv_t, "y", NY, k))

    sides = [shape(side + side // 2, LANES)] * SIDES
    flexed, extra, counts, *sends = call(
        first_kernel, [shape(order, loads), shape(corners, width), shape(TILE, LANES)] + sides
    )(ids_line, side_rows[0], right, flex_block)

    own_rows, other_rows = call(
        rows_kernel, [shape(cols_held, half)] * 2, scratch=[pltpu.VMEM((2 * half, rows_held), BF16)]
    )(own_ids, other_ids, *inv_blocks)
    own_rows = own_rows + turned(other_rows, "c", NC, 1)

    row_parts = [own_rows]
    for k in range(1, NZ):
        row_parts.append(turned(own_rows, "z", NZ, k))

    tops, lows = shape(TOP, loads), shape(order - TOP, loads)
    ride_shape = shape(TILE, width)
    corner_scratch = [pltpu.VMEM((NY * corners, width), F32)]
    rho_prev = 1.0 / cheb_sigma
    norms = []
    for iteration in range(ITERS):
        last = iteration + 1 == ITERS
        ins = []
        for k in range(SIDES):
            axes, count = (GY, N_GY) if k < 2 else (GX, N_GX)
            ins.append(swapped(sends[k], axes, count, k % 2))
        balanced, told = call(
            balance_kernel, [shape(order, loads, dtype=BF16), shape(1, corners, width)]
        )(counts, flexed, *ins, stiff_block, extra)
        steps = None
        if not last:
            rho_next = 1.0 / (2.0 * cheb_sigma - rho_prev)
            steps = (rho_next * rho_prev, 2.0 * rho_next / cheb_half)
            rho_prev = rho_next
        values = [told]
        for k in range(1, NY):
            values.append(turned(told, "y", NY, k))
        if iteration == 0:
            (stacked,) = call(stack_kernel, [shape(NY, corners, width)])(*values)
            values = [stacked]
            for k in range(1, NX):
                values.append(turned(stacked, "x", NX, k))
            kernel, state = first_bulk_kernel, (right,)
        else:
            kernel, state = bulk_kernel, (res_top, res_low, dir_top, dir_low, sol_top, sol_low)
        outs = call(
            functools.partial(kernel, steps),
            [tops, lows, tops, lows, shape(1, loads)] + ([] if last else [lows, shape(order, loads)]),
        )(balanced, stiff_block, flex_block, *state)
        res_top, res_low, sol_top, sol_low, squares = outs[:5]
        others = []
        for value in values:
            others.append(turned(value, "c", NC, 1))
        if iteration == 0:
            dir_top = sol_top
            own_high, own_low, other_high, other_low, *shares = call(
                cols_kernel,
                [shape(half, half, dtype=BF16)] * 4 + [shape(half // NX * 2, half)] * NX,
                scratch=[pltpu.VMEM((2 * half, cols_held), BF16), pltpu.VMEM((2 * half, half), F32)],
            )(*values, *others, *row_parts)
            (partial,) = call(first_half_kernel, [shape(half, width)])(own_high, own_low, *values)
            (partial,) = call(first_product_kernel, [shape(N_GY, corners, width)])(
                other_high, other_low, partial, *others
            )
            for k in range(1, NX):
                shares[k] = turned(shares[k], "x", NX, k)
            block = call(block_kernel, [shape(half, NY * corners, dtype=BF16)] * 4)(*shares)
        else:
            partial, ride = call(
                half_product_kernel, [shape(half, width), ride_shape], scratch=corner_scratch
            )(*block[:2], *values)
            (partial,) = call(
                functools.partial(product_kernel, loads), [shape(N_GY, corners, width)], scratch=corner_scratch
            )(squares, *block[2:], partial, ride, *others)
        terms = to_all(partial, GY)
        if last:
            res_top, earlier, told = call(
                last_kernel, [tops, ride_shape, shape(N_GX * N_GY, 1, width)]
            )(terms, squares, res_top)
        else:
            dir_low, flex_base = outs[5:]
            outs = call(
                functools.partial(correct_kernel, steps, iteration == 0),
                ([ride_shape] if iteration > 0 else [])
                + [tops, shape(corners, width), tops, shape(order, loads)]
                + sides,
            )(counts, terms, squares, res_top, dir_top, flex_block, flex_base)
            if iteration > 0:
                earlier, *outs = outs
            res_top, extra, dir_top, flexed, *sends = outs
        if iteration > 0:
            norms.append(rider_values(earlier, loads))
    norms.append(to_all(told, ALL).sum(axis=0)[0, :loads])
    resid_norm = jnp.sqrt(jnp.stack(norms) / (N_GX * N_GY * order))
    solution = jnp.concatenate([sol_top, sol_low]).T
    residual = jnp.concatenate([res_top, res_low]).T
    return (solution[None, None], residual[None, None], resid_norm)


def solution(mesh):
    torus = Mesh(mesh.devices.reshape(NY, NC, NX, NZ), ALL)
    return jax.shard_map(
        local,
        mesh=torus,
        in_specs=(
            P(GX, GY, None, None),
            P(GX, GY, None, None),
            P(GX, GY, None, None),
            P(GX, GY),
            P(GX, GY, None),
            P(GX, GY, None),
        ),
        out_specs=(P(GX, GY, None, None), P(GX, GY, None, None), P()),
        check_vma=False,
    )
```

```python
import functools

import jax
import jax.numpy as jnp
from jax import lax
from jax.experimental import pallas as pl
from jax.experimental.pallas import tpu as pltpu
from jax.sharding import Mesh
from jax.sharding import PartitionSpec as P

ITERS = 3
GX = ("y", "c")
GY = ("x", "z")
ALL = ("y", "c", "x", "z")
NY, NC, NX, NZ = 4, 2, 4, 4
N_GX, N_GY = NY * NC, NX * NZ
SIDES = 4
TOP = 128
LANES = 128
TILE = 8
VMEM_BYTES = 16 * 2**20

cheb_center = 1.15
cheb_half = 0.85
cheb_sigma = cheb_center / cheb_half
F32 = jnp.float32
BF16 = jnp.bfloat16


def turned(array, axes, count, by):
    return lax.ppermute(array, axes, [(i, (i + by) % count) for i in range(count)])


def swapped(array, axes, count, shift):
    pairs = [(i, (((i + shift) ^ 1) - shift) % count) for i in range(count)]
    return lax.ppermute(array, axes, pairs)


def to_all(copies, axes):
    return lax.all_to_all(copies, axes, split_axis=0, concat_axis=0, tiled=True)


def vm():
    return pl.BlockSpec(memory_space=pltpu.VMEM)


def call(body, outs, scratch=(), unread=()):
    def run(*operands):
        return pl.pallas_call(
            body,
            out_shape=outs,
            in_specs=[vm() for _ in operands] + [pl.BlockSpec(memory_space=pltpu.HBM) for _ in unread],
            out_specs=[vm() for _ in outs],
            scratch_shapes=scratch,
            compiler_params=pltpu.CompilerParams(vmem_limit_bytes=VMEM_BYTES),
        )(
            *[pltpu.with_memory_space_constraint(o, pltpu.VMEM) for o in operands],
            *[pltpu.with_memory_space_constraint(o, pltpu.HBM) for o in unread],
        )

    return run


def shape(*dims, dtype=F32):
    return pltpu.VMEM(dims, dtype)


def dot(a, b, contract=((1,), (0,))):
    return lax.dot_general(a, b, (contract, ((), ())), preferred_element_type=F32)


def split(a):
    high = a.astype(BF16)
    return high, (a - high.astype(F32)).astype(BF16)


def mark(pick, columns, held):
    corners = columns[0].shape[0]
    at = lax.broadcasted_iota(jnp.int32, (2 * corners, held), 1).astype(F32)
    for n in range(0, len(columns), 2):
        ids = jnp.concatenate(columns[n : n + 2], axis=0)
        pick[n * corners : (n + 2) * corners, :] = jnp.where(at == ids, 1.0, 0.0).astype(BF16)


def rows_kernel(ids_own, ids_other, *refs):
    blocks, own, other, pick = refs[:-3], refs[-3], refs[-2], refs[-1]
    my_y, my_c = lax.axis_index("y"), lax.axis_index("c")
    held = blocks[0].shape[1]
    half = own.shape[1]
    corners = half // N_GY
    lists = [ids[...].T[:corners] for ids in (ids_own, ids_other)]
    total = 0.0
    for k, block in enumerate(blocks):
        base = ((((my_y + NY - k) % NY) * NC + my_c) * held).astype(F32)
        shifted = [ids - base for ids in lists]
        mark(pick, [ids[:, n : n + 1] for ids in shifted for n in range(N_GY)], held)
        for part in split(block[...]):
            total = total + dot(part, pick[...], ((1,), (1,)))
    own[...] = total[:, :half]
    other[...] = total[:, half:]


def cols_kernel(own, other, *refs):
    blocks, outs, sends, pick, total = refs[:NZ], refs[NZ : NZ + 4], refs[NZ + 4 : -2], refs[-2], refs[-1]
    my_x, my_z = lax.axis_index("x"), lax.axis_index("z")
    held = blocks[0].shape[0]
    half = outs[0].shape[1]
    last = own.shape[2] - 1
    corners = own.shape[1]
    columns = [v[n, :, last:] for v in (own, other) for n in range(v.shape[0])]
    summed = 0.0
    for k, block in enumerate(blocks):
        base = ((my_x * NZ + (my_z + NZ - k) % NZ) * held).astype(F32)
        mark(pick, [ids - base for ids in columns], held)
        for part in split(block[...]):
            summed = summed + dot(pick[...], part)
    total[...] = summed
    for n in range(2):
        outs[2 * n][...], outs[2 * n + 1][...] = split(summed[n * half : (n + 1) * half].T)
    for k, send in enumerate(sends):
        for n in range(NC * NY):
            start = pl.multiple_of((n * NX + (my_x + k) % NX) * corners, TILE)
            send[n * corners : (n + 1) * corners, :] = total[pl.ds(start, corners), :]


def block_kernel(*refs):
    parts, outs = refs[:NX], refs[NX:]
    block = ((parts[0][...] + parts[1][...]) + (parts[2][...] + parts[3][...])).T
    half = block.shape[1] // 2
    for n in range(2):
        outs[2 * n][...], outs[2 * n + 1][...] = split(block[:, n * half : (n + 1) * half])


def pack(out, main, rest, count):
    side, wide = main.shape[0], rest.shape[1]
    half = side // 2
    out[0:side, :] = main
    out[side : side + half, 0:wide] = rest[:half]
    out[side : side + half, wide : 2 * wide] = rest[half:]
    out[side : side + half, 2 * wide :] = jnp.broadcast_to(count[:, 2 * wide :], (half, LANES - 2 * wide))


def sent_sides():
    odd_b, odd_a = lax.axis_index("z") % 2, lax.axis_index("c")
    return (1 - odd_b, odd_b, 3 - odd_a, 2 + odd_a)


def ids_kernel(ids, right, flex, told, line):
    line[...] = jnp.zeros_like(line)
    line[:, 0 : ids.shape[1]] = ids[...].astype(F32)
    told[...] = jnp.broadcast_to(line[...][None], told.shape)


def first_kernel(after, ids, side_rows, right, flex, flexed, extra, counts, *sends):
    direction = (right[...] / cheb_center).astype(BF16)
    flexed[...] = dot(flex[...], direction, ((1,), (1,)))
    live = side_rows[...].astype(F32)
    which = lax.broadcasted_iota(jnp.int32, counts.shape, 0)
    counts[...] = jnp.where(which == 0, live[:, 0:1], live[:, 1:2])
    send_sides(counts, flexed, *sends)
    column = jnp.broadcast_to(ids[...], (LANES, LANES)).T
    extra[...] = jnp.zeros_like(extra)
    extra[:, extra.shape[1] - LANES :] = column[: extra.shape[0]]


def send_sides(counts, flexed, *sends):
    side = flexed.shape[0] // SIDES
    for k, wanted in enumerate(sent_sides()):
        rows = pl.ds(pl.multiple_of(wanted * side, 32), side)
        pack(sends[k], flexed[rows, 0:LANES], flexed[rows, LANES:], counts[k // 2 : k // 2 + 1, :])


def balance_kernel(counts, flexed, in_a, in_b, in_c, in_y, stiff, extra, balanced, told):
    side = flexed.shape[0] // SIDES
    loads = flexed.shape[1]
    wide = loads - LANES
    half = side // 2
    my_y, my_c, my_x, my_z = (lax.axis_index(a) for a in ALL)
    row = my_y * NC + my_c
    col = my_x * NZ + my_z
    odd_b, odd_a = my_z % 2 == 1, my_c == 1
    spot = (slice(side, side + 1), slice(2 * wide, 2 * wide + 1))
    count_west = jnp.where(odd_b, in_a[spot], in_b[spot])
    count_north = jnp.where(odd_a, in_c[spot], in_y[spot])
    count_east = counts[0:1, 0:1]
    count_south = counts[1:2, 0:1]

    for rows, lanes, there in (
        ((0, side), (0, LANES), ((0, side), (0, LANES))),
        ((0, half), (LANES, loads), ((side, side + half), (0, wide))),
        ((half, side), (LANES, loads), ((side, side + half), (wide, 2 * wide))),
    ):
        size = (rows[1] - rows[0], lanes[1] - lanes[0])
        at = (lax.broadcasted_iota(jnp.int32, size, 0) + rows[0]).astype(F32)
        a, b, c, y = (m[there[0][0] : there[0][1], there[1][0] : there[1][1]] for m in (in_a, in_b, in_c, in_y))
        west, east, north, south = (
            flexed[k * side + rows[0] : k * side + rows[1], lanes[0] : lanes[1]] for k in range(SIDES)
        )

        def half_jump(count, inside, ahead, behind):
            return jnp.where(jnp.logical_and(at < count, inside), 0.5 * (ahead - behind), 0.0)

        results = (
            west + half_jump(count_west, col > 0, jnp.where(odd_b, a, b), west),
            east - half_jump(count_east, col < N_GY - 1, east, jnp.where(odd_b, b, a)),
            north + half_jump(count_north, row > 0, jnp.where(odd_a, c, y), north),
            south - half_jump(count_south, row < N_GX - 1, south, jnp.where(odd_a, y, c)),
        )
        for k, result in enumerate(results):
            balanced[k * side + rows[0] : k * side + rows[1], lanes[0] : lanes[1]] = result.astype(BF16)
    corners = told.shape[1]
    told[0] = extra[...]
    told[0, :, 0:loads] = dot(stiff[0:32, :], balanced[...])[:corners]
    for k in range(1, told.shape[0]):
        told[k] = told[0]


def step_on(steps, flex, dir_low, low, new_dir_low, flex_base):
    new_dir = steps[0] * dir_low + steps[1] * low
    new_dir_low[...] = new_dir
    flex_base[...] = dot(flex[:, TOP:], new_dir.astype(BF16))


def first_bulk_kernel(steps, after, balanced, stiff, flex, right, *outs):
    right = right[...].T
    res_top, res_low, sol_top, sol_low, squares = outs[:5]
    stiffed = dot(stiff[...], balanced[...])
    direction = right / cheb_center
    low = right[TOP:, :] - stiffed[TOP:]
    res_top[...] = right[:TOP, :] - stiffed[:TOP]
    res_low[...] = low
    sol_top[...] = direction[:TOP]
    sol_low[...] = direction[TOP:]
    squares[...] = jnp.sum(low * low, axis=0, keepdims=True)
    step_on(steps, flex, direction[TOP:], low, *outs[5:])


def bulk_kernel(steps, balanced, stiff, flex, res_top, res_low, dir_top, dir_low, sol_top, sol_low, *outs):
    new_res_top, new_res_low, new_sol_top, new_sol_low, squares = outs[:5]
    stiffed = dot(stiff[...], balanced[...])
    low = res_low[...] - stiffed[TOP:]
    new_res_top[...] = res_top[...] - stiffed[:TOP]
    new_res_low[...] = low
    new_sol_top[...] = sol_top[...] + dir_top[...]
    new_sol_low[...] = sol_low[...] + dir_low[...]
    squares[...] = jnp.sum(low * low, axis=0, keepdims=True)
    if steps is not None:
        step_on(steps, flex, dir_low[...], low, *outs[5:])


def split_dot(high, low, values):
    values_high, values_low = split(values)
    return dot(high[...], values_high) + (dot(high[...], values_low) + dot(low[...], values_high))


def tree_sum(parts):
    while len(parts) > 1:
        parts = [p + q for p, q in zip(parts[::2], parts[1::2])]
    return parts[0]


def first_half_kernel(high, low, values, total):
    total[...] = split_dot(high, low, values[...].reshape(-1, values.shape[2]))


def first_product_kernel(after, high, low, values, half, total):
    more = split_dot(high, low, values[...].reshape(-1, values.shape[2]))
    total[...] = (half[...] + more).reshape(total.shape)


def gathered(blocks, stack):
    my_y = lax.axis_index("y")
    corners = blocks[0].shape[1]
    for k, block in enumerate(blocks):
        at = pl.multiple_of(((my_y + NY - k) % NY) * corners, TILE)
        stack[pl.ds(at, corners), :] = block[0]
    b = [block[0, 0:TILE, :] for block in blocks]
    return (b[0] + b[2]) + (b[1] + b[3])


def half_product_kernel(high, low, *refs):
    blocks, total, ride, stack = refs[:NY], refs[NY], refs[NY + 1], refs[NY + 2]
    ride[...] = gathered(blocks, stack)
    total[...] = split_dot(high, low, stack[...])


def product_kernel(loads, after, high, low, half, ride, *refs):
    blocks, total, stack = refs[:NY], refs[NY], refs[NY + 1]
    both = ride[...] + gathered(blocks, stack)
    result = (half[...] + split_dot(high, low, stack[...])).reshape(total.shape)
    lane = lax.broadcasted_iota(jnp.int32, both.shape, 1)
    for k in range(total.shape[0]):
        total[k] = result[k]
        total[k, 0:TILE, :] = jnp.where(lane < loads, result[k, 0:TILE, :], both)


def correction_of(terms, squares, res_top, new_res_top, earlier):
    corners = terms.shape[1]
    total = tree_sum([terms[k] for k in range(terms.shape[0])])
    if earlier is not None:
        earlier[...] = total[0:TILE, :]
    new_res_top[...] = res_top[...]
    new_res_top[:corners, :] = res_top[:corners, :] - total[:, : res_top.shape[1]]
    top = new_res_top[...]
    return top, squares[...] + jnp.sum(top * top, axis=0, keepdims=True)


def last_kernel(terms, squares, res_top, new_res_top, earlier, told):
    _, norm = correction_of(terms, squares, res_top, new_res_top, earlier)
    padded = jnp.concatenate([norm, jnp.zeros((1, told.shape[2] - norm.shape[1]), F32)], axis=1)
    told[...] = jnp.broadcast_to(padded[None], told.shape)


def correct_kernel(steps, first, counts, terms, squares, res_top, dir_top, flex, flex_base, *outs):
    earlier, outs = (None, outs) if first else (outs[0], outs[1:])
    new_res_top, extra, new_dir_top, flexed = outs[:4]
    top, norm = correction_of(terms, squares, res_top, new_res_top, earlier)
    new_dir = steps[0] * dir_top[...] + steps[1] * top
    new_dir_top[...] = new_dir
    flexed[...] = flex_base[...] + dot(flex[:, :TOP], new_dir.astype(BF16))
    send_sides(counts, flexed, *outs[4:])
    loads, width = norm.shape[1], extra.shape[1]
    spare = width - loads
    padded = jnp.concatenate([norm, jnp.zeros((1, spare), F32)], axis=1)
    padded = jnp.broadcast_to(padded, (TILE, width))
    line = lax.broadcasted_iota(jnp.int32, padded.shape, 0)
    ride = jnp.zeros_like(padded)
    for n in range(-(-loads // spare)):
        ride = jnp.where(line == n, pltpu.roll(padded, (loads - n * spare) % width, 1), ride)
    extra[...] = jnp.zeros_like(extra)
    extra[0:TILE, :] = ride


def rider_values(earlier, loads):
    spare = earlier.shape[1] - loads
    lines = -(-loads // spare)
    return earlier[:lines, loads:].reshape(-1)[:loads]


def local(right_side, flex, stiff, coarse_inv, corner_map, side_rows):
    right = right_side[0, 0]
    flex_block = flex[0, 0]
    stiff_block = stiff[0, 0]
    order = flex_block.shape[0]
    side = order // SIDES
    loads = right.shape[0]
    width = -(-loads // LANES) * LANES
    corners = corner_map.shape[2]
    rows_held, cols_held = coarse_inv.shape
    half = N_GY * corners
    inv_t = coarse_inv.T
    inv_blocks = [inv_t]
    for k in range(1, NY):
        inv_blocks.append(turned(inv_t, "y", NY, k))

    own_ids, ids_line = call(
        ids_kernel, [shape(N_GY, 1, LANES), shape(1, LANES)], unread=(right, flex_block)
    )(corner_map[0])
    own_ids = to_all(own_ids, GY).reshape(N_GY, LANES)

    sides = [shape(side + side // 2, LANES)] * SIDES
    flexed, extra, counts, *sends = call(
        first_kernel, [shape(order, loads), shape(corners, width), shape(TILE, LANES)] + sides
    )(own_ids, ids_line, side_rows[0], right, flex_block)

    other_ids = turned(own_ids, "c", NC, 1)
    own_rows, other_rows = call(
        rows_kernel, [shape(cols_held, half)] * 2, scratch=[pltpu.VMEM((2 * half, rows_held), BF16)]
    )(own_ids, other_ids, *inv_blocks)
    own_rows = own_rows + turned(other_rows, "c", NC, 1)

    row_parts = [own_rows]
    for k in range(1, NZ):
        row_parts.append(turned(own_rows, "z", NZ, k))

    tops, lows = shape(TOP, loads), shape(order - TOP, loads)
    ride_shape = shape(TILE, width)
    corner_scratch = [pltpu.VMEM((NY * corners, width), F32)]
    rho_prev = 1.0 / cheb_sigma
    norms = []
    for iteration in range(ITERS):
        last = iteration + 1 == ITERS
        ins = []
        for k in range(SIDES):
            axes, count = (GY, N_GY) if k < 2 else (GX, N_GX)
            ins.append(swapped(sends[k], axes, count, k % 2))
        balanced, told = call(
            balance_kernel, [shape(order, loads, dtype=BF16), shape(NY * NX if iteration == 0 else 1, corners, width)]
        )(counts, flexed, *ins, stiff_block, extra)
        steps = None
        if not last:
            rho_next = 1.0 / (2.0 * cheb_sigma - rho_prev)
            steps = (rho_next * rho_prev, 2.0 * rho_next / cheb_half)
            rho_prev = rho_next
        if iteration == 0:
            values = to_all(told, ("y", "x"))
            kernel, state = first_bulk_kernel, (right,)
            order_after = (values,)
        else:
            values = [told]
            for k in range(1, NY):
                values.append(turned(told, "y", NY, k))
            kernel, state = bulk_kernel, (res_top, res_low, dir_top, dir_low, sol_top, sol_low)
            order_after = ()
        outs = call(
            functools.partial(kernel, steps),
            [tops, lows, tops, lows, shape(1, loads)] + ([] if last else [lows, shape(order, loads)]),
        )(*order_after, balanced, stiff_block, flex_block, *state)
        res_top, res_low, sol_top, sol_low, squares = outs[:5]
        if iteration == 0:
            dir_top = sol_top
            values_other = turned(values, "c", NC, 1)
            own_high, own_low, other_high, other_low, *shares = call(
                cols_kernel,
                [shape(half, half, dtype=BF16)] * 4 + [shape(half // NX * 2, half)] * NX,
                scratch=[pltpu.VMEM((2 * half, cols_held), BF16), pltpu.VMEM((2 * half, half), F32)],
            )(values, values_other, *row_parts)
            (partial,) = call(first_half_kernel, [shape(half, width)])(own_high, own_low, values)
            (partial,) = call(first_product_kernel, [shape(N_GY, corners, width)])(
                squares, other_high, other_low, values_other, partial
            )
            for k in range(1, NX):
                shares[k] = turned(shares[k], "x", NX, k)
            block = call(block_kernel, [shape(half, NY * corners, dtype=BF16)] * 4)(*shares)
        else:
            others = []
            for k in range(NY):
                others.append(turned(values[k], "c", NC, 1))
            partial, ride = call(
                half_product_kernel, [shape(half, width), ride_shape], scratch=corner_scratch
            )(*block[:2], *values)
            (partial,) = call(
                functools.partial(product_kernel, loads), [shape(N_GY, corners, width)], scratch=corner_scratch
            )(squares, *block[2:], partial, ride, *others)
        terms = to_all(partial, GY)
        if last:
            res_top, earlier, told = call(
                last_kernel, [tops, ride_shape, shape(N_GX * N_GY, 1, width)]
            )(terms, squares, res_top)
        else:
            dir_low, flex_base = outs[5:]
            outs = call(
                functools.partial(correct_kernel, steps, iteration == 0),
                ([ride_shape] if iteration > 0 else [])
                + [tops, shape(corners, width), tops, shape(order, loads)]
                + sides,
            )(counts, terms, squares, res_top, dir_top, flex_block, flex_base)
            if iteration > 0:
                earlier, *outs = outs
            res_top, extra, dir_top, flexed, *sends = outs
        if iteration > 0:
            norms.append(rider_values(earlier, loads))
    norms.append(to_all(told, ALL).sum(axis=0)[0, :loads])
    resid_norm = jnp.sqrt(jnp.stack(norms) / (N_GX * N_GY * order))
    solution = jnp.concatenate([sol_top, sol_low]).T
    residual = jnp.concatenate([res_top, res_low]).T
    return (solution[None, None], residual[None, None], resid_norm)


def solution(mesh):
    torus = Mesh(mesh.devices.reshape(NY, NC, NX, NZ), ALL)
    return jax.shard_map(
        local,
        mesh=torus,
        in_specs=(
            P(GX, GY, None, None),
            P(GX, GY, None, None),
            P(GX, GY, None, None),
            P(GX, GY),
            P(GX, GY, None),
            P(GX, GY, None),
        ),
        out_specs=(P(GX, GY, None, None), P(GX, GY, None, None), P()),
        check_vma=False,
    )
```
